32 devices in a mesh: req: 4 (over z), head: 2 (over core), exp: 4 (over y, x).
Axes of the slice: x: 2, y: 2, z: 4, core: 2. Of those that a mesh axis runs over, the one named last changes fastest.
Arguments:
- queries: bfloat16 [16, 64, 32, 128], P('req', 'exp', 'head'), may hold values from -8 to 8
- new_keys: bfloat16 [16, 64, 4, 128], P('req', 'exp', 'head'), may hold values from -8 to 8
- new_values: bfloat16 [16, 64, 4, 128], P('req', 'exp', 'head'), may hold values from -6 to 6
- key_cache: bfloat16 [16, 24576, 4, 128], P('req', 'exp', 'head'), may hold values from -6 to 6
- value_cache: bfloat16 [16, 24576, 4, 128], P('req', 'exp', 'head'), may hold values from -6 to 6
- lengths: int32 [16], P('req'), may hold values from 1 to 24576, 131072 in all
- residual: bfloat16 [1024, 2048], P(('req', 'exp')), may hold values from -24 to 24
- out_weight: bfloat16 [4096, 2048], P('head', 'exp'), may hold values from -1.796875 to 1.796875
- norm_gain: float32 [2048], replicated, may hold values from 0.1 to 1.9
- route_ids: int32 [1024, 8], P(('req', 'exp')), may hold values from 0 to 15, all different within a row; in each aligned block of 64 rows (0 to 63, 64 to 127, ...) at most 64 rows name the same one
- route_weights: float32 [1024, 8], P(('req', 'exp')), may hold values from 0.05 to 0.3
- expert_in: bfloat16 [16, 2048, 2, 768], P(('req', 'exp'), None, None, 'head'), may hold values from -0.125 to 0.125
- expert_out: bfloat16 [16, 768, 2048], P(('req', 'exp'), 'head'), may hold values from -0.21875 to 0.21875
Outputs:
- output: bfloat16 [1024, 2048], P(('req', 'exp'), 'head')
The draws below stay inside these ranges and needn't reach their ends.
Inputs may be any that keep to these rules, and one draw needn't show every extreme that they name: `route_ids`: each row names 8 different experts. Among the 64 rows of one device (aligned blocks of rows 0 to 63, 64 to 127 and so on) no expert is named by more than 64 rows.
All inputs are finite; a program needn't handle non-finite values. No bound on the sum of `lengths` on one device may be relied on, other than what follows from the above.
Results may differ from the reference program's by a relative error of at most 0.0051.
Values may be sent and summed in bfloat16 or wider, within the bound.
No kernel may reach another device: no remote copies, remote signals or barrier semaphores. Data moves between devices by JAX's collectives and lax.ppermute only.
A program may use at most 192 MiB of HBM per device.

```python
import math
import jax
import jax.numpy as jnp
import numpy as np
from jax import lax

D = 2048
H = 32
KVH = 4
HD = 128
FF = 768
TOPK = 8
EXPERTS = 16
BLOCK = 64
MAXLEN = 24576
MEAN_LEN = 8192
REQUESTS = 16
TOKENS = 1024
ROWS_DEV = 64
CAP = 64


def draw_queries(key, part):
    values = 1.5 * jax.random.normal(jax.random.fold_in(key, 11), (REQUESTS, BLOCK, H, HD), jnp.float32)
    values = jnp.clip(values, -8.0, 8.0)
    return values.astype(jnp.bfloat16)


def draw_new_keys(key, part):
    values = 2.0 * jax.random.normal(jax.random.fold_in(key, 23), (REQUESTS, BLOCK, KVH, HD), jnp.float32)
    values = jnp.clip(values, -8.0, 8.0)
    return values.astype(jnp.bfloat16)


def draw_residual(key, part):
    row_scales = jnp.exp(jax.random.uniform(jax.random.fold_in(key, 31), (TOKENS, 1), jnp.float32, math.log(0.3), math.log(3.0)))
    column_scales = jnp.exp(jax.random.uniform(jax.random.fold_in(key, 32), (1, D), jnp.float32, math.log(0.2), math.log(2.0)))
    base_values = jnp.clip(jax.random.normal(jax.random.fold_in(key, 33), (TOKENS, D), jnp.float32), -4.0, 4.0)
    return (base_values * row_scales * column_scales).astype(jnp.bfloat16)


def block_scale(own_key, shape, shards, smallest, top_value):
    def one(position, parts):
        draws = jax.random.uniform(jax.random.fold_in(jax.random.fold_in(own_key, 6), position), (parts,), jnp.float32, smallest / len(shards), top_value / len(shards))
        return jnp.repeat(jnp.exp(draws), shape[position] // parts).reshape((-1,) + (1,) * (len(shape) - position - 1))

    loudness = one(*shards[0])
    for cut in shards[1:]:
        loudness = loudness * one(*cut)
    return loudness


def split_up(number_of, total, most, slope):
    loads = [(1 << 20) // math.isqrt(rank ** slope) + 1 for rank in range(2, number_of + 1)]
    surplus, counts = total - most - (number_of - 1), [1] * (number_of - 1)
    while surplus > 0:
        movable = [i for i in range(number_of - 1) if counts[i] < most]
        mass, left = sum([loads[i] for i in movable]), surplus
        for i in movable:
            more = min(most - counts[i], max(1, left * loads[i] // mass), surplus)
            counts[i] = counts[i] + more
            surplus = surplus - more
    return np.array([most] + counts)


def ragged(rng, count, total, most, lean):
    if count == 2:
        one = jax.random.randint(rng, (), max(1, total - most), min(most, total - 1) + 1)
        return jnp.stack([one, total - one])
    tallies = jnp.asarray(split_up(count, total, most, lean), jnp.int32)
    twos = (count - 1) // 2
    giver, receiver = tallies[1:1 + 2 * twos:2], tallies[2:2 + 2 * twos:2]
    slack = jnp.minimum(giver - 1, most - receiver)
    shifted = jax.random.randint(jax.random.fold_in(rng, 1), (twos,), 0, 1 << 20) % (slack + 1)
    tallies = tallies.at[1:1 + 2 * twos:2].set(giver - shifted).at[2:2 + 2 * twos:2].set(receiver + shifted)
    return tallies[jax.random.permutation(jax.random.fold_in(rng, 2), count)]


def shared_out(key, own, number, rows, count, top, reach, slope):
    order = jax.random.permutation(key, count)
    heavy_load, common = portions_of(count, rows * top, reach, slope, True), portions_of(count, rows * top, reach, slope, False)
    places = jnp.arange(count)

    def named(sizes, turn):
        used = int((sizes > 0).sum())
        fixed = max(1, used // 4)
        shifted = fixed + (places - fixed + turn * (used - fixed)) % max(1, count - fixed)
        return jnp.zeros((count,), jnp.int32).at[order[jnp.where(places < fixed, places, shifted)]].set(jnp.asarray(sizes, jnp.int32))

    sizes = jnp.where(number % 4 == 0, named(heavy_load, number // 4), named(common, number - number // 4 - 1))
    mixed = jax.random.permutation(jax.random.fold_in(own, 3), count)
    source_of, sink = mixed[0:count // 2 * 2:2], mixed[1:count // 2 * 2:2]
    slack = jnp.minimum(sizes[source_of] - 1, reach - sizes[sink]) // 2
    slack = jnp.where((source_of == order[0]) | (sink == order[0]) | (sizes[sink] == 0), 0, jnp.maximum(slack, 0))
    shifted = jax.random.randint(jax.random.fold_in(own, 4), (count // 2,), 0, 1 << 20) % (slack + 1)
    sizes = sizes.at[source_of].add(-shifted).at[sink].add(shifted)
    labels = jnp.searchsorted(jnp.cumsum(sizes), jnp.arange(rows * top), side="right").astype(jnp.int32)
    table = labels.reshape(top, rows).T
    table = table[jax.random.permutation(jax.random.fold_in(own, 1), rows)]
    turn = jax.random.randint(jax.random.fold_in(own, 2), (rows, 1), 0, top)
    return jnp.take_along_axis(table, (jnp.arange(top)[None, :] + turn) % top, axis=1)


def portions_of(number_of, total, reach, skew, full):
    weights = [(1 << 20) // math.isqrt(rank ** skew) + 1 for rank in range(1, number_of + 1)]
    largest = reach if full else min(reach, max(-(-total // number_of), total * weights[0] // sum(weights)))
    least = 1 if total - largest >= number_of - 1 else 0
    counts, rest = [largest] + [least] * (number_of - 1), total - largest - least * (number_of - 1)
    while rest > 0:
        candidates = [i for i in range(1, number_of) if counts[i] < largest] or [i for i in range(1, number_of) if counts[i] < reach]
        pool, budget = sum([weights[i] for i in candidates]), rest
        for i in candidates:
            more = min(reach - counts[i], max(1, budget * weights[i] // pool), rest)
            counts[i] = counts[i] + more
            rest = rest - more
    return np.array(counts)


def gaussian(rng, dims, width, most, pieces=(), kind=jnp.bfloat16):
    loudness = block_scale(rng, dims, pieces, -0.22, 0.18) if pieces else 1.0
    values = jax.random.normal(rng, dims, jnp.float32) * width * loudness
    return jnp.minimum(jnp.maximum(values, -most), most).astype(kind)


def setup_inputs(seed: int = 0) -> dict:
    splits = jax.random.split(jax.random.key(seed), 14)
    queries = draw_queries(jax.random.fold_in(splits[13], 71), 0)
    new_keys = draw_new_keys(jax.random.fold_in(splits[13], 71), 0)
    new_values = gaussian(splits[2], (REQUESTS, BLOCK, KVH, HD), 1.0, 6.0, ((0, 4), (1, 4), (2, 2)))
    key_cache = gaussian(splits[3], (REQUESTS, MAXLEN, KVH, HD), 1.0, 6.0, ((0, 4), (1, 4), (2, 2)))
    value_cache = gaussian(splits[4], (REQUESTS, MAXLEN, KVH, HD), 1.0, 6.0, ((0, 4), (1, 4), (2, 2)))
    lengths = ragged(splits[5], REQUESTS, REQUESTS * MEAN_LEN, MAXLEN, 2).astype(jnp.int32)
    residual = draw_residual(jax.random.fold_in(splits[13], 71), 0)
    out_weight = gaussian(splits[7], (H * HD, D), 0.3, 1.796875, ((0, 2), (1, 4)))
    norm_gain = jnp.clip(1.0 + 0.18 * jax.random.normal(splits[8], (D,), jnp.float32), 0.1, 1.9)
    route_ids_keys = jax.random.split(jax.random.fold_in(splits[9], 1), TOKENS // ROWS_DEV)
    route_ids_turns = jax.random.permutation(jax.random.fold_in(splits[9], 3), TOKENS // ROWS_DEV)
    route_ids = jax.vmap(lambda own, number: shared_out(jax.random.fold_in(splits[9], 2), own, number, ROWS_DEV, EXPERTS, TOPK, CAP, 2))(route_ids_keys, route_ids_turns).reshape((TOKENS, TOPK))
    route_weights = jnp.clip(0.05 + 0.25 * jax.random.uniform(splits[10], (TOKENS, TOPK), jnp.float32) ** block_scale(splits[10], (TOKENS, TOPK), ((0, 16),), -0.2, 0.2), 0.05, 0.3)
    expert_in = gaussian(splits[11], (EXPERTS, D, 2, FF), D ** -0.5, 0.125, ((0, 16), (3, 2)))
    expert_out = gaussian(splits[12], (EXPERTS, FF, D), FF ** -0.5, 0.21875, ((0, 16), (1, 2)))
    return dict(queries=queries, new_keys=new_keys, new_values=new_values, key_cache=key_cache, value_cache=value_cache, lengths=lengths, residual=residual, out_weight=out_weight, norm_gain=norm_gain, route_ids=route_ids, route_weights=route_weights, expert_in=expert_in, expert_out=expert_out)


masked_score = -1e+30
norm_epsilon = 1e-06

def attend(operands):
    query, new_key, new_value, cached_key, cached_value, length = operands
    group_size = H // KVH
    query_rows = query.astype(jnp.float32).reshape(BLOCK, KVH, group_size, HD)
    all_keys = jnp.concatenate([cached_key, new_key], axis=0).astype(jnp.float32)
    all_values = jnp.concatenate([cached_value, new_value], axis=0).astype(jnp.float32)
    positions = jnp.arange(MAXLEN + BLOCK, dtype=jnp.int32)
    included = (positions < length) | (positions >= MAXLEN)
    scores = jnp.einsum('bkgd,skd->kgbs', query_rows, all_keys) * HD ** (-0.5)
    scores = jnp.where(included, scores, masked_score)
    row_max = lax.optimization_barrier(jnp.max(scores, axis=-1, keepdims=True))
    exponent = jnp.exp(scores - row_max)
    totals = lax.optimization_barrier(jnp.sum(exponent, axis=-1))
    rounded = lax.optimization_barrier(exponent.astype(jnp.bfloat16)).astype(jnp.float32)
    summed = jnp.einsum('kgbs,skd->bkgd', rounded, all_values)
    result = summed / jnp.transpose(totals, (2, 0, 1))[..., None]
    return result.reshape(BLOCK, H * HD).astype(jnp.bfloat16)

def reference(queries, new_keys, new_values, key_cache, value_cache, lengths, residual, out_weight, norm_gain, route_ids, route_weights, expert_in, expert_out):
    attn = lax.map(attend, (queries, new_keys, new_values, key_cache, value_cache, lengths))
    attn = attn.reshape(TOKENS, H * HD)
    projected = jnp.dot(attn, out_weight, preferred_element_type=jnp.float32)
    hidden = residual.astype(jnp.float32) + projected
    normed = (hidden * lax.rsqrt(lax.optimization_barrier(jnp.mean(hidden * hidden, axis=-1, keepdims=True)) + norm_epsilon) * norm_gain).astype(jnp.bfloat16)
    load_cap = TOKENS // ROWS_DEV * CAP
    padded_rows = jnp.concatenate([normed, jnp.zeros((1, D), jnp.bfloat16)], axis=0)

    def one_expert(accumulated, expert_id):
        hit_mask = route_ids == expert_id
        routed = jnp.any(hit_mask, axis=1)
        weight_row = lax.optimization_barrier(jnp.sum(jnp.where(hit_mask, route_weights, jnp.float32(0.0)), axis=1))
        weight_row = jnp.concatenate([weight_row, jnp.zeros((1,), jnp.float32)])
        selected = jnp.nonzero(routed, size=load_cap, fill_value=TOKENS)[0]
        gathered_rows = padded_rows[selected]
        gate_up = jnp.dot(gathered_rows, expert_in[expert_id].reshape(D, 2 * FF), preferred_element_type=jnp.float32)
        activated = (jax.nn.silu(gate_up[:, :FF]) * gate_up[:, FF:]).astype(jnp.bfloat16)
        result = jnp.dot(activated, expert_out[expert_id], preferred_element_type=jnp.float32).astype(jnp.bfloat16)
        accumulated = accumulated.at[selected].add(weight_row[selected][:, None] * result.astype(jnp.float32))
        return (accumulated, None)
    mixture, unused = lax.scan(one_expert, jnp.zeros((TOKENS + 1, D), jnp.float32), jnp.arange(EXPERTS, dtype=jnp.int32))
    return (hidden + mixture[:TOKENS]).astype(jnp.bfloat16)
```

```python
import functools
import math
import jax
import jax.numpy as jnp
from jax import lax
from jax.experimental import pallas as pl
from jax.experimental.pallas import tpu as pltpu
from jax.sharding import PartitionSpec as P

masked_score = -1e30
norm_epsilon = 1e-06


def largest_block(total, unit, most):
    best = unit
    for size in range(unit, min(total, most) + 1, unit):
        if total % size == 0:
            best = size
    return best


def split_kernel(block, len_ref, k_ref, v_ref, ko_ref, vo_ref, k_scr, v_scr):
    request, step = pl.program_id(0), pl.program_id(1)

    @pl.when(step * block < len_ref[request])
    def _():
        k_scr[...] = k_ref[0].astype(jnp.float32)
        v_scr[...] = v_ref[0].astype(jnp.float32)
        kv = ko_ref.shape[1]
        head_size = ko_ref.shape[3]
        for head in range(kv):
            ko_ref[0, head] = k_scr[pl.ds(head, block, stride=kv), :].astype(jnp.bfloat16)
            value = v_scr[pl.ds(head, block, stride=kv), :]
            vo_ref[0, head, :head_size, :] = value.T.astype(jnp.bfloat16)
            vo_ref[0, head, head_size:, :] = jnp.ones(
                (vo_ref.shape[2] - head_size, block), jnp.bfloat16
            )


def split_heads(key_cache, value_cache, local_lengths, block):
    requests, span, kv, head_size = key_cache.shape
    flat_k = key_cache.reshape(requests, span * kv, head_size)
    flat_v = value_cache.reshape(requests, span * kv, head_size)

    def last(r, i, lens):
        return jnp.minimum(i, jnp.maximum((lens[r] + block - 1) // block - 1, 0))

    return pl.pallas_call(
        functools.partial(split_kernel, block),
        grid_spec=pltpu.PrefetchScalarGridSpec(
            num_scalar_prefetch=1,
            grid=(requests, span // block),
            in_specs=[
                pl.BlockSpec((1, block * kv, head_size), lambda r, i, lens: (r, last(r, i, lens), 0)),
                pl.BlockSpec((1, block * kv, head_size), lambda r, i, lens: (r, last(r, i, lens), 0)),
            ],
            out_specs=[
                pl.BlockSpec(
                    (1, kv, block, head_size), lambda r, i, lens: (r, 0, last(r, i, lens), 0)
                ),
                pl.BlockSpec(
                    (1, kv, head_size + 16, block), lambda r, i, lens: (r, 0, 0, last(r, i, lens))
                ),
            ],
            scratch_shapes=[
                pltpu.VMEM((block * kv, head_size), jnp.float32),
                pltpu.VMEM((block * kv, head_size), jnp.float32),
            ],
        ),
        out_shape=[
            jax.ShapeDtypeStruct((requests, kv, span, head_size), jnp.bfloat16),
            jax.ShapeDtypeStruct((requests, kv, head_size + 16, span), jnp.bfloat16),
        ],
        compiler_params=pltpu.CompilerParams(dimension_semantics=("arbitrary", "arbitrary")),
        name="split_heads",
    )(local_lengths, flat_k, flat_v)


def attend_kernel(pieces, sub, factor, exp_count, info_ref, *refs):
    q_refs = refs[:pieces]
    nk_ref, nv_ref, k_ref, vt_ref, o_ref = refs[pieces : pieces + 5]
    q_all, q_t, m_scr, acc, turned, stats = refs[pieces + 5 :]
    requests = pl.num_programs(0)
    request, step = pl.program_id(0), pl.program_id(1)
    kv = k_ref.shape[1]
    block, head_size = k_ref.shape[2], k_ref.shape[3]
    piece_rows, heads = q_refs[0].shape[1], q_refs[0].shape[2]
    group = heads // kv
    rows = piece_rows * pieces
    lanes = rows * group
    length = info_ref[request]

    @pl.when((request == 0) & (step == 0))
    def _():
        stats[...] = jnp.zeros_like(stats)

    @pl.when(step == 0)
    def _():
        for piece in range(pieces):
            where_to = info_ref[requests + piece] * piece_rows
            q_all[pl.ds(where_to, piece_rows)] = q_refs[piece][0].astype(jnp.float32) * factor
        fresh_rows = nk_ref.shape[1]
        fresh_k = nk_ref[0].astype(jnp.float32)
        fresh_v = nv_ref[0].astype(jnp.float32)
        for head in range(kv):
            chosen = q_all[:, head * group : (head + 1) * group, :].reshape(lanes, head_size)
            q_t[head] = chosen.T.astype(jnp.bfloat16)
            keys = fresh_k[:, head, :].astype(jnp.bfloat16)
            values = fresh_v[:, head, :]
            scores = jnp.dot(keys, q_t[head], preferred_element_type=jnp.float32)
            top = jnp.max(scores, axis=0, keepdims=True).astype(jnp.bfloat16).astype(jnp.float32)
            probs = jnp.exp2(scores - top).astype(jnp.bfloat16)
            extended = jnp.concatenate(
                [values, jnp.ones((fresh_rows, head_size), jnp.float32)], axis=1
            )
            first = lax.dot_general(
                extended.astype(jnp.bfloat16),
                probs,
                (((0,), (0,)), ((), ())),
                preferred_element_type=jnp.float32,
            )
            acc[head] = first[: head_size + 16]
            m_scr[head] = top

    def one(start, masked):
        for head in range(kv):
            keys = k_ref[0, head, pl.ds(start, sub), :]
            scores = jnp.dot(keys, q_t[head], preferred_element_type=jnp.float32)
            if masked:
                position = step * block + start + lax.broadcasted_iota(jnp.int32, (sub, lanes), 0)
                scores = jnp.where(position < length, scores, masked_score)
            before = m_scr[head]
            top = jnp.maximum(before, jnp.max(scores, axis=0, keepdims=True))
            top = top.astype(jnp.bfloat16).astype(jnp.float32)
            probs = jnp.exp2(scores - top).astype(jnp.bfloat16)
            m_scr[head] = top
            update = jnp.dot(
                vt_ref[0, head, :, pl.ds(start, sub)], probs, preferred_element_type=jnp.float32
            )
            acc[head] = acc[head] * jnp.exp2(before - top) + update

    here = jnp.clip(length - step * block, 0, block)
    whole = here // sub

    def loop(i, carry):
        one(pl.multiple_of(i * sub, sub), False)
        return carry

    lax.fori_loop(0, whole, loop, 0)

    @pl.when(here > whole * sub)
    def _():
        one(pl.multiple_of(whole * sub, sub), True)

    @pl.when(step == pl.num_programs(1) - 1)
    def _():
        share = heads // exp_count
        lane_group = lax.broadcasted_iota(jnp.int32, (8, lanes), 1) % group
        slot = lax.broadcasted_iota(jnp.int32, (8, lanes), 0)
        own = lane_group == slot
        for head in range(kv):
            total = acc[head, head_size : head_size + 1, :]
            scaled = acc[head, :head_size, :] / total
            turned[0] = scaled.T
            upper = total.astype(jnp.bfloat16).astype(jnp.float32)
            kinds = [upper, m_scr[head], total - upper]
            columns = [jnp.where(own, jnp.broadcast_to(x, own.shape), 0.0) for x in kinds]
            padding = jnp.zeros((head_size - 24, lanes), jnp.float32)
            spread = jnp.concatenate(columns + [padding], axis=0).T
            gathered = jnp.sum(spread.reshape(rows, group, head_size), axis=1)
            shift = 24 * request
            placed = pltpu.roll(gathered, shift, 1)
            stats[head] = stats[head] + placed
            for member in range(group):
                index = head * group + member
                target, inside = index // share, index % share
                width = share * head_size
                offset = pl.multiple_of(request * width + inside * head_size, head_size)
                o_ref[target, :, pl.ds(offset, head_size)] = turned[
                    0, pl.ds(member, rows, stride=group), :
                ].astype(jnp.bfloat16)

        @pl.when(request == requests - 1)
        def _():
            for target in range(exp_count):
                head = target * share // group
                o_ref[target, :, requests * share * head_size :] = stats[head].astype(jnp.bfloat16)


def attend(queries, order, new_keys, new_values, keys, values_t, local_lengths, block, sub, exp_count):
    requests, kv, span, head_size = keys.shape
    piece_rows, heads = queries[0].shape[1:3]
    pieces = len(queries)
    rows = piece_rows * pieces
    group = heads // kv
    share = heads // exp_count
    fresh = new_keys.shape[1]
    width = requests * share * head_size + 128
    info = jnp.concatenate([local_lengths, order])
    factor = head_size ** (-0.5) * math.log2(math.e)

    def last(r, i, info):
        return jnp.minimum(i, jnp.maximum((info[r] + block - 1) // block - 1, 0))

    lanes = rows * group
    return pl.pallas_call(
        functools.partial(attend_kernel, pieces, sub, factor, exp_count),
        grid_spec=pltpu.PrefetchScalarGridSpec(
            num_scalar_prefetch=1,
            grid=(requests, span // block),
            in_specs=[
                pl.BlockSpec((1, piece_rows, heads, head_size), lambda r, i, info: (r, 0, 0, 0))
            ]
            * pieces
            + [
                pl.BlockSpec((1, fresh, kv, head_size), lambda r, i, info: (r, 0, 0, 0)),
                pl.BlockSpec((1, fresh, kv, head_size), lambda r, i, info: (r, 0, 0, 0)),
                pl.BlockSpec(
                    (1, kv, block, head_size), lambda r, i, info: (r, 0, last(r, i, info), 0)
                ),
                pl.BlockSpec(
                    (1, kv, head_size + 16, block), lambda r, i, info: (r, 0, 0, last(r, i, info))
                ),
            ],
            out_specs=pl.BlockSpec((exp_count, rows, width), lambda r, i, info: (0, 0, 0)),
            scratch_shapes=[
                pltpu.VMEM((rows, heads, head_size), jnp.float32),
                pltpu.VMEM((kv, head_size, lanes), jnp.bfloat16),
                pltpu.VMEM((kv, 1, lanes), jnp.float32),
                pltpu.VMEM((kv, head_size + 16, lanes), jnp.float32),
                pltpu.VMEM((1, lanes, head_size), jnp.float32),
                pltpu.VMEM((kv, rows, head_size), jnp.float32),
            ],
        ),
        out_shape=jax.ShapeDtypeStruct((exp_count, rows, width), jnp.bfloat16),
        compiler_params=pltpu.CompilerParams(dimension_semantics=("arbitrary", "arbitrary")),
        name="attend",
    )(info, *queries, new_keys, new_values, keys, values_t)


def merge_kernel(parts, share, info_ref, *refs):
    x_refs = refs[:parts]
    w_refs = refs[parts : 2 * parts]
    keep_ref, send_ref, attn = refs[2 * parts :]
    rows, width = x_refs[0].shape
    head_size = 128
    requests = (width - head_size) // (share * head_size)
    group_shift = info_ref[0]
    half = info_ref[1]
    tables = []
    for x_ref in x_refs:
        table = x_ref[:, width - head_size :].astype(jnp.float32)
        tables.append(pltpu.roll(table, group_shift, 1))
    for request in range(requests):
        for member in range(share):
            at = 24 * request + member
            tops = [t[:, at + 8 : at + 9] for t in tables]
            sums = [t[:, at : at + 1] + t[:, at + 16 : at + 17] for t in tables]
            top = functools.reduce(jnp.maximum, tops)
            weights = [s * jnp.exp2(m - top) for s, m in zip(sums, tops)]
            inverse = 1.0 / functools.reduce(jnp.add, weights)
            start = (request * share + member) * head_size
            mixed = jnp.zeros((rows, head_size), jnp.float32)
            for weight, x_ref in zip(weights, x_refs):
                part = x_ref[:, start : start + head_size].astype(jnp.float32)
                mixed = mixed + jnp.broadcast_to(weight * inverse, part.shape) * part
            attn[
                request * rows : (request + 1) * rows, member * head_size : (member + 1) * head_size
            ] = mixed.astype(jnp.bfloat16)
    columns = w_refs[0].shape[1]
    per_half = keep_ref.shape[1] // columns
    for part in range(parts):
        made = jnp.dot(attn[...], w_refs[part][...], preferred_element_type=jnp.float32)
        chunk = info_ref[2 + part]
        inside = pl.multiple_of((chunk % per_half) * columns, columns)

        @pl.when(chunk // per_half == half)
        def _():
            keep_ref[:, pl.ds(inside, columns)] = made

        @pl.when(chunk // per_half != half)
        def _():
            send_ref[:, pl.ds(inside, columns)] = made.astype(jnp.bfloat16)


def merge_project(messages, weights, info, share, requests):
    rows, width = messages[0].shape
    columns = weights[0].shape[1]
    parts = len(messages)
    half_width = parts * columns // 2
    shape = (requests * rows, half_width)
    return pl.pallas_call(
        functools.partial(merge_kernel, parts, share),
        in_specs=[pl.BlockSpec(memory_space=pltpu.SMEM)]
        + [pl.BlockSpec(memory_space=pltpu.VMEM)] * (2 * parts),
        out_specs=[pl.BlockSpec(memory_space=pltpu.VMEM)] * 2,
        out_shape=[
            jax.ShapeDtypeStruct(shape, jnp.float32),
            jax.ShapeDtypeStruct(shape, jnp.bfloat16),
        ],
        scratch_shapes=[pltpu.VMEM((requests * rows, share * head_size_of(weights, share)), jnp.bfloat16)],
        name="merge_project",
    )(info, *messages, *weights)


def head_size_of(weights, share):
    return weights[0].shape[0] // share


def shift(value, axis, step):
    size = lax.axis_size(axis)
    return lax.ppermute(value, axis, [(i, (i + step) % size) for i in range(size)])


def take_block(value, index):
    return lax.dynamic_index_in_dim(value, index, 0, keepdims=False)


def gather_blocks(block, axis):
    return [block] + [shift(block, axis, s) for s in range(1, lax.axis_size(axis))]


def dense_experts(half_hidden, route_ids, route_weights, norm_gain, expert_in, expert_out):
    row_count, half_width = half_hidden.shape
    model_width = 2 * half_width
    req_size, exp_size = lax.axis_size("req"), lax.axis_size("exp")
    req_at, exp_at, head_at = lax.axis_index("req"), lax.axis_index("exp"), lax.axis_index("head")
    groups = req_size * exp_size
    table = jnp.sum(
        jnp.where(
            route_ids[None, :, :] == lax.iota(jnp.int32, groups)[:, None, None],
            route_weights[None, :, :],
            0.0,
        ),
        axis=2,
    )
    mine = lax.all_to_all(table, ("req", "exp"), split_axis=0, concat_axis=0, tiled=True)
    by_req = (req_at - lax.iota(jnp.int32, req_size)) % req_size
    by_exp = (exp_at - lax.iota(jnp.int32, exp_size)) % exp_size
    order = by_req[None, :] * exp_size + by_exp[:, None]
    row_weights = jnp.take(mine, order.reshape(-1), axis=0).reshape(-1, 1)

    sent = half_hidden.astype(jnp.bfloat16)
    column = jnp.stack(gather_blocks(sent, "req"))
    plane = jnp.stack(gather_blocks(column, "exp"))
    own_half = plane.reshape(groups * row_count, half_width)
    other_half = shift(own_half, "head", 1)
    first = jnp.where(head_at == 0, own_half, other_half)
    second = jnp.where(head_at == 0, other_half, own_half)
    rows = jnp.concatenate([first, second], axis=1).astype(jnp.float32)
    normed = (
        rows * lax.rsqrt(jnp.mean(rows * rows, axis=-1, keepdims=True) + norm_epsilon) * norm_gain
    ).astype(jnp.bfloat16)
    gate_up = jnp.dot(
        normed, expert_in[0].reshape(model_width, -1), preferred_element_type=jnp.float32
    )
    half_units = gate_up.shape[-1] // 2
    activated = (jax.nn.silu(gate_up[:, :half_units]) * gate_up[:, half_units:]).astype(
        jnp.bfloat16
    )
    partial = jnp.dot(activated, expert_out[0], preferred_element_type=jnp.float32) * row_weights
    kept = lax.dynamic_slice_in_dim(partial, head_at * half_width, half_width, 1)
    other = lax.dynamic_slice_in_dim(partial, (1 - head_at) * half_width, half_width, 1)
    summed = kept + shift(other.astype(jnp.bfloat16), "head", 1).astype(jnp.float32)
    summed = summed.reshape(exp_size, req_size * row_count, half_width)
    plane_sum = summed[0]
    outgoing = summed.astype(jnp.bfloat16)
    for s in range(1, exp_size):
        plane_sum = plane_sum + shift(outgoing[s], "exp", -s).astype(jnp.float32)
    plane_sum = plane_sum.reshape(req_size, row_count, half_width)
    mixture = plane_sum[0]
    outgoing = plane_sum.astype(jnp.bfloat16)
    for s in range(1, req_size):
        mixture = mixture + shift(outgoing[s], "req", -s).astype(jnp.float32)
    return mixture


def sparse_experts(half_hidden, route_ids, route_weights, norm_gain, expert_in, expert_out, capacity):
    row_count, half_width = half_hidden.shape
    head_at = lax.axis_index("head")
    other = shift(half_hidden, "head", 1)
    first = jnp.where(head_at == 0, half_hidden, other)
    second = jnp.where(head_at == 0, other, half_hidden)
    hidden = jnp.concatenate([first, second], axis=1)
    normed = (
        hidden
        * lax.rsqrt(jnp.mean(hidden * hidden, axis=-1, keepdims=True) + norm_epsilon)
        * norm_gain
    ).astype(jnp.bfloat16)
    model_width = 2 * half_width
    local_experts = expert_in.shape[0]
    groups = lax.axis_size("req") * lax.axis_size("exp")
    experts_all = local_experts * groups
    expert_iota = lax.iota(jnp.int32, experts_all)
    named_count = jnp.sum((route_ids[:, :, None] == expert_iota).astype(jnp.int32), axis=1)
    earlier = jnp.cumsum(named_count, axis=0) - named_count
    slot_rank = jnp.take_along_axis(earlier, route_ids, axis=1)
    slot_index = route_ids * capacity + slot_rank
    slot_iota = lax.iota(jnp.int32, experts_all * capacity)
    placing = jnp.any(slot_index[None, :, :] == slot_iota[:, None, None], axis=2).astype(
        jnp.bfloat16
    )
    outgoing = jnp.dot(placing, normed, preferred_element_type=jnp.float32).astype(jnp.bfloat16)
    outgoing = outgoing.reshape(groups, local_experts, capacity, model_width)
    input_maps = expert_in.reshape(local_experts, model_width, -1)
    gate_up = jnp.einsum(
        "geci,eif->gecf",
        lax.all_to_all(outgoing, ("req", "exp"), split_axis=0, concat_axis=0, tiled=True),
        input_maps,
        preferred_element_type=jnp.float32,
    )
    half_units = gate_up.shape[-1] // 2
    activated = (jax.nn.silu(gate_up[..., :half_units]) * gate_up[..., half_units:]).astype(
        jnp.bfloat16
    )
    partial_value = jnp.einsum(
        "gecf,efi->geci", activated, expert_out, preferred_element_type=jnp.float32
    )
    summed = lax.psum_scatter(partial_value, "head", scatter_dimension=3, tiled=True).astype(
        jnp.bfloat16
    )
    returned = lax.all_to_all(summed, ("req", "exp"), split_axis=0, concat_axis=0, tiled=True)
    flat_results = returned.reshape(experts_all * capacity, half_width)
    picked = jnp.take(flat_results, slot_index, axis=0).astype(jnp.float32)
    return jnp.sum(picked * route_weights[:, :, None], axis=1)


def local(
    queries,
    new_keys,
    new_values,
    key_cache,
    value_cache,
    lengths,
    residual,
    out_weight,
    norm_gain,
    route_ids,
    route_weights,
    expert_in,
    expert_out,
):
    requests, span, kv, head_size = key_cache.shape
    heads = queries.shape[2]
    exp_size = lax.axis_size("exp")
    exp_at, head_at = lax.axis_index("exp"), lax.axis_index("head")
    share = heads // exp_size
    group = heads // kv
    sources = (exp_at - lax.iota(jnp.int32, exp_size)) % exp_size
    targets = [(exp_at + s) % exp_size for s in range(exp_size)]

    pieces = gather_blocks(queries, "exp")
    local_lengths = jnp.clip(lengths - exp_at * span, 0, span)
    keys, values_t = split_heads(
        key_cache, value_cache, local_lengths, largest_block(span, 512, 1024)
    )
    split_weight = out_weight.reshape(exp_size, share * head_size, -1)
    weight_parts = [take_block(split_weight, targets[0])] + [
        shift(take_block(split_weight, targets[s]), "exp", s) for s in range(1, exp_size)
    ]
    messages = attend(
        pieces,
        sources,
        new_keys,
        new_values,
        keys,
        values_t,
        local_lengths,
        largest_block(span, 512, 2048),
        512,
        exp_size,
    )
    received = [take_block(messages, targets[0])] + [
        shift(take_block(messages, targets[s]), "exp", s) for s in range(1, exp_size)
    ]
    group_shift = (head_size - (exp_at * share) % group) % head_size
    info = jnp.concatenate([jnp.stack([group_shift, head_at]).astype(jnp.int32), sources])
    kept, sent = merge_project(received, weight_parts, info, share, requests)
    both = kept + shift(sent, "head", 1).astype(jnp.float32)
    row_count, model_width = residual.shape
    half_width = model_width // 2
    both = both.reshape(exp_size, row_count, half_width)
    outgoing = both.astype(jnp.bfloat16)
    hidden = lax.dynamic_slice_in_dim(residual, head_at * half_width, half_width, 1).astype(
        jnp.float32
    ) + take_block(both, targets[0])
    for s in range(1, exp_size):
        hidden = hidden + shift(take_block(outgoing, targets[s]), "exp", s).astype(jnp.float32)

    groups = lax.axis_size("req") * exp_size
    experts_all = expert_in.shape[0] * groups
    capacity = max(2, 2 * row_count * route_ids.shape[1] // experts_all)
    if capacity >= row_count and experts_all == groups:
        mixture = dense_experts(hidden, route_ids, route_weights, norm_gain, expert_in, expert_out)
    else:
        mixture = sparse_experts(
            hidden, route_ids, route_weights, norm_gain, expert_in, expert_out, capacity
        )
    return (hidden + mixture).astype(jnp.bfloat16)


def solution(mesh):
    return jax.shard_map(
        local,
        mesh=mesh,
        in_specs=(
            P("req", "exp", "head", None),
            P("req", "exp", "head", None),
            P("req", "exp", "head", None),
            P("req", "exp", "head", None),
            P("req", "exp", "head", None),
            P("req"),
            P(("req", "exp"), None),
            P("head", "exp"),
            P(),
            P(("req", "exp"), None),
            P(("req", "exp"), None),
            P(("req", "exp"), None, None, "head"),
            P(("req", "exp"), "head", None),
        ),
        out_specs=P(("req", "exp"), "head"),
        check_vma=False,
    )
```

```python
import functools
import math
import jax
import jax.numpy as jnp
from jax import lax
from jax.experimental import pallas as pl
from jax.experimental.pallas import tpu as pltpu
from jax.sharding import PartitionSpec as P

masked_score = -1e30
norm_epsilon = 1e-06


def attend_kernel(pieces, sub, tail, factor, exp_count, info_ref, *refs):
    q_refs = refs[:pieces]
    nk_ref, nv_ref, k_ref, v_ref, o_ref = refs[pieces : pieces + 5]
    q_all, q_cat, pattern, m_scr, l_scr, acc, p_even, p_odd, stats, turned = refs[pieces + 5 :]
    requests = pl.num_programs(0)
    request = pl.program_id(0)
    head_size = k_ref.shape[2]
    kv = 2
    piece_rows, heads = q_refs[0].shape[1], q_refs[0].shape[2]
    group = heads // kv
    rows = piece_rows * pieces
    lanes = rows * group
    length = info_ref[request]
    even_lane = lax.broadcasted_iota(jnp.int32, (lanes, 128), 1) % 2 == 0

    @pl.when(request == 0)
    def _():
        stats[...] = jnp.zeros_like(stats)
        parity = lax.broadcasted_iota(jnp.int32, (16, head_size), 0) % 2
        pattern[0] = (1 - parity).astype(jnp.float32).astype(jnp.bfloat16)
        pattern[1] = parity.astype(jnp.float32).astype(jnp.bfloat16)

    for piece in range(pieces):
        where_to = info_ref[requests + piece] * piece_rows
        q_all[pl.ds(where_to, piece_rows)] = q_refs[piece][0].astype(jnp.float32)
    for head in range(kv):
        chosen = q_all[:, head * group : (head + 1) * group, :].reshape(lanes, head_size)
        q_cat[:, head * head_size : (head + 1) * head_size] = chosen.astype(jnp.bfloat16)

    def spread(block):
        if block.shape[0] < 16:
            left = block * pattern[0, : block.shape[0]]
            right = block * pattern[1, : block.shape[0]]
        else:
            tiles = block.reshape(block.shape[0] // 16, 16, head_size)
            left = (tiles * pattern[0][None]).reshape(block.shape)
            right = (tiles * pattern[1][None]).reshape(block.shape)
        return jnp.concatenate([left, right], axis=1)

    def score(block):
        return lax.dot_general(
            q_cat[...],
            spread(block),
            (((1,), (1,)), ((), ())),
            preferred_element_type=jnp.float32,
        )

    def both_columns(even, odd):
        shape = (lanes, 128)
        return jnp.where(even_lane, jnp.broadcast_to(even, shape), jnp.broadcast_to(odd, shape))

    def reduce_parity(wide, op, neutral):
        even = op(jnp.where(even_lane, wide, neutral), axis=1, keepdims=True)
        odd = op(jnp.where(even_lane, neutral, wide), axis=1, keepdims=True)
        return even, odd

    def init():
        scores = score(nk_ref[0]) * factor
        fresh = scores.shape[1]
        even = lax.broadcasted_iota(jnp.int32, scores.shape, 1) % 2 == 0
        top_even = jnp.max(jnp.where(even, scores, -jnp.inf), axis=1, keepdims=True)
        top_odd = jnp.max(jnp.where(even, -jnp.inf, scores), axis=1, keepdims=True)
        top_even = top_even.astype(jnp.bfloat16).astype(jnp.float32)
        top_odd = top_odd.astype(jnp.bfloat16).astype(jnp.float32)
        m_scr[...] = both_columns(top_even, top_odd)
        probs = jnp.exp2(
            scores
            - jnp.where(
                even,
                jnp.broadcast_to(top_even, scores.shape),
                jnp.broadcast_to(top_odd, scores.shape),
            )
        )
        l_even = jnp.sum(jnp.where(even, probs, 0.0), axis=1, keepdims=True)
        l_odd = jnp.sum(jnp.where(even, 0.0, probs), axis=1, keepdims=True)
        lane = lax.broadcasted_iota(jnp.int32, (lanes, 128), 1)
        l_scr[...] = jnp.where(lane < 2, both_columns(l_even, l_odd), 0.0)
        acc[...] = jnp.dot(
            probs.astype(jnp.bfloat16), spread(nv_ref[0]), preferred_element_type=jnp.float32
        )

    def piece_of(ref, start, size):
        return ref[0, pl.ds(pl.multiple_of(start * kv, kv * tail), size * kv), :]

    step = 256

    def soften(start, size, target, masked):
        top = m_scr[...]
        total = l_scr[...]
        for tile in range(size * kv // step):
            scores = score(piece_of_tile(k_ref, start, tile))
            for part in range(step // 128):
                piece = scores[:, part * 128 : (part + 1) * 128]
                probs = jnp.exp2(piece * factor - top)
                if masked:
                    lane = lax.broadcasted_iota(jnp.int32, (1, 128), 1)
                    position = start + (tile * step + part * 128 + lane) // kv
                    probs = jnp.where(position < length, probs, 0.0)
                total = total + probs
                at = tile * step + part * 128
                target[:, at : at + 128] = probs.astype(jnp.bfloat16)
        l_scr[...] = total

    def piece_of_tile(ref, start, tile):
        first = pl.multiple_of(start * kv, kv * tail) + tile * step
        return ref[0, pl.ds(first, step), :]

    def weigh(start, size, source):
        values = spread(piece_of(v_ref, start, size))
        acc[...] += jnp.dot(source[:, : size * kv], values, preferred_element_type=jnp.float32)

    init()
    here = length
    pairs = here // (2 * sub)

    def loop(i, carry):
        start = pl.multiple_of(i * 2 * sub, 2 * sub)
        before = jnp.maximum(start - sub, 0)
        soften(start, sub, p_even, False)
        weigh(before, sub, p_odd)
        soften(start + sub, sub, p_odd, False)
        weigh(start, sub, p_even)
        return carry

    p_odd[...] = jnp.zeros_like(p_odd)
    lax.fori_loop(0, pairs, loop, 0)
    weigh(pl.multiple_of(jnp.maximum(pairs * 2 * sub - sub, 0), sub), sub, p_odd)

    def tail_loop(i, carry):
        start = pl.multiple_of(pairs * 2 * sub + i * tail, tail)
        soften(start, tail, p_even, True)
        weigh(start, tail, p_even)
        return carry

    lax.fori_loop(0, (here - pairs * 2 * sub + tail - 1) // tail, tail_loop, 0)
    largest = jnp.max(l_scr[...])

    @pl.when(jnp.logical_not(largest < 1e30))
    def _():
        init()

        def slow_loop(i, carry):
            start = pl.multiple_of(i * tail, tail)
            scores = score(piece_of(k_ref, start, tail)) * factor
            lane = lax.broadcasted_iota(jnp.int32, (1, tail * kv), 1)
            inside = start + lane // kv < length
            scores = jnp.where(inside, scores, masked_score)
            wide = m_scr[...]
            for part in range(tail * kv // 128):
                wide = jnp.maximum(wide, scores[:, part * 128 : (part + 1) * 128])
            even, odd = reduce_parity(wide, jnp.max, -jnp.inf)
            even = even.astype(jnp.bfloat16).astype(jnp.float32)
            odd = odd.astype(jnp.bfloat16).astype(jnp.float32)
            top = both_columns(even, odd)
            fade = jnp.exp2(m_scr[...] - top)
            total = l_scr[...] * fade
            for part in range(tail * kv // 128):
                at = part * 128
                probs = jnp.where(
                    inside[:, at : at + 128], jnp.exp2(scores[:, at : at + 128] - top), 0.0
                )
                total = total + probs
                p_even[:, at : at + 128] = probs.astype(jnp.bfloat16)
            l_scr[...] = total
            m_scr[...] = top
            for head in range(kv):
                columns = slice(head * head_size, (head + 1) * head_size)
                acc[:, columns] = acc[:, columns] * jnp.broadcast_to(
                    fade[:, head : head + 1], (lanes, head_size)
                )
            weigh(start, tail, p_even)
            return carry

        lax.fori_loop(0, (here + tail - 1) // tail, slow_loop, 0)

    share = heads // exp_count
    totals = reduce_parity(l_scr[...], jnp.sum, 0.0)
    lane = lax.broadcasted_iota(jnp.int32, (lanes, head_size), 1)
    member_of_row = lax.broadcasted_iota(jnp.int32, (lanes, head_size), 0) % group
    for head in range(kv):
        total = totals[head]
        inverse = jnp.broadcast_to(1.0 / total, (lanes, head_size))
        columns = slice(head * head_size, (head + 1) * head_size)
        turned[...] = acc[:, columns] * inverse
        upper = total.astype(jnp.bfloat16).astype(jnp.float32)
        kinds = [upper, m_scr[:, head : head + 1], total - upper]
        placed = jnp.zeros((lanes, head_size), jnp.float32)
        for kind, column in enumerate(kinds):
            placed = jnp.where(
                lane == member_of_row + 8 * kind,
                jnp.broadcast_to(column, placed.shape),
                placed,
            )
        gathered = jnp.sum(placed.reshape(rows, group, head_size), axis=1)
        stats[head] = stats[head] + pltpu.roll(gathered, 24 * request, 1)
        for member in range(group):
            index = head * group + member
            target, inside = index // share, index % share
            offset = pl.multiple_of(
                request * (share * head_size) + inside * head_size, head_size
            )
            o_ref[target, :, pl.ds(offset, head_size)] = turned[
                pl.ds(member, rows, stride=group), :
            ].astype(jnp.bfloat16)

    @pl.when(request == requests - 1)
    def _():
        for target in range(exp_count):
            head = target * share // group
            o_ref[target, :, requests * share * head_size :] = stats[head].astype(jnp.bfloat16)


def attend(queries, order, new_keys, new_values, keys, values, local_lengths, sub, tail, exp_count):
    requests, span, kv, head_size = keys.shape
    piece_rows, heads = queries[0].shape[1:3]
    pieces = len(queries)
    rows = piece_rows * pieces
    share = heads // exp_count
    fresh = new_keys.shape[1]
    width = requests * share * head_size + 128
    info = jnp.concatenate([local_lengths, order])
    factor = head_size ** (-0.5) * math.log2(math.e)
    lanes = rows * heads // kv
    flat = lambda x: x.reshape(requests, x.shape[1] * kv, head_size)
    block = lambda n: pl.BlockSpec((1, n, head_size), lambda r, info: (r, 0, 0))
    return pl.pallas_call(
        functools.partial(attend_kernel, pieces, sub, tail, factor, exp_count),
        grid_spec=pltpu.PrefetchScalarGridSpec(
            num_scalar_prefetch=1,
            grid=(requests,),
            in_specs=[
                pl.BlockSpec((1, piece_rows, heads, head_size), lambda r, info: (r, 0, 0, 0))
            ]
            * pieces
            + [block(fresh * kv), block(fresh * kv), block(span * kv), block(span * kv)],
            out_specs=pl.BlockSpec((exp_count, rows, width), lambda r, info: (0, 0, 0)),
            scratch_shapes=[
                pltpu.VMEM((rows, heads, head_size), jnp.float32),
                pltpu.VMEM((lanes, kv * head_size), jnp.bfloat16),
                pltpu.VMEM((2, 16, head_size), jnp.bfloat16),
                pltpu.VMEM((lanes, 128), jnp.float32),
                pltpu.VMEM((lanes, 128), jnp.float32),
                pltpu.VMEM((lanes, kv * head_size), jnp.float32),
                pltpu.VMEM((lanes, 2 * sub * kv), jnp.bfloat16),
                pltpu.VMEM((lanes, sub * kv), jnp.bfloat16),
                pltpu.VMEM((kv, rows, head_size), jnp.float32),
                pltpu.VMEM((lanes, head_size), jnp.float32),
            ],
        ),
        out_shape=jax.ShapeDtypeStruct((exp_count, rows, width), jnp.bfloat16),
        compiler_params=pltpu.CompilerParams(dimension_semantics=("arbitrary",)),
        name="attend",
    )(info, *queries, flat(new_keys), flat(new_values), flat(keys), flat(values))


def merge_kernel(parts, share, info_ref, *refs):
    x_refs = refs[:parts]
    w_refs = refs[parts : 2 * parts]
    keep_ref, send_ref, attn = refs[2 * parts :]
    rows, width = x_refs[0].shape
    head_size = 128
    requests = (width - head_size) // (share * head_size)
    group_shift = info_ref[0]
    half = info_ref[1]
    tables = []
    for x_ref in x_refs:
        table = x_ref[:, width - head_size :].astype(jnp.float32)
        tables.append(pltpu.roll(table, group_shift, 1))
    for request in range(requests):
        for member in range(share):
            at = 24 * request + member
            tops = [t[:, at + 8 : at + 9] for t in tables]
            sums = [t[:, at : at + 1] + t[:, at + 16 : at + 17] for t in tables]
            top = functools.reduce(jnp.maximum, tops)
            weights = [s * jnp.exp2(m - top) for s, m in zip(sums, tops)]
            inverse = 1.0 / functools.reduce(jnp.add, weights)
            start = (request * share + member) * head_size
            mixed = jnp.zeros((rows, head_size), jnp.float32)
            for weight, x_ref in zip(weights, x_refs):
                part = x_ref[:, start : start + head_size].astype(jnp.float32)
                mixed = mixed + jnp.broadcast_to(weight * inverse, part.shape) * part
            attn[
                request * rows : (request + 1) * rows, member * head_size : (member + 1) * head_size
            ] = mixed.astype(jnp.bfloat16)
    columns = w_refs[0].shape[1]
    per_half = keep_ref.shape[1] // columns
    for part in range(parts):
        made = jnp.dot(attn[...], w_refs[part][...], preferred_element_type=jnp.float32)
        chunk = info_ref[2 + part]
        inside = pl.multiple_of((chunk % per_half) * columns, columns)

        @pl.when(chunk // per_half == half)
        def _():
            keep_ref[:, pl.ds(inside, columns)] = made

        @pl.when(chunk // per_half != half)
        def _():
            send_ref[:, pl.ds(inside, columns)] = made.astype(jnp.bfloat16)


def merge_project(messages, weights, info, share, requests):
    rows, width = messages[0].shape
    columns = weights[0].shape[1]
    parts = len(messages)
    half_width = parts * columns // 2
    shape = (requests * rows, half_width)
    return pl.pallas_call(
        functools.partial(merge_kernel, parts, share),
        in_specs=[pl.BlockSpec(memory_space=pltpu.SMEM)]
        + [pl.BlockSpec(memory_space=pltpu.VMEM)] * (2 * parts),
        out_specs=[pl.BlockSpec(memory_space=pltpu.VMEM)] * 2,
        out_shape=[
            jax.ShapeDtypeStruct(shape, jnp.float32),
            jax.ShapeDtypeStruct(shape, jnp.bfloat16),
        ],
        scratch_shapes=[pltpu.VMEM((requests * rows, share * head_size_of(weights, share)), jnp.bfloat16)],
        name="merge_project",
    )(info, *messages, *weights)


def head_size_of(weights, share):
    return weights[0].shape[0] // share


def shift(value, axis, step):
    size = lax.axis_size(axis)
    return lax.ppermute(value, axis, [(i, (i + step) % size) for i in range(size)])


def take_block(value, index):
    return lax.dynamic_index_in_dim(value, index, 0, keepdims=False)


def gather_blocks(block, axis):
    return [block] + [shift(block, axis, s) for s in range(1, lax.axis_size(axis))]


def route_table(route_ids, route_weights):
    req_size, exp_size = lax.axis_size("req"), lax.axis_size("exp")
    req_at, exp_at = lax.axis_index("req"), lax.axis_index("exp")
    groups = req_size * exp_size
    table = jnp.sum(
        jnp.where(
            route_ids[None, :, :] == lax.iota(jnp.int32, groups)[:, None, None],
            route_weights[None, :, :],
            0.0,
        ),
        axis=2,
    )
    mine = lax.all_to_all(table, ("req", "exp"), split_axis=0, concat_axis=0, tiled=True)
    by_req = (req_at - lax.iota(jnp.int32, req_size)) % req_size
    by_exp = (exp_at - lax.iota(jnp.int32, exp_size)) % exp_size
    order = by_req[None, :] * exp_size + by_exp[:, None]
    return jnp.take(mine, order.reshape(-1), axis=0).reshape(exp_size, -1)


def halves(value, width, axis):
    head_at = lax.axis_index("head")
    own = lax.dynamic_slice_in_dim(value, head_at * width, width, axis)
    other = lax.dynamic_slice_in_dim(value, (1 - head_at) * width, width, axis)
    return own, other


def dense_experts(half_hidden, row_weights, gains, maps_in, maps_out):
    row_count, half_width = half_hidden.shape
    req_size, exp_size = lax.axis_size("req"), lax.axis_size("exp")
    sent = half_hidden.astype(jnp.bfloat16)
    column = jnp.concatenate(gather_blocks(sent, "req"), axis=0)
    blocks = gather_blocks(column, "exp")
    back = []
    for s, own in enumerate(blocks):
        other = shift(own, "head", 1)
        wide = [own.astype(jnp.float32), other.astype(jnp.float32)]
        squares = sum(jnp.sum(x * x, axis=-1, keepdims=True) for x in wide)
        factor = lax.rsqrt(squares / (2 * half_width) + norm_epsilon)
        gate_up = sum(
            jnp.dot(
                (x * factor * gain).astype(jnp.bfloat16), maps, preferred_element_type=jnp.float32
            )
            for x, gain, maps in zip(wide, gains, maps_in)
        )
        half_units = gate_up.shape[-1] // 2
        activated = (
            jax.nn.silu(gate_up[:, :half_units])
            * gate_up[:, half_units:]
        ).astype(jnp.bfloat16)
        weight = row_weights[s][:, None]
        kept, passed = [
            jnp.dot(activated, maps, preferred_element_type=jnp.float32) * weight
            for maps in maps_out
        ]
        swapped = shift(passed.astype(jnp.bfloat16), "head", 1).astype(jnp.float32)
        back.append(kept + swapped)
    plane_sum = back[0]
    for s in range(1, exp_size):
        plane_sum = plane_sum + shift(back[s].astype(jnp.bfloat16), "exp", -s).astype(jnp.float32)
    plane_sum = plane_sum.reshape(req_size, row_count, half_width)
    mixture = plane_sum[0]
    outgoing = plane_sum.astype(jnp.bfloat16)
    for s in range(1, req_size):
        mixture = mixture + shift(outgoing[s], "req", -s).astype(jnp.float32)
    return mixture


def sparse_experts(half_hidden, route_ids, route_weights, norm_gain, expert_in, expert_out, capacity):
    row_count, half_width = half_hidden.shape
    head_at = lax.axis_index("head")
    other = shift(half_hidden, "head", 1)
    first = jnp.where(head_at == 0, half_hidden, other)
    second = jnp.where(head_at == 0, other, half_hidden)
    hidden = jnp.concatenate([first, second], axis=1)
    normed = (
        hidden
        * lax.rsqrt(jnp.mean(hidden * hidden, axis=-1, keepdims=True) + norm_epsilon)
        * norm_gain
    ).astype(jnp.bfloat16)
    model_width = 2 * half_width
    local_experts = expert_in.shape[0]
    groups = lax.axis_size("req") * lax.axis_size("exp")
    experts_all = local_experts * groups
    expert_iota = lax.iota(jnp.int32, experts_all)
    named_count = jnp.sum((route_ids[:, :, None] == expert_iota).astype(jnp.int32), axis=1)
    earlier = jnp.cumsum(named_count, axis=0) - named_count
    slot_rank = jnp.take_along_axis(earlier, route_ids, axis=1)
    slot_index = route_ids * capacity + slot_rank
    slot_iota = lax.iota(jnp.int32, experts_all * capacity)
    placing = jnp.any(slot_index[None, :, :] == slot_iota[:, None, None], axis=2).astype(
        jnp.bfloat16
    )
    outgoing = jnp.dot(placing, normed, preferred_element_type=jnp.float32).astype(jnp.bfloat16)
    outgoing = outgoing.reshape(groups, local_experts, capacity, model_width)
    input_maps = expert_in.reshape(local_experts, model_width, -1)
    gate_up = jnp.einsum(
        "geci,eif->gecf",
        lax.all_to_all(outgoing, ("req", "exp"), split_axis=0, concat_axis=0, tiled=True),
        input_maps,
        preferred_element_type=jnp.float32,
    )
    half_units = gate_up.shape[-1] // 2
    activated = (jax.nn.silu(gate_up[..., :half_units]) * gate_up[..., half_units:]).astype(
        jnp.bfloat16
    )
    partial_value = jnp.einsum(
        "gecf,efi->geci", activated, expert_out, preferred_element_type=jnp.float32
    )
    summed = lax.psum_scatter(partial_value, "head", scatter_dimension=3, tiled=True).astype(
        jnp.bfloat16
    )
    returned = lax.all_to_all(summed, ("req", "exp"), split_axis=0, concat_axis=0, tiled=True)
    flat_results = returned.reshape(experts_all * capacity, half_width)
    picked = jnp.take(flat_results, slot_index, axis=0).astype(jnp.float32)
    return jnp.sum(picked * route_weights[:, :, None], axis=1)


def local(
    queries,
    new_keys,
    new_values,
    key_cache,
    value_cache,
    lengths,
    residual,
    out_weight,
    norm_gain,
    route_ids,
    route_weights,
    expert_in,
    expert_out,
):
    requests, span, kv, head_size = key_cache.shape
    heads = queries.shape[2]
    exp_size = lax.axis_size("exp")
    exp_at, head_at = lax.axis_index("exp"), lax.axis_index("head")
    share = heads // exp_size
    group = heads // kv
    sources = (exp_at - lax.iota(jnp.int32, exp_size)) % exp_size
    targets = [(exp_at + s) % exp_size for s in range(exp_size)]

    row_count, model_width = residual.shape
    half_width = model_width // 2
    groups = lax.axis_size("req") * exp_size
    experts_all = expert_in.shape[0] * groups
    capacity = max(2, 2 * row_count * route_ids.shape[1] // experts_all)
    dense = capacity >= row_count and experts_all == groups

    pieces = gather_blocks(queries, "exp")
    local_lengths = jnp.clip(lengths - exp_at * span, 0, span)
    split_weight = out_weight.reshape(exp_size, share * head_size, -1)
    weight_parts = [take_block(split_weight, targets[0])] + [
        shift(take_block(split_weight, targets[s]), "exp", s) for s in range(1, exp_size)
    ]
    if dense:
        row_weights = route_table(route_ids, route_weights)
        maps_in = halves(expert_in[0].reshape(model_width, -1), half_width, 0)
        maps_out = halves(expert_out[0], half_width, 1)
        gains = halves(norm_gain, half_width, 0)
        pieces, row_weights, maps_in, maps_out = lax.optimization_barrier(
            (pieces, row_weights, maps_in, maps_out)
        )
    messages = attend(
        pieces, sources, new_keys, new_values, key_cache, value_cache, local_lengths,
        512, 256, exp_size,
    )
    received = [take_block(messages, targets[0])] + [
        shift(take_block(messages, targets[s]), "exp", s) for s in range(1, exp_size)
    ]
    group_shift = (head_size - (exp_at * share) % group) % head_size
    info = jnp.concatenate([jnp.stack([group_shift, head_at]).astype(jnp.int32), sources])
    kept, sent = merge_project(received, weight_parts, info, share, requests)
    both = kept + shift(sent, "head", 1).astype(jnp.float32)
    both = both.reshape(exp_size, row_count, half_width)
    outgoing = both.astype(jnp.bfloat16)
    hidden = lax.dynamic_slice_in_dim(residual, head_at * half_width, half_width, 1).astype(
        jnp.float32
    ) + take_block(both, targets[0])
    for s in range(1, exp_size):
        hidden = hidden + shift(take_block(outgoing, targets[s]), "exp", s).astype(jnp.float32)

    if dense:
        mixture = dense_experts(hidden, row_weights, gains, maps_in, maps_out)
    else:
        mixture = sparse_experts(
            hidden, route_ids, route_weights, norm_gain, expert_in, expert_out, capacity
        )
    return (hidden + mixture).astype(jnp.bfloat16)


def solution(mesh):
    return jax.shard_map(
        local,
        mesh=mesh,
        in_specs=(
            P("req", "exp", "head", None),
            P("req", "exp", "head", None),
            P("req", "exp", "head", None),
            P("req", "exp", "head", None),
            P("req", "exp", "head", None),
            P("req"),
            P(("req", "exp"), None),
            P("head", "exp"),
            P(),
            P(("req", "exp"), None),
            P(("req", "exp"), None),
            P(("req", "exp"), None, None, "head"),
            P(("req", "exp"), "head", None),
        ),
        out_specs=P(("req", "exp"), "head"),
        check_vma=False,
    )
```

```python
import functools
import math
import jax
import jax.numpy as jnp
from jax import lax
from jax.experimental import pallas as pl
from jax.experimental.pallas import tpu as pltpu
from jax.sharding import PartitionSpec as P

masked_score = -1e30
norm_epsilon = 1e-06


def attend_kernel(pieces, sub, tail, factor, exp_count, info_ref, *refs):
    q_refs = refs[:pieces]
    nk_ref, nv_ref, k_ref, v_ref, o_ref = refs[pieces : pieces + 5]
    q_all, q_cat, pattern, m_scr, l_scr, acc, p_even, p_odd, stats, turned = refs[pieces + 5 :]
    requests = pl.num_programs(0)
    request = pl.program_id(0)
    head_size = k_ref.shape[2]
    kv = 2
    piece_rows, heads = q_refs[0].shape[1], q_refs[0].shape[2]
    group = heads // kv
    rows = piece_rows * pieces
    lanes = rows * group
    length = info_ref[request]
    even_lane = lax.broadcasted_iota(jnp.int32, (lanes, 128), 1) % 2 == 0

    @pl.when(request == 0)
    def _():
        stats[...] = jnp.zeros_like(stats)
        parity = lax.broadcasted_iota(jnp.int32, (16, head_size), 0) % 2
        pattern[0] = (1 - parity).astype(jnp.float32).astype(jnp.bfloat16)
        pattern[1] = parity.astype(jnp.float32).astype(jnp.bfloat16)

    for piece in range(pieces):
        where_to = info_ref[requests + piece] * piece_rows
        q_all[pl.ds(where_to, piece_rows)] = q_refs[piece][0].astype(jnp.float32)
    for head in range(kv):
        chosen = q_all[:, head * group : (head + 1) * group, :].reshape(lanes, head_size)
        q_cat[:, head * head_size : (head + 1) * head_size] = chosen.astype(jnp.bfloat16)

    def spread(block):
        if block.shape[0] < 16:
            left = block * pattern[0, : block.shape[0]]
            right = block * pattern[1, : block.shape[0]]
        else:
            tiles = block.reshape(block.shape[0] // 16, 16, head_size)
            left = (tiles * pattern[0][None]).reshape(block.shape)
            right = (tiles * pattern[1][None]).reshape(block.shape)
        return jnp.concatenate([left, right], axis=1)

    def score(block):
        return lax.dot_general(
            q_cat[...],
            spread(block),
            (((1,), (1,)), ((), ())),
            preferred_element_type=jnp.float32,
        )

    def both_columns(even, odd):
        shape = (lanes, 128)
        return jnp.where(even_lane, jnp.broadcast_to(even, shape), jnp.broadcast_to(odd, shape))

    def reduce_parity(wide, op, neutral):
        even = op(jnp.where(even_lane, wide, neutral), axis=1, keepdims=True)
        odd = op(jnp.where(even_lane, neutral, wide), axis=1, keepdims=True)
        return even, odd

    def init():
        scores = score(nk_ref[0]) * factor
        fresh = scores.shape[1]
        even = lax.broadcasted_iota(jnp.int32, scores.shape, 1) % 2 == 0
        top_even = jnp.max(jnp.where(even, scores, -jnp.inf), axis=1, keepdims=True)
        top_odd = jnp.max(jnp.where(even, -jnp.inf, scores), axis=1, keepdims=True)
        top_even = top_even.astype(jnp.bfloat16).astype(jnp.float32)
        top_odd = top_odd.astype(jnp.bfloat16).astype(jnp.float32)
        m_scr[...] = both_columns(top_even, top_odd)
        probs = jnp.exp2(
            scores
            - jnp.where(
                even,
                jnp.broadcast_to(top_even, scores.shape),
                jnp.broadcast_to(top_odd, scores.shape),
            )
        )
        l_even = jnp.sum(jnp.where(even, probs, 0.0), axis=1, keepdims=True)
        l_odd = jnp.sum(jnp.where(even, 0.0, probs), axis=1, keepdims=True)
        lane = lax.broadcasted_iota(jnp.int32, (lanes, 128), 1)
        l_scr[...] = jnp.where(lane < 2, both_columns(l_even, l_odd), 0.0)
        acc[...] = jnp.dot(
            probs.astype(jnp.bfloat16), spread(nv_ref[0]), preferred_element_type=jnp.float32
        )

    def piece_of(ref, start, size):
        return ref[0, pl.ds(pl.multiple_of(start * kv, kv * tail), size * kv), :]

    step = 256

    def soften(start, size, target, masked):
        top = m_scr[...]
        total = l_scr[...]
        for tile in range(size * kv // step):
            scores = score(piece_of_tile(k_ref, start, tile))
            for part in range(step // 128):
                piece = scores[:, part * 128 : (part + 1) * 128]
                probs = jnp.exp2(piece * factor - top)
                if masked:
                    lane = lax.broadcasted_iota(jnp.int32, (1, 128), 1)
                    position = start + (tile * step + part * 128 + lane) // kv
                    probs = jnp.where(position < length, probs, 0.0)
                total = total + probs
                at = tile * step + part * 128
                target[:, at : at + 128] = probs.astype(jnp.bfloat16)
        l_scr[...] = total

    def piece_of_tile(ref, start, tile):
        first = pl.multiple_of(start * kv, kv * tail) + tile * step
        return ref[0, pl.ds(first, step), :]

    def weigh(start, size, source):
        values = spread(piece_of(v_ref, start, size))
        acc[...] += jnp.dot(source[:, : size * kv], values, preferred_element_type=jnp.float32)

    init()
    here = length
    pairs = here // (2 * sub)

    def loop(i, carry):
        start = pl.multiple_of(i * 2 * sub, 2 * sub)
        before = jnp.maximum(start - sub, 0)
        soften(start, sub, p_even, False)
        weigh(before, sub, p_odd)
        soften(start + sub, sub, p_odd, False)
        weigh(start, sub, p_even)
        return carry

    p_odd[...] = jnp.zeros_like(p_odd)
    lax.fori_loop(0, pairs, loop, 0)
    weigh(pl.multiple_of(jnp.maximum(pairs * 2 * sub - sub, 0), sub), sub, p_odd)

    def tail_loop(i, carry):
        start = pl.multiple_of(pairs * 2 * sub + i * tail, tail)
        soften(start, tail, p_even, True)
        weigh(start, tail, p_even)
        return carry

    lax.fori_loop(0, (here - pairs * 2 * sub + tail - 1) // tail, tail_loop, 0)
    largest = jnp.max(l_scr[...])

    @pl.when(jnp.logical_not(largest < 1e30))
    def _():
        init()

        def slow_loop(i, carry):
            start = pl.multiple_of(i * tail, tail)
            scores = score(piece_of(k_ref, start, tail)) * factor
            lane = lax.broadcasted_iota(jnp.int32, (1, tail * kv), 1)
            inside = start + lane // kv < length
            scores = jnp.where(inside, scores, masked_score)
            wide = m_scr[...]
            for part in range(tail * kv // 128):
                wide = jnp.maximum(wide, scores[:, part * 128 : (part + 1) * 128])
            even, odd = reduce_parity(wide, jnp.max, -jnp.inf)
            even = even.astype(jnp.bfloat16).astype(jnp.float32)
            odd = odd.astype(jnp.bfloat16).astype(jnp.float32)
            top = both_columns(even, odd)
            fade = jnp.exp2(m_scr[...] - top)
            total = l_scr[...] * fade
            for part in range(tail * kv // 128):
                at = part * 128
                probs = jnp.where(
                    inside[:, at : at + 128], jnp.exp2(scores[:, at : at + 128] - top), 0.0
                )
                total = total + probs
                p_even[:, at : at + 128] = probs.astype(jnp.bfloat16)
            l_scr[...] = total
            m_scr[...] = top
            for head in range(kv):
                columns = slice(head * head_size, (head + 1) * head_size)
                acc[:, columns] = acc[:, columns] * jnp.broadcast_to(
                    fade[:, head : head + 1], (lanes, head_size)
                )
            weigh(start, tail, p_even)
            return carry

        lax.fori_loop(0, (here + tail - 1) // tail, slow_loop, 0)

    share = heads // exp_count
    totals = reduce_parity(l_scr[...], jnp.sum, 0.0)
    lane = lax.broadcasted_iota(jnp.int32, (lanes, head_size), 1)
    member_of_row = lax.broadcasted_iota(jnp.int32, (lanes, head_size), 0) % group
    for head in range(kv):
        total = totals[head]
        inverse = jnp.broadcast_to(1.0 / total, (lanes, head_size))
        columns = slice(head * head_size, (head + 1) * head_size)
        turned[...] = acc[:, columns] * inverse
        upper = total.astype(jnp.bfloat16).astype(jnp.float32)
        kinds = [upper, m_scr[:, head : head + 1], total - upper]
        placed = jnp.zeros((lanes, head_size), jnp.float32)
        for kind, column in enumerate(kinds):
            placed = jnp.where(
                lane == member_of_row + 8 * kind,
                jnp.broadcast_to(column, placed.shape),
                placed,
            )
        gathered = jnp.sum(placed.reshape(rows, group, head_size), axis=1)
        stats[head] = stats[head] + pltpu.roll(gathered, 24 * request, 1)
        for member in range(group):
            index = head * group + member
            target, inside = index // share, index % share
            offset = pl.multiple_of(
                request * (share * head_size) + inside * head_size, head_size
            )
            o_ref[target, :, pl.ds(offset, head_size)] = turned[
                pl.ds(member, rows, stride=group), :
            ].astype(jnp.bfloat16)

    @pl.when(request == requests - 1)
    def _():
        for target in range(exp_count):
            head = target * share // group
            o_ref[target, :, requests * share * head_size :] = stats[head].astype(jnp.bfloat16)


def attend(queries, order, new_keys, new_values, keys, values, local_lengths, sub, tail, exp_count):
    requests, span, kv, head_size = keys.shape
    piece_rows, heads = queries[0].shape[1:3]
    pieces = len(queries)
    rows = piece_rows * pieces
    share = heads // exp_count
    fresh = new_keys.shape[1]
    width = requests * share * head_size + 128
    info = jnp.concatenate([local_lengths, order])
    factor = head_size ** (-0.5) * math.log2(math.e)
    lanes = rows * heads // kv
    flat = lambda x: x.reshape(requests, x.shape[1] * kv, head_size)
    block = lambda n: pl.BlockSpec((1, n, head_size), lambda r, info: (r, 0, 0))
    return pl.pallas_call(
        functools.partial(attend_kernel, pieces, sub, tail, factor, exp_count),
        grid_spec=pltpu.PrefetchScalarGridSpec(
            num_scalar_prefetch=1,
            grid=(requests,),
            in_specs=[
                pl.BlockSpec((1, piece_rows, heads, head_size), lambda r, info: (r, 0, 0, 0))
            ]
            * pieces
            + [block(fresh * kv), block(fresh * kv), block(span * kv), block(span * kv)],
            out_specs=pl.BlockSpec((exp_count, rows, width), lambda r, info: (0, 0, 0)),
            scratch_shapes=[
                pltpu.VMEM((rows, heads, head_size), jnp.float32),
                pltpu.VMEM((lanes, kv * head_size), jnp.bfloat16),
                pltpu.VMEM((2, 16, head_size), jnp.bfloat16),
                pltpu.VMEM((lanes, 128), jnp.float32),
                pltpu.VMEM((lanes, 128), jnp.float32),
                pltpu.VMEM((lanes, kv * head_size), jnp.float32),
                pltpu.VMEM((lanes, 2 * sub * kv), jnp.bfloat16),
                pltpu.VMEM((lanes, sub * kv), jnp.bfloat16),
                pltpu.VMEM((kv, rows, head_size), jnp.float32),
                pltpu.VMEM((lanes, head_size), jnp.float32),
            ],
        ),
        out_shape=jax.ShapeDtypeStruct((exp_count, rows, width), jnp.bfloat16),
        compiler_params=pltpu.CompilerParams(dimension_semantics=("arbitrary",)),
        name="attend",
    )(info, *queries, flat(new_keys), flat(new_values), flat(keys), flat(values))


def merge_kernel(parts, share, info_ref, *refs):
    x_refs = refs[:parts]
    w_refs = refs[parts : 2 * parts]
    keep_ref, send_ref, attn = refs[2 * parts :]
    rows, width = x_refs[0].shape
    head_size = 128
    requests = (width - head_size) // (share * head_size)
    group_shift = info_ref[0]
    half = info_ref[1]
    tables = []
    for x_ref in x_refs:
        table = x_ref[:, width - head_size :].astype(jnp.float32)
        tables.append(pltpu.roll(table, group_shift, 1))
    for request in range(requests):
        for member in range(share):
            at = 24 * request + member
            tops = [t[:, at + 8 : at + 9] for t in tables]
            sums = [t[:, at : at + 1] + t[:, at + 16 : at + 17] for t in tables]
            top = functools.reduce(jnp.maximum, tops)
            weights = [s * jnp.exp2(m - top) for s, m in zip(sums, tops)]
            inverse = 1.0 / functools.reduce(jnp.add, weights)
            start = (request * share + member) * head_size
            mixed = jnp.zeros((rows, head_size), jnp.float32)
            for weight, x_ref in zip(weights, x_refs):
                part = x_ref[:, start : start + head_size].astype(jnp.float32)
                mixed = mixed + jnp.broadcast_to(weight * inverse, part.shape) * part
            attn[
                request * rows : (request + 1) * rows, member * head_size : (member + 1) * head_size
            ] = mixed.astype(jnp.bfloat16)
    columns = w_refs[0].shape[1]
    per_half = keep_ref.shape[1] // columns
    for part in range(parts):
        made = jnp.dot(attn[...], w_refs[part][...], preferred_element_type=jnp.float32)
        chunk = info_ref[2 + part]
        inside = pl.multiple_of((chunk % per_half) * columns, columns)

        @pl.when(chunk // per_half == half)
        def _():
            keep_ref[:, pl.ds(inside, columns)] = made

        @pl.when(chunk // per_half != half)
        def _():
            send_ref[:, pl.ds(inside, columns)] = made.astype(jnp.bfloat16)


def merge_project(messages, weights, info, share, requests):
    rows, width = messages[0].shape
    columns = weights[0].shape[1]
    parts = len(messages)
    half_width = parts * columns // 2
    shape = (requests * rows, half_width)
    return pl.pallas_call(
        functools.partial(merge_kernel, parts, share),
        in_specs=[pl.BlockSpec(memory_space=pltpu.SMEM)]
        + [pl.BlockSpec(memory_space=pltpu.VMEM)] * (2 * parts),
        out_specs=[pl.BlockSpec(memory_space=pltpu.VMEM)] * 2,
        out_shape=[
            jax.ShapeDtypeStruct(shape, jnp.float32),
            jax.ShapeDtypeStruct(shape, jnp.bfloat16),
        ],
        scratch_shapes=[pltpu.VMEM((requests * rows, share * head_size_of(weights, share)), jnp.bfloat16)],
        name="merge_project",
    )(info, *messages, *weights)


def head_size_of(weights, share):
    return weights[0].shape[0] // share


def shift(value, axis, step):
    size = lax.axis_size(axis)
    return lax.ppermute(value, axis, [(i, (i + step) % size) for i in range(size)])


def take_block(value, index):
    return lax.dynamic_index_in_dim(value, index, 0, keepdims=False)


def gather_blocks(block, axis):
    return [block] + [shift(block, axis, s) for s in range(1, lax.axis_size(axis))]


def swap(value, axis, bits):
    size = lax.axis_size(axis)
    return lax.ppermute(value, axis, [(i, i ^ bits) for i in range(size)])


def route_table(route_ids, route_weights):
    groups = lax.axis_size("req") * lax.axis_size("exp")
    return jnp.sum(
        jnp.where(
            route_ids[None, :, :] == lax.iota(jnp.int32, groups)[:, None, None],
            route_weights[None, :, :],
            0.0,
        ),
        axis=2,
    )


def exchange_table(table):
    req_size, exp_size = lax.axis_size("req"), lax.axis_size("exp")
    mine = lax.all_to_all(table, ("req", "exp"), split_axis=0, concat_axis=0, tiled=True)
    by_req = (lax.axis_index("req") - lax.iota(jnp.int32, req_size)) % req_size
    by_exp = lax.axis_index("exp") ^ lax.iota(jnp.int32, exp_size)
    order = by_req[None, :] * exp_size + by_exp[:, None]
    return jnp.take(mine, order.reshape(-1), axis=0).reshape(exp_size, -1)


def halves(value, width, axis):
    head_at = lax.axis_index("head")
    own = lax.dynamic_slice_in_dim(value, head_at * width, width, axis)
    other = lax.dynamic_slice_in_dim(value, (1 - head_at) * width, width, axis)
    return own, other


def expert_block(own, weights, gains, maps_in, maps_out):
    other = swap(own, "head", 1)
    wide = [own.astype(jnp.float32), other.astype(jnp.float32)]
    squares = sum(jnp.sum(x * x, axis=-1, keepdims=True) for x in wide)
    factor = lax.rsqrt(squares / (2 * own.shape[1]) + norm_epsilon)
    gate_up = sum(
        jnp.dot((x * factor * gain).astype(jnp.bfloat16), maps, preferred_element_type=jnp.float32)
        for x, gain, maps in zip(wide, gains, maps_in)
    )
    half_units = gate_up.shape[-1] // 2
    activated = (jax.nn.silu(gate_up[:, :half_units]) * gate_up[:, half_units:]).astype(
        jnp.bfloat16
    )
    kept, passed = [
        jnp.dot(activated, maps, preferred_element_type=jnp.float32) * weights[:, None]
        for maps in maps_out
    ]
    return kept + swap(passed.astype(jnp.bfloat16), "head", 1).astype(jnp.float32)


def dense_experts(half_hidden, table, gains, maps_in, maps_out):
    row_count, half_width = half_hidden.shape
    req_size = lax.axis_size("req")
    sent = half_hidden.astype(jnp.bfloat16)
    column = jnp.concatenate(gather_blocks(sent, "req"), axis=0)
    column, table = lax.optimization_barrier((column, table))
    row_weights = exchange_table(table)
    middle = column.shape[0] // 2

    def run(block, weights):
        return expert_block(block, weights, gains, maps_in, maps_out)

    def over(value, bits):
        return swap(value.astype(jnp.bfloat16), "exp", bits).astype(jnp.float32)

    near_x = swap(column, "exp", 1)
    near_y = swap(column, "exp", 2)
    far_top = swap(near_x[:middle], "exp", 2)
    far_low = swap(near_y[middle:], "exp", 1)
    own = run(column, row_weights[0])
    for_x = run(near_x, row_weights[1])
    for_y = run(near_y, row_weights[2])
    top = own[:middle] + over(for_x[:middle], 1)
    low = own[middle:] + over(for_y[middle:], 2)
    far = run(jnp.concatenate([far_top, far_low], axis=0), row_weights[3])
    top = top + over(for_y[:middle] + over(far[:middle], 1), 2)
    low = low + over(for_x[middle:] + over(far[middle:], 2), 1)
    plane_sum = jnp.concatenate([top, low], axis=0).reshape(req_size, row_count, half_width)
    mixture = plane_sum[0]
    outgoing = plane_sum.astype(jnp.bfloat16)
    for s in range(1, req_size):
        mixture = mixture + shift(outgoing[s], "req", -s).astype(jnp.float32)
    return mixture


def sparse_experts(half_hidden, route_ids, route_weights, norm_gain, expert_in, expert_out, capacity):
    row_count, half_width = half_hidden.shape
    head_at = lax.axis_index("head")
    other = shift(half_hidden, "head", 1)
    first = jnp.where(head_at == 0, half_hidden, other)
    second = jnp.where(head_at == 0, other, half_hidden)
    hidden = jnp.concatenate([first, second], axis=1)
    normed = (
        hidden
        * lax.rsqrt(jnp.mean(hidden * hidden, axis=-1, keepdims=True) + norm_epsilon)
        * norm_gain
    ).astype(jnp.bfloat16)
    model_width = 2 * half_width
    local_experts = expert_in.shape[0]
    groups = lax.axis_size("req") * lax.axis_size("exp")
    experts_all = local_experts * groups
    expert_iota = lax.iota(jnp.int32, experts_all)
    named_count = jnp.sum((route_ids[:, :, None] == expert_iota).astype(jnp.int32), axis=1)
    earlier = jnp.cumsum(named_count, axis=0) - named_count
    slot_rank = jnp.take_along_axis(earlier, route_ids, axis=1)
    slot_index = route_ids * capacity + slot_rank
    slot_iota = lax.iota(jnp.int32, experts_all * capacity)
    placing = jnp.any(slot_index[None, :, :] == slot_iota[:, None, None], axis=2).astype(
        jnp.bfloat16
    )
    outgoing = jnp.dot(placing, normed, preferred_element_type=jnp.float32).astype(jnp.bfloat16)
    outgoing = outgoing.reshape(groups, local_experts, capacity, model_width)
    input_maps = expert_in.reshape(local_experts, model_width, -1)
    gate_up = jnp.einsum(
        "geci,eif->gecf",
        lax.all_to_all(outgoing, ("req", "exp"), split_axis=0, concat_axis=0, tiled=True),
        input_maps,
        preferred_element_type=jnp.float32,
    )
    half_units = gate_up.shape[-1] // 2
    activated = (jax.nn.silu(gate_up[..., :half_units]) * gate_up[..., half_units:]).astype(
        jnp.bfloat16
    )
    partial_value = jnp.einsum(
        "gecf,efi->geci", activated, expert_out, preferred_element_type=jnp.float32
    )
    summed = lax.psum_scatter(partial_value, "head", scatter_dimension=3, tiled=True).astype(
        jnp.bfloat16
    )
    returned = lax.all_to_all(summed, ("req", "exp"), split_axis=0, concat_axis=0, tiled=True)
    flat_results = returned.reshape(experts_all * capacity, half_width)
    picked = jnp.take(flat_results, slot_index, axis=0).astype(jnp.float32)
    return jnp.sum(picked * route_weights[:, :, None], axis=1)


def local(
    queries,
    new_keys,
    new_values,
    key_cache,
    value_cache,
    lengths,
    residual,
    out_weight,
    norm_gain,
    route_ids,
    route_weights,
    expert_in,
    expert_out,
):
    requests, span, kv, head_size = key_cache.shape
    heads = queries.shape[2]
    exp_size = lax.axis_size("exp")
    exp_at, head_at = lax.axis_index("exp"), lax.axis_index("head")
    share = heads // exp_size
    group = heads // kv
    sources = (exp_at - lax.iota(jnp.int32, exp_size)) % exp_size
    targets = [(exp_at + s) % exp_size for s in range(exp_size)]

    row_count, model_width = residual.shape
    half_width = model_width // 2
    groups = lax.axis_size("req") * exp_size
    experts_all = expert_in.shape[0] * groups
    capacity = max(2, 2 * row_count * route_ids.shape[1] // experts_all)
    dense = capacity >= row_count and experts_all == groups and exp_size == 4

    pieces = gather_blocks(queries, "exp")
    local_lengths = jnp.clip(lengths - exp_at * span, 0, span)
    split_weight = out_weight.reshape(exp_size, share * head_size, -1)
    weight_parts = [take_block(split_weight, targets[0])] + [
        shift(take_block(split_weight, targets[s]), "exp", s) for s in range(1, exp_size)
    ]
    messages = attend(
        pieces, sources, new_keys, new_values, key_cache, value_cache, local_lengths,
        512, 256, exp_size,
    )
    received = [take_block(messages, targets[0])] + [
        shift(take_block(messages, targets[s]), "exp", s) for s in range(1, exp_size)
    ]
    if dense:
        table = route_table(route_ids, route_weights)
        maps_in = halves(expert_in[0].reshape(model_width, -1), half_width, 0)
        maps_out = halves(expert_out[0], half_width, 1)
        gains = halves(norm_gain, half_width, 0)
        own_message = received[0]
        own_message, maps_in, maps_out = lax.optimization_barrier(
            (own_message, maps_in, maps_out)
        )
        received = [own_message] + received[1:]
    group_shift = (head_size - (exp_at * share) % group) % head_size
    info = jnp.concatenate([jnp.stack([group_shift, head_at]).astype(jnp.int32), sources])
    kept, sent = merge_project(received, weight_parts, info, share, requests)
    both = kept + shift(sent, "head", 1).astype(jnp.float32)
    both = both.reshape(exp_size, row_count, half_width)
    outgoing = both.astype(jnp.bfloat16)
    hidden = lax.dynamic_slice_in_dim(residual, head_at * half_width, half_width, 1).astype(
        jnp.float32
    ) + take_block(both, targets[0])
    for s in range(1, exp_size):
        hidden = hidden + shift(take_block(outgoing, targets[s]), "exp", s).astype(jnp.float32)

    if dense:
        mixture = dense_experts(hidden, table, gains, maps_in, maps_out)
    else:
        mixture = sparse_experts(
            hidden, route_ids, route_weights, norm_gain, expert_in, expert_out, capacity
        )
    return (hidden + mixture).astype(jnp.bfloat16)


def solution(mesh):
    return jax.shard_map(
        local,
        mesh=mesh,
        in_specs=(
            P("req", "exp", "head", None),
            P("req", "exp", "head", None),
            P("req", "exp", "head", None),
            P("req", "exp", "head", None),
            P("req", "exp", "head", None),
            P("req"),
            P(("req", "exp"), None),
            P("head", "exp"),
            P(),
            P(("req", "exp"), None),
            P(("req", "exp"), None),
            P(("req", "exp"), None, None, "head"),
            P(("req", "exp"), "head", None),
        ),
        out_specs=P(("req", "exp"), "head"),
        check_vma=False,
    )
```

```python
import functools
import math
import jax
import jax.numpy as jnp
from jax import lax
from jax.experimental import pallas as pl
from jax.experimental.pallas import tpu as pltpu
from jax.sharding import PartitionSpec as P

masked_score = -1e30
norm_epsilon = 1e-06


def attend_kernel(pieces, base, listed, sub, tail, factor, exp_count, info_ref, *refs):
    q_refs = refs[:pieces]
    nk_ref, nv_ref, k_ref, v_ref = refs[pieces : pieces + 4]
    out_refs = refs[pieces + 4 : pieces + 4 + exp_count]
    scratch = refs[pieces + 4 + exp_count :]
    q_all, q_cat, pattern, m_scr, l_scr, acc, p_even, p_odd, stats, turned, staged = scratch
    requests = pl.num_programs(0)
    request = pl.program_id(0)
    head_size = k_ref.shape[2]
    kv = 2
    piece_rows, heads = q_refs[0].shape[1], q_refs[0].shape[2]
    group = heads // kv
    rows = piece_rows * pieces
    lanes = rows * group
    length = info_ref[request + base]
    even_lane = lax.broadcasted_iota(jnp.int32, (lanes, 128), 1) % 2 == 0

    @pl.when(request == 0)
    def _():
        stats[...] = jnp.zeros_like(stats)
        parity = lax.broadcasted_iota(jnp.int32, (16, head_size), 0) % 2
        pattern[0] = (1 - parity).astype(jnp.float32).astype(jnp.bfloat16)
        pattern[1] = parity.astype(jnp.float32).astype(jnp.bfloat16)

    for piece in range(pieces):
        where_to = info_ref[listed + piece] * piece_rows
        q_all[pl.ds(where_to, piece_rows)] = q_refs[piece][0].astype(jnp.float32)
    for head in range(kv):
        chosen = q_all[:, head * group : (head + 1) * group, :].reshape(lanes, head_size)
        q_cat[:, head * head_size : (head + 1) * head_size] = chosen.astype(jnp.bfloat16)

    def spread(block):
        if block.shape[0] < 16:
            left = block * pattern[0, : block.shape[0]]
            right = block * pattern[1, : block.shape[0]]
        else:
            tiles = block.reshape(block.shape[0] // 16, 16, head_size)
            left = (tiles * pattern[0][None]).reshape(block.shape)
            right = (tiles * pattern[1][None]).reshape(block.shape)
        return jnp.concatenate([left, right], axis=1)

    def score(block):
        return lax.dot_general(
            q_cat[...],
            spread(block),
            (((1,), (1,)), ((), ())),
            preferred_element_type=jnp.float32,
        )

    def both_columns(even, odd):
        shape = (lanes, 128)
        return jnp.where(even_lane, jnp.broadcast_to(even, shape), jnp.broadcast_to(odd, shape))

    def reduce_parity(wide, op, neutral):
        even = op(jnp.where(even_lane, wide, neutral), axis=1, keepdims=True)
        odd = op(jnp.where(even_lane, neutral, wide), axis=1, keepdims=True)
        return even, odd

    def init():
        scores = score(nk_ref[0]) * factor
        fresh = scores.shape[1]
        even = lax.broadcasted_iota(jnp.int32, scores.shape, 1) % 2 == 0
        top_even = jnp.max(jnp.where(even, scores, -jnp.inf), axis=1, keepdims=True)
        top_odd = jnp.max(jnp.where(even, -jnp.inf, scores), axis=1, keepdims=True)
        top_even = top_even.astype(jnp.bfloat16).astype(jnp.float32)
        top_odd = top_odd.astype(jnp.bfloat16).astype(jnp.float32)
        m_scr[...] = both_columns(top_even, top_odd)
        probs = jnp.exp2(
            scores
            - jnp.where(
                even,
                jnp.broadcast_to(top_even, scores.shape),
                jnp.broadcast_to(top_odd, scores.shape),
            )
        )
        l_even = jnp.sum(jnp.where(even, probs, 0.0), axis=1, keepdims=True)
        l_odd = jnp.sum(jnp.where(even, 0.0, probs), axis=1, keepdims=True)
        lane = lax.broadcasted_iota(jnp.int32, (lanes, 128), 1)
        l_scr[...] = jnp.where(lane < 2, both_columns(l_even, l_odd), 0.0)
        acc[...] = jnp.dot(
            probs.astype(jnp.bfloat16), spread(nv_ref[0]), preferred_element_type=jnp.float32
        )

    def piece_of(ref, start, size):
        return ref[0, pl.ds(pl.multiple_of(start * kv, kv * tail), size * kv), :]

    step = 256

    def soften(start, size, target, masked):
        top = m_scr[...]
        total = l_scr[...]
        for tile in range(size * kv // step):
            scores = score(piece_of_tile(k_ref, start, tile))
            for part in range(step // 128):
                piece = scores[:, part * 128 : (part + 1) * 128]
                probs = jnp.exp2(piece * factor - top)
                if masked:
                    lane = lax.broadcasted_iota(jnp.int32, (1, 128), 1)
                    position = start + (tile * step + part * 128 + lane) // kv
                    probs = jnp.where(position < length, probs, 0.0)
                total = total + probs
                at = tile * step + part * 128
                target[:, at : at + 128] = probs.astype(jnp.bfloat16)
        l_scr[...] = total

    def piece_of_tile(ref, start, tile):
        first = pl.multiple_of(start * kv, kv * tail) + tile * step
        return ref[0, pl.ds(first, step), :]

    def weigh(start, size, source):
        values = spread(piece_of(v_ref, start, size))
        acc[...] += jnp.dot(source[:, : size * kv], values, preferred_element_type=jnp.float32)

    init()
    here = length
    pairs = here // (2 * sub)

    def loop(i, carry):
        start = pl.multiple_of(i * 2 * sub, 2 * sub)
        before = jnp.maximum(start - sub, 0)
        soften(start, sub, p_even, False)
        weigh(before, sub, p_odd)
        soften(start + sub, sub, p_odd, False)
        weigh(start, sub, p_even)
        return carry

    p_odd[...] = jnp.zeros_like(p_odd)
    lax.fori_loop(0, pairs, loop, 0)
    weigh(pl.multiple_of(jnp.maximum(pairs * 2 * sub - sub, 0), sub), sub, p_odd)

    def tail_loop(i, carry):
        start = pl.multiple_of(pairs * 2 * sub + i * tail, tail)
        soften(start, tail, p_even, True)
        weigh(start, tail, p_even)
        return carry

    lax.fori_loop(0, (here - pairs * 2 * sub + tail - 1) // tail, tail_loop, 0)
    largest = jnp.max(l_scr[...])

    @pl.when(jnp.logical_not(largest < 1e30))
    def _():
        init()

        def slow_loop(i, carry):
            start = pl.multiple_of(i * tail, tail)
            scores = score(piece_of(k_ref, start, tail)) * factor
            lane = lax.broadcasted_iota(jnp.int32, (1, tail * kv), 1)
            inside = start + lane // kv < length
            scores = jnp.where(inside, scores, masked_score)
            wide = m_scr[...]
            for part in range(tail * kv // 128):
                wide = jnp.maximum(wide, scores[:, part * 128 : (part + 1) * 128])
            even, odd = reduce_parity(wide, jnp.max, -jnp.inf)
            even = even.astype(jnp.bfloat16).astype(jnp.float32)
            odd = odd.astype(jnp.bfloat16).astype(jnp.float32)
            top = both_columns(even, odd)
            fade = jnp.exp2(m_scr[...] - top)
            total = l_scr[...] * fade
            for part in range(tail * kv // 128):
                at = part * 128
                probs = jnp.where(
                    inside[:, at : at + 128], jnp.exp2(scores[:, at : at + 128] - top), 0.0
                )
                total = total + probs
                p_even[:, at : at + 128] = probs.astype(jnp.bfloat16)
            l_scr[...] = total
            m_scr[...] = top
            for head in range(kv):
                columns = slice(head * head_size, (head + 1) * head_size)
                acc[:, columns] = acc[:, columns] * jnp.broadcast_to(
                    fade[:, head : head + 1], (lanes, head_size)
                )
            weigh(start, tail, p_even)
            return carry

        lax.fori_loop(0, (here + tail - 1) // tail, slow_loop, 0)

    share = heads // exp_count
    totals = reduce_parity(l_scr[...], jnp.sum, 0.0)
    lane = lax.broadcasted_iota(jnp.int32, (lanes, head_size), 1)
    member_of_row = lax.broadcasted_iota(jnp.int32, (lanes, head_size), 0) % group
    for head in range(kv):
        total = totals[head]
        inverse = jnp.broadcast_to(1.0 / total, (lanes, head_size))
        columns = slice(head * head_size, (head + 1) * head_size)
        turned[...] = acc[:, columns] * inverse
        upper = total.astype(jnp.bfloat16).astype(jnp.float32)
        kinds = [upper, m_scr[:, head : head + 1], total - upper]
        placed = jnp.zeros((lanes, head_size), jnp.float32)
        for kind, column in enumerate(kinds):
            placed = jnp.where(
                lane == member_of_row + 8 * kind,
                jnp.broadcast_to(column, placed.shape),
                placed,
            )
        gathered = jnp.sum(placed.reshape(rows, group, head_size), axis=1)
        stats[head] = stats[head] + pltpu.roll(gathered, 24 * request, 1)
        for member in range(group):
            index = head * group + member
            target, inside = index // share, index % share
            offset = pl.multiple_of(
                request * (share * head_size) + inside * head_size, head_size
            )
            staged[target, :, pl.ds(offset, head_size)] = turned[
                pl.ds(member, rows, stride=group), :
            ].astype(jnp.bfloat16)

    @pl.when(request == requests - 1)
    def _():
        for target in range(exp_count):
            head = target * share // group
            staged[target, :, requests * share * head_size :] = stats[head].astype(jnp.bfloat16)
        for step_away in range(exp_count):
            out_refs[step_away][...] = staged[info_ref[listed + (-step_away) % exp_count]]


def attend(queries, order, new_keys, new_values, keys, values, local_lengths, base, sub, tail):
    listed, span, kv, head_size = keys.shape
    requests, piece_rows, heads = queries[0].shape[:3]
    pieces = exp_count = len(queries)
    rows = piece_rows * pieces
    share = heads // exp_count
    fresh = new_keys.shape[1]
    width = requests * share * head_size + 128
    info = jnp.concatenate([local_lengths, order])
    factor = head_size ** (-0.5) * math.log2(math.e)
    lanes = rows * heads // kv
    flat = lambda x: x.reshape(listed, x.shape[1] * kv, head_size)
    block = lambda n: pl.BlockSpec((1, n, head_size), lambda r, info: (r + base, 0, 0))
    return pl.pallas_call(
        functools.partial(attend_kernel, pieces, base, listed, sub, tail, factor, exp_count),
        grid_spec=pltpu.PrefetchScalarGridSpec(
            num_scalar_prefetch=1,
            grid=(requests,),
            in_specs=[
                pl.BlockSpec((1, piece_rows, heads, head_size), lambda r, info: (r, 0, 0, 0))
            ]
            * pieces
            + [block(fresh * kv), block(fresh * kv), block(span * kv), block(span * kv)],
            out_specs=[pl.BlockSpec((rows, width), lambda r, info: (0, 0))] * exp_count,
            scratch_shapes=[
                pltpu.VMEM((rows, heads, head_size), jnp.float32),
                pltpu.VMEM((lanes, kv * head_size), jnp.bfloat16),
                pltpu.VMEM((2, 16, head_size), jnp.bfloat16),
                pltpu.VMEM((lanes, 128), jnp.float32),
                pltpu.VMEM((lanes, 128), jnp.float32),
                pltpu.VMEM((lanes, kv * head_size), jnp.float32),
                pltpu.VMEM((lanes, sub * kv), jnp.bfloat16),
                pltpu.VMEM((lanes, sub * kv), jnp.bfloat16),
                pltpu.VMEM((kv, rows, head_size), jnp.float32),
                pltpu.VMEM((lanes, head_size), jnp.float32),
                pltpu.VMEM((exp_count, rows, width), jnp.bfloat16),
            ],
        ),
        out_shape=[jax.ShapeDtypeStruct((rows, width), jnp.bfloat16)] * exp_count,
        compiler_params=pltpu.CompilerParams(dimension_semantics=("arbitrary",)),
        name="attend",
    )(info, *queries, flat(new_keys), flat(new_values), flat(keys), flat(values))


def merge_kernel(parts, batches, share, info_ref, *refs):
    w_refs = refs[batches * parts : (batches + 1) * parts]
    keep_ref, send_ref, attn = refs[(batches + 1) * parts :]
    rows, width = refs[0].shape
    head_size = 128
    requests = (width - head_size) // (share * head_size)
    group_shift = info_ref[0]
    half = info_ref[1]
    for batch in range(batches):
        x_refs = refs[batch * parts : (batch + 1) * parts]
        tables = []
        for x_ref in x_refs:
            table = x_ref[:, width - head_size :].astype(jnp.float32)
            tables.append(pltpu.roll(table, group_shift, 1))
        for request in range(requests):
            first = (batch * requests + request) * rows
            for member in range(share):
                at = 24 * request + member
                tops = [t[:, at + 8 : at + 9] for t in tables]
                sums = [t[:, at : at + 1] + t[:, at + 16 : at + 17] for t in tables]
                top = functools.reduce(jnp.maximum, tops)
                weights = [s * jnp.exp2(m - top) for s, m in zip(sums, tops)]
                inverse = 1.0 / functools.reduce(jnp.add, weights)
                start = (request * share + member) * head_size
                mixed = jnp.zeros((rows, head_size), jnp.float32)
                for weight, x_ref in zip(weights, x_refs):
                    part = x_ref[:, start : start + head_size].astype(jnp.float32)
                    mixed = mixed + jnp.broadcast_to(weight * inverse, part.shape) * part
                attn[
                    first : first + rows, member * head_size : (member + 1) * head_size
                ] = mixed.astype(jnp.bfloat16)
    columns = w_refs[0].shape[1]
    per_half = keep_ref.shape[1] // columns
    for part in range(parts):
        made = jnp.dot(attn[...], w_refs[part][...], preferred_element_type=jnp.float32)
        chunk = info_ref[2 + part]
        inside = pl.multiple_of((chunk % per_half) * columns, columns)

        @pl.when(chunk // per_half == half)
        def _():
            keep_ref[:, pl.ds(inside, columns)] = made

        @pl.when(chunk // per_half != half)
        def _():
            send_ref[:, pl.ds(inside, columns)] = made.astype(jnp.bfloat16)


def merge_project(batches, weights, info, share, requests):
    rows = batches[0][0].shape[0]
    columns = weights[0].shape[1]
    parts = len(weights)
    half_width = parts * columns // 2
    shape = (requests * rows, half_width)
    return pl.pallas_call(
        functools.partial(merge_kernel, parts, len(batches), share),
        in_specs=[pl.BlockSpec(memory_space=pltpu.SMEM)]
        + [pl.BlockSpec(memory_space=pltpu.VMEM)] * ((len(batches) + 1) * parts),
        out_specs=[pl.BlockSpec(memory_space=pltpu.VMEM)] * 2,
        out_shape=[
            jax.ShapeDtypeStruct(shape, jnp.float32),
            jax.ShapeDtypeStruct(shape, jnp.bfloat16),
        ],
        scratch_shapes=[pltpu.VMEM((requests * rows, share * head_size_of(weights, share)), jnp.bfloat16)],
        name="merge_project",
    )(info, *[message for batch in batches for message in batch], *weights)


def head_size_of(weights, share):
    return weights[0].shape[0] // share


def shift(value, axis, step):
    size = lax.axis_size(axis)
    return lax.ppermute(value, axis, [(i, (i + step) % size) for i in range(size)])


def take_block(value, index):
    return lax.dynamic_index_in_dim(value, index, 0, keepdims=False)


def gather_blocks(block, axis):
    return [block] + [shift(block, axis, s) for s in range(1, lax.axis_size(axis))]


def swap(value, axis, bits):
    size = lax.axis_size(axis)
    return lax.ppermute(value, axis, [(i, i ^ bits) for i in range(size)])


def route_table(route_ids, route_weights):
    groups = lax.axis_size("req") * lax.axis_size("exp")
    return jnp.sum(
        jnp.where(
            route_ids[None, :, :] == lax.iota(jnp.int32, groups)[:, None, None],
            route_weights[None, :, :],
            0.0,
        ),
        axis=2,
    )


def exchange_table(table):
    req_size, exp_size = lax.axis_size("req"), lax.axis_size("exp")
    mine = lax.all_to_all(table, ("req", "exp"), split_axis=0, concat_axis=0, tiled=True)
    by_req = (lax.axis_index("req") - lax.iota(jnp.int32, req_size)) % req_size
    by_exp = lax.axis_index("exp") ^ lax.iota(jnp.int32, exp_size)
    order = by_req[None, :] * exp_size + by_exp[:, None]
    return jnp.take(mine, order.reshape(-1), axis=0).reshape(exp_size, -1)


def halves(value, width, axis):
    head_at = lax.axis_index("head")
    own = lax.dynamic_slice_in_dim(value, head_at * width, width, axis)
    other = lax.dynamic_slice_in_dim(value, (1 - head_at) * width, width, axis)
    return own, other


def expert_block(own, weights, gains, maps_in, maps_out):
    other = swap(own, "head", 1)
    wide = [own.astype(jnp.float32), other.astype(jnp.float32)]
    squares = sum(jnp.sum(x * x, axis=-1, keepdims=True) for x in wide)
    factor = lax.rsqrt(squares / (2 * own.shape[1]) + norm_epsilon)
    gate_up = sum(
        jnp.dot((x * factor * gain).astype(jnp.bfloat16), maps, preferred_element_type=jnp.float32)
        for x, gain, maps in zip(wide, gains, maps_in)
    )
    half_units = gate_up.shape[-1] // 2
    activated = (jax.nn.silu(gate_up[:, :half_units]) * gate_up[:, half_units:]).astype(
        jnp.bfloat16
    )
    kept, passed = [
        jnp.dot(activated, maps, preferred_element_type=jnp.float32) * weights[:, None]
        for maps in maps_out
    ]
    return kept + swap(passed.astype(jnp.bfloat16), "head", 1).astype(jnp.float32)


def dense_experts(half_hidden, table, gains, maps_in, maps_out):
    row_count, half_width = half_hidden.shape
    req_size = lax.axis_size("req")
    sent = half_hidden.astype(jnp.bfloat16)
    sent, table = lax.optimization_barrier((sent, table))
    column = jnp.concatenate(gather_blocks(sent, "req"), axis=0)
    row_weights = exchange_table(table)
    middle = column.shape[0] // 2

    def run(block, weights):
        return expert_block(block, weights, gains, maps_in, maps_out)

    def over(value, bits):
        return swap(value.astype(jnp.bfloat16), "exp", bits).astype(jnp.float32)

    near_x = swap(column, "exp", 1)
    near_y = swap(column, "exp", 2)
    far_top = swap(near_x[:middle], "exp", 2)
    far_low = swap(near_y[middle:], "exp", 1)
    own = run(column, row_weights[0])
    for_x = run(near_x, row_weights[1])
    for_y = run(near_y, row_weights[2])
    top = own[:middle] + over(for_x[:middle], 1)
    low = own[middle:] + over(for_y[middle:], 2)
    far = run(jnp.concatenate([far_top, far_low], axis=0), row_weights[3])
    top = top + over(for_y[:middle] + over(far[:middle], 1), 2)
    low = low + over(for_x[middle:] + over(far[middle:], 2), 1)
    plane_sum = jnp.concatenate([top, low], axis=0).reshape(req_size, row_count, half_width)
    mixture = plane_sum[0]
    outgoing = plane_sum.astype(jnp.bfloat16)
    for s in range(1, req_size):
        mixture = mixture + shift(outgoing[s], "req", -s).astype(jnp.float32)
    return mixture


def sparse_experts(half_hidden, route_ids, route_weights, norm_gain, expert_in, expert_out, capacity):
    row_count, half_width = half_hidden.shape
    head_at = lax.axis_index("head")
    other = shift(half_hidden, "head", 1)
    first = jnp.where(head_at == 0, half_hidden, other)
    second = jnp.where(head_at == 0, other, half_hidden)
    hidden = jnp.concatenate([first, second], axis=1)
    normed = (
        hidden
        * lax.rsqrt(jnp.mean(hidden * hidden, axis=-1, keepdims=True) + norm_epsilon)
        * norm_gain
    ).astype(jnp.bfloat16)
    model_width = 2 * half_width
    local_experts = expert_in.shape[0]
    groups = lax.axis_size("req") * lax.axis_size("exp")
    experts_all = local_experts * groups
    expert_iota = lax.iota(jnp.int32, experts_all)
    named_count = jnp.sum((route_ids[:, :, None] == expert_iota).astype(jnp.int32), axis=1)
    earlier = jnp.cumsum(named_count, axis=0) - named_count
    slot_rank = jnp.take_along_axis(earlier, route_ids, axis=1)
    slot_index = route_ids * capacity + slot_rank
    slot_iota = lax.iota(jnp.int32, experts_all * capacity)
    placing = jnp.any(slot_index[None, :, :] == slot_iota[:, None, None], axis=2).astype(
        jnp.bfloat16
    )
    outgoing = jnp.dot(placing, normed, preferred_element_type=jnp.float32).astype(jnp.bfloat16)
    outgoing = outgoing.reshape(groups, local_experts, capacity, model_width)
    input_maps = expert_in.reshape(local_experts, model_width, -1)
    gate_up = jnp.einsum(
        "geci,eif->gecf",
        lax.all_to_all(outgoing, ("req", "exp"), split_axis=0, concat_axis=0, tiled=True),
        input_maps,
        preferred_element_type=jnp.float32,
    )
    half_units = gate_up.shape[-1] // 2
    activated = (jax.nn.silu(gate_up[..., :half_units]) * gate_up[..., half_units:]).astype(
        jnp.bfloat16
    )
    partial_value = jnp.einsum(
        "gecf,efi->geci", activated, expert_out, preferred_element_type=jnp.float32
    )
    summed = lax.psum_scatter(partial_value, "head", scatter_dimension=3, tiled=True).astype(
        jnp.bfloat16
    )
    returned = lax.all_to_all(summed, ("req", "exp"), split_axis=0, concat_axis=0, tiled=True)
    flat_results = returned.reshape(experts_all * capacity, half_width)
    picked = jnp.take(flat_results, slot_index, axis=0).astype(jnp.float32)
    return jnp.sum(picked * route_weights[:, :, None], axis=1)


def local(
    queries,
    new_keys,
    new_values,
    key_cache,
    value_cache,
    lengths,
    residual,
    out_weight,
    norm_gain,
    route_ids,
    route_weights,
    expert_in,
    expert_out,
):
    requests, span, kv, head_size = key_cache.shape
    heads = queries.shape[2]
    exp_size = lax.axis_size("exp")
    exp_at, head_at = lax.axis_index("exp"), lax.axis_index("head")
    share = heads // exp_size
    group = heads // kv
    sources = (exp_at - lax.iota(jnp.int32, exp_size)) % exp_size
    targets = [(exp_at + s) % exp_size for s in range(exp_size)]

    row_count, model_width = residual.shape
    half_width = model_width // 2
    groups = lax.axis_size("req") * exp_size
    experts_all = expert_in.shape[0] * groups
    capacity = max(2, 2 * row_count * route_ids.shape[1] // experts_all)
    dense = capacity >= row_count and experts_all == groups and exp_size == 4

    batch = requests // 2 if requests % 2 == 0 else requests
    starts = range(0, requests, batch)
    pieces = [
        gather_blocks(lax.slice_in_dim(queries, start, start + batch), "exp") for start in starts
    ]
    local_lengths = jnp.clip(lengths - exp_at * span, 0, span)
    split_weight = out_weight.reshape(exp_size, share * head_size, -1)
    weight_parts = [take_block(split_weight, targets[0])] + [
        shift(take_block(split_weight, targets[s]), "exp", s) for s in range(1, exp_size)
    ]
    received = []
    for start, gathered in zip(starts, pieces):
        messages = attend(
            gathered, sources, new_keys, new_values, key_cache, value_cache, local_lengths,
            start, 512, 256,
        )
        received.append(
            [messages[0]] + [shift(messages[s], "exp", s) for s in range(1, exp_size)]
        )
    if dense:
        table = route_table(route_ids, route_weights)
        maps_in = halves(expert_in[0].reshape(model_width, -1), half_width, 0)
        maps_out = halves(expert_out[0], half_width, 1)
        gains = halves(norm_gain, half_width, 0)
        own_message, maps_in, maps_out = lax.optimization_barrier(
            (received[-1][0], maps_in, maps_out)
        )
        received[-1] = [own_message] + received[-1][1:]
    group_shift = (head_size - (exp_at * share) % group) % head_size
    info = jnp.concatenate([jnp.stack([group_shift, head_at]).astype(jnp.int32), sources])
    kept, sent = merge_project(received, weight_parts, info, share, requests)
    both = kept + shift(sent, "head", 1).astype(jnp.float32)
    both = both.reshape(exp_size, row_count, half_width)
    outgoing = both.astype(jnp.bfloat16)
    hidden = lax.dynamic_slice_in_dim(residual, head_at * half_width, half_width, 1).astype(
        jnp.float32
    ) + take_block(both, targets[0])
    for s in range(1, exp_size):
        hidden = hidden + shift(take_block(outgoing, targets[s]), "exp", s).astype(jnp.float32)

    if dense:
        mixture = dense_experts(hidden, table, gains, maps_in, maps_out)
    else:
        mixture = sparse_experts(
            hidden, route_ids, route_weights, norm_gain, expert_in, expert_out, capacity
        )
    return (hidden + mixture).astype(jnp.bfloat16)


def solution(mesh):
    return jax.shard_map(
        local,
        mesh=mesh,
        in_specs=(
            P("req", "exp", "head", None),
            P("req", "exp", "head", None),
            P("req", "exp", "head", None),
            P("req", "exp", "head", None),
            P("req", "exp", "head", None),
            P("req"),
            P(("req", "exp"), None),
            P("head", "exp"),
            P(),
            P(("req", "exp"), None),
            P(("req", "exp"), None),
            P(("req", "exp"), None, None, "head"),
            P(("req", "exp"), "head", None),
        ),
        out_specs=P(("req", "exp"), "head"),
        check_vma=False,
    )
```

```python
import functools
import math
import jax
import jax.numpy as jnp
from jax import lax
from jax.experimental import pallas as pl
from jax.experimental.pallas import tpu as pltpu
from jax.sharding import PartitionSpec as P

masked_score = -1e30
norm_epsilon = 1e-06


def attend_kernel(pieces, base, listed, sub, tail, factor, exp_count, info_ref, *refs):
    q_refs = refs[:pieces]
    nk_ref, nv_ref, k_ref, v_ref = refs[pieces : pieces + 4]
    out_refs = refs[pieces + 4 : pieces + 4 + exp_count]
    scratch = refs[pieces + 4 + exp_count :]
    q_all, q_cat, pattern, m_scr, l_scr, acc, p_even, p_odd, stats, turned, staged = scratch
    requests = pl.num_programs(0)
    request = pl.program_id(0)
    head_size = k_ref.shape[2]
    kv = 2
    piece_rows, heads = q_refs[0].shape[1], q_refs[0].shape[2]
    group = heads // kv
    rows = piece_rows * pieces
    lanes = rows * group
    length = info_ref[request + base]
    even_lane = lax.broadcasted_iota(jnp.int32, (lanes, 128), 1) % 2 == 0

    @pl.when(request == 0)
    def _():
        stats[...] = jnp.zeros_like(stats)
        parity = lax.broadcasted_iota(jnp.int32, (16, head_size), 0) % 2
        pattern[0] = (1 - parity).astype(jnp.float32).astype(jnp.bfloat16)
        pattern[1] = parity.astype(jnp.float32).astype(jnp.bfloat16)

    for piece in range(pieces):
        where_to = info_ref[listed + piece] * piece_rows
        q_all[pl.ds(where_to, piece_rows)] = q_refs[piece][0].astype(jnp.float32)
    for head in range(kv):
        chosen = q_all[:, head * group : (head + 1) * group, :].reshape(lanes, head_size)
        q_cat[:, head * head_size : (head + 1) * head_size] = chosen.astype(jnp.bfloat16)

    def spread(block):
        if block.shape[0] < 16:
            left = block * pattern[0, : block.shape[0]]
            right = block * pattern[1, : block.shape[0]]
        else:
            tiles = block.reshape(block.shape[0] // 16, 16, head_size)
            left = (tiles * pattern[0][None]).reshape(block.shape)
            right = (tiles * pattern[1][None]).reshape(block.shape)
        return jnp.concatenate([left, right], axis=1)

    def score(block):
        return lax.dot_general(
            q_cat[...],
            spread(block),
            (((1,), (1,)), ((), ())),
            preferred_element_type=jnp.float32,
        )

    def both_columns(even, odd):
        shape = (lanes, 128)
        return jnp.where(even_lane, jnp.broadcast_to(even, shape), jnp.broadcast_to(odd, shape))

    def reduce_parity(wide, op, neutral):
        even = op(jnp.where(even_lane, wide, neutral), axis=1, keepdims=True)
        odd = op(jnp.where(even_lane, neutral, wide), axis=1, keepdims=True)
        return even, odd

    def init():
        scores = score(nk_ref[0]) * factor
        fresh = scores.shape[1]
        even = lax.broadcasted_iota(jnp.int32, scores.shape, 1) % 2 == 0
        top_even = jnp.max(jnp.where(even, scores, -jnp.inf), axis=1, keepdims=True)
        top_odd = jnp.max(jnp.where(even, -jnp.inf, scores), axis=1, keepdims=True)
        top_even = top_even.astype(jnp.bfloat16).astype(jnp.float32)
        top_odd = top_odd.astype(jnp.bfloat16).astype(jnp.float32)
        m_scr[...] = both_columns(top_even, top_odd)
        probs = jnp.exp2(
            scores
            - jnp.where(
                even,
                jnp.broadcast_to(top_even, scores.shape),
                jnp.broadcast_to(top_odd, scores.shape),
            )
        )
        l_even = jnp.sum(jnp.where(even, probs, 0.0), axis=1, keepdims=True)
        l_odd = jnp.sum(jnp.where(even, 0.0, probs), axis=1, keepdims=True)
        lane = lax.broadcasted_iota(jnp.int32, (lanes, 128), 1)
        l_scr[...] = jnp.where(lane < 2, both_columns(l_even, l_odd), 0.0)
        acc[...] = jnp.dot(
            probs.astype(jnp.bfloat16), spread(nv_ref[0]), preferred_element_type=jnp.float32
        )

    def piece_of(ref, start, size):
        return ref[0, pl.ds(pl.multiple_of(start * kv, kv * tail), size * kv), :]

    step = 256

    def soften(start, size, target, masked):
        top = m_scr[...]
        total = l_scr[...]
        for tile in range(size * kv // step):
            scores = score(piece_of_tile(k_ref, start, tile))
            for part in range(step // 128):
                piece = scores[:, part * 128 : (part + 1) * 128]
                probs = jnp.exp2(piece * factor - top)
                if masked:
                    lane = lax.broadcasted_iota(jnp.int32, (1, 128), 1)
                    position = start + (tile * step + part * 128 + lane) // kv
                    probs = jnp.where(position < length, probs, 0.0)
                total = total + probs
                at = tile * step + part * 128
                target[:, at : at + 128] = probs.astype(jnp.bfloat16)
        l_scr[...] = total

    def piece_of_tile(ref, start, tile):
        first = pl.multiple_of(start * kv, kv * tail) + tile * step
        return ref[0, pl.ds(first, step), :]

    def weigh(start, size, source):
        values = spread(piece_of(v_ref, start, size))
        acc[...] += jnp.dot(source[:, : size * kv], values, preferred_element_type=jnp.float32)

    init()
    here = length
    pairs = here // (2 * sub)

    def loop(i, carry):
        start = pl.multiple_of(i * 2 * sub, 2 * sub)
        before = jnp.maximum(start - sub, 0)
        soften(start, sub, p_even, False)
        weigh(before, sub, p_odd)
        soften(start + sub, sub, p_odd, False)
        weigh(start, sub, p_even)
        return carry

    p_odd[...] = jnp.zeros_like(p_odd)
    lax.fori_loop(0, pairs, loop, 0)
    weigh(pl.multiple_of(jnp.maximum(pairs * 2 * sub - sub, 0), sub), sub, p_odd)

    def tail_loop(i, carry):
        start = pl.multiple_of(pairs * 2 * sub + i * tail, tail)
        soften(start, tail, p_even, True)
        weigh(start, tail, p_even)
        return carry

    lax.fori_loop(0, (here - pairs * 2 * sub + tail - 1) // tail, tail_loop, 0)
    largest = jnp.max(l_scr[...])

    @pl.when(jnp.logical_not(largest < 1e30))
    def _():
        init()

        def slow_loop(i, carry):
            start = pl.multiple_of(i * tail, tail)
            scores = score(piece_of(k_ref, start, tail)) * factor
            lane = lax.broadcasted_iota(jnp.int32, (1, tail * kv), 1)
            inside = start + lane // kv < length
            scores = jnp.where(inside, scores, masked_score)
            wide = m_scr[...]
            for part in range(tail * kv // 128):
                wide = jnp.maximum(wide, scores[:, part * 128 : (part + 1) * 128])
            even, odd = reduce_parity(wide, jnp.max, -jnp.inf)
            even = even.astype(jnp.bfloat16).astype(jnp.float32)
            odd = odd.astype(jnp.bfloat16).astype(jnp.float32)
            top = both_columns(even, odd)
            fade = jnp.exp2(m_scr[...] - top)
            total = l_scr[...] * fade
            for part in range(tail * kv // 128):
                at = part * 128
                probs = jnp.where(
                    inside[:, at : at + 128], jnp.exp2(scores[:, at : at + 128] - top), 0.0
                )
                total = total + probs
                p_even[:, at : at + 128] = probs.astype(jnp.bfloat16)
            l_scr[...] = total
            m_scr[...] = top
            for head in range(kv):
                columns = slice(head * head_size, (head + 1) * head_size)
                acc[:, columns] = acc[:, columns] * jnp.broadcast_to(
                    fade[:, head : head + 1], (lanes, head_size)
                )
            weigh(start, tail, p_even)
            return carry

        lax.fori_loop(0, (here + tail - 1) // tail, slow_loop, 0)

    share = heads // exp_count
    totals = reduce_parity(l_scr[...], jnp.sum, 0.0)
    lane = lax.broadcasted_iota(jnp.int32, (lanes, head_size), 1)
    member_of_row = lax.broadcasted_iota(jnp.int32, (lanes, head_size), 0) % group
    for head in range(kv):
        total = totals[head]
        inverse = jnp.broadcast_to(1.0 / total, (lanes, head_size))
        columns = slice(head * head_size, (head + 1) * head_size)
        turned[...] = acc[:, columns] * inverse
        upper = total.astype(jnp.bfloat16).astype(jnp.float32)
        kinds = [upper, m_scr[:, head : head + 1], total - upper]
        placed = jnp.zeros((lanes, head_size), jnp.float32)
        for kind, column in enumerate(kinds):
            placed = jnp.where(
                lane == member_of_row + 8 * kind,
                jnp.broadcast_to(column, placed.shape),
                placed,
            )
        gathered = jnp.sum(placed.reshape(rows, group, head_size), axis=1)
        stats[head] = stats[head] + pltpu.roll(gathered, 24 * request, 1)
        for member in range(group):
            index = head * group + member
            target, inside = index // share, index % share
            offset = pl.multiple_of(
                request * (share * head_size) + inside * head_size, head_size
            )
            staged[target, :, pl.ds(offset, head_size)] = turned[
                pl.ds(member, rows, stride=group), :
            ].astype(jnp.bfloat16)

    @pl.when(request == requests - 1)
    def _():
        for target in range(exp_count):
            head = target * share // group
            staged[target, :, requests * share * head_size :] = stats[head].astype(jnp.bfloat16)
        for step_away in range(exp_count):
            out_refs[step_away][...] = staged[info_ref[listed + (-step_away) % exp_count]]


def attend(queries, order, new_keys, new_values, keys, values, local_lengths, base, sub, tail):
    listed, span, kv, head_size = keys.shape
    requests, piece_rows, heads = queries[0].shape[:3]
    pieces = exp_count = len(queries)
    rows = piece_rows * pieces
    share = heads // exp_count
    fresh = new_keys.shape[1]
    width = requests * share * head_size + 128
    info = jnp.concatenate([local_lengths, order])
    factor = head_size ** (-0.5) * math.log2(math.e)
    lanes = rows * heads // kv
    flat = lambda x: x.reshape(listed, x.shape[1] * kv, head_size)
    block = lambda n: pl.BlockSpec((1, n, head_size), lambda r, info: (r + base, 0, 0))
    return pl.pallas_call(
        functools.partial(attend_kernel, pieces, base, listed, sub, tail, factor, exp_count),
        grid_spec=pltpu.PrefetchScalarGridSpec(
            num_scalar_prefetch=1,
            grid=(requests,),
            in_specs=[
                pl.BlockSpec((1, piece_rows, heads, head_size), lambda r, info: (r, 0, 0, 0))
            ]
            * pieces
            + [block(fresh * kv), block(fresh * kv), block(span * kv), block(span * kv)],
            out_specs=[pl.BlockSpec((rows, width), lambda r, info: (0, 0))] * exp_count,
            scratch_shapes=[
                pltpu.VMEM((rows, heads, head_size), jnp.float32),
                pltpu.VMEM((lanes, kv * head_size), jnp.bfloat16),
                pltpu.VMEM((2, 16, head_size), jnp.bfloat16),
                pltpu.VMEM((lanes, 128), jnp.float32),
                pltpu.VMEM((lanes, 128), jnp.float32),
                pltpu.VMEM((lanes, kv * head_size), jnp.float32),
                pltpu.VMEM((lanes, sub * kv), jnp.bfloat16),
                pltpu.VMEM((lanes, sub * kv), jnp.bfloat16),
                pltpu.VMEM((kv, rows, head_size), jnp.float32),
                pltpu.VMEM((lanes, head_size), jnp.float32),
                pltpu.VMEM((exp_count, rows, width), jnp.bfloat16),
            ],
        ),
        out_shape=[jax.ShapeDtypeStruct((rows, width), jnp.bfloat16)] * exp_count,
        compiler_params=pltpu.CompilerParams(dimension_semantics=("arbitrary",)),
        name="attend",
    )(info, *queries, flat(new_keys), flat(new_values), flat(keys), flat(values))


def merge_kernel(parts, batches, share, info_ref, *refs):
    w_refs = refs[batches * parts : (batches + 1) * parts]
    keep_ref, send_ref, attn = refs[(batches + 1) * parts :]
    rows, width = refs[0].shape
    head_size = 128
    requests = (width - head_size) // (share * head_size)
    group_shift = info_ref[0]
    half = info_ref[1]
    for batch in range(batches):
        x_refs = refs[batch * parts : (batch + 1) * parts]
        tables = []
        for x_ref in x_refs:
            table = x_ref[:, width - head_size :].astype(jnp.float32)
            tables.append(pltpu.roll(table, group_shift, 1))
        for request in range(requests):
            first = (batch * requests + request) * rows
            for member in range(share):
                at = 24 * request + member
                tops = [t[:, at + 8 : at + 9] for t in tables]
                sums = [t[:, at : at + 1] + t[:, at + 16 : at + 17] for t in tables]
                top = functools.reduce(jnp.maximum, tops)
                weights = [s * jnp.exp2(m - top) for s, m in zip(sums, tops)]
                inverse = 1.0 / functools.reduce(jnp.add, weights)
                start = (request * share + member) * head_size
                mixed = jnp.zeros((rows, head_size), jnp.float32)
                for weight, x_ref in zip(weights, x_refs):
                    part = x_ref[:, start : start + head_size].astype(jnp.float32)
                    mixed = mixed + jnp.broadcast_to(weight * inverse, part.shape) * part
                attn[
                    first : first + rows, member * head_size : (member + 1) * head_size
                ] = mixed.astype(jnp.bfloat16)
    columns = w_refs[0].shape[1]
    per_half = keep_ref.shape[1] // columns
    for part in range(parts):
        made = jnp.dot(attn[...], w_refs[part][...], preferred_element_type=jnp.float32)
        chunk = info_ref[2 + part]
        inside = pl.multiple_of((chunk % per_half) * columns, columns)

        @pl.when(chunk // per_half == half)
        def _():
            keep_ref[:, pl.ds(inside, columns)] = made

        @pl.when(chunk // per_half != half)
        def _():
            send_ref[:, pl.ds(inside, columns)] = made.astype(jnp.bfloat16)


def merge_project(batches, weights, info, share, requests):
    rows = batches[0][0].shape[0]
    columns = weights[0].shape[1]
    parts = len(weights)
    half_width = parts * columns // 2
    shape = (requests * rows, half_width)
    return pl.pallas_call(
        functools.partial(merge_kernel, parts, len(batches), share),
        in_specs=[pl.BlockSpec(memory_space=pltpu.SMEM)]
        + [pl.BlockSpec(memory_space=pltpu.VMEM)] * ((len(batches) + 1) * parts),
        out_specs=[pl.BlockSpec(memory_space=pltpu.VMEM)] * 2,
        out_shape=[
            jax.ShapeDtypeStruct(shape, jnp.float32),
            jax.ShapeDtypeStruct(shape, jnp.bfloat16),
        ],
        scratch_shapes=[pltpu.VMEM((requests * rows, share * head_size_of(weights, share)), jnp.bfloat16)],
        name="merge_project",
    )(info, *[message for batch in batches for message in batch], *weights)


def head_size_of(weights, share):
    return weights[0].shape[0] // share


def shift(value, axis, step):
    size = lax.axis_size(axis)
    return lax.ppermute(value, axis, [(i, (i + step) % size) for i in range(size)])


def take_block(value, index):
    return lax.dynamic_index_in_dim(value, index, 0, keepdims=False)


def gather_blocks(block, axis):
    return [block] + [shift(block, axis, s) for s in range(1, lax.axis_size(axis))]


def swap(value, axis, bits):
    size = lax.axis_size(axis)
    return lax.ppermute(value, axis, [(i, i ^ bits) for i in range(size)])


def route_table(route_ids, route_weights):
    groups = lax.axis_size("req") * lax.axis_size("exp")
    return jnp.sum(
        jnp.where(
            route_ids[None, :, :] == lax.iota(jnp.int32, groups)[:, None, None],
            route_weights[None, :, :],
            0.0,
        ),
        axis=2,
    )


def exchange_table(table):
    req_size, exp_size = lax.axis_size("req"), lax.axis_size("exp")
    mine = lax.all_to_all(table, ("req", "exp"), split_axis=0, concat_axis=0, tiled=True)
    by_req = (lax.axis_index("req") - lax.iota(jnp.int32, req_size)) % req_size
    by_exp = lax.axis_index("exp") ^ lax.iota(jnp.int32, exp_size)
    order = by_req[None, :] * exp_size + by_exp[:, None]
    return jnp.take(mine, order.reshape(-1), axis=0).reshape(-1, 1)


def halves(value, width, axis):
    head_at = lax.axis_index("head")
    own = lax.dynamic_slice_in_dim(value, head_at * width, width, axis)
    other = lax.dynamic_slice_in_dim(value, (1 - head_at) * width, width, axis)
    return own, other


def expert_kernel(first, own_ref, other_ref, weight_ref, gain_0, gain_1, in_0, in_1, out_0, out_1, kept_ref, sent_ref):
    rows, half_width = own_ref.shape
    wide = [own_ref[...].astype(jnp.float32), other_ref[...].astype(jnp.float32)]
    squares = sum(jnp.sum(x * x, axis=-1, keepdims=True) for x in wide)
    factor = lax.rsqrt(squares / (2 * half_width) + norm_epsilon)
    gate_up = sum(
        jnp.dot(
            (x * factor * gain[...]).astype(jnp.bfloat16),
            maps[...],
            preferred_element_type=jnp.float32,
        )
        for x, gain, maps in zip(wide, (gain_0, gain_1), (in_0, in_1))
    )
    half_units = gate_up.shape[-1] // 2
    gate = gate_up[:, :half_units]
    activated = (gate / (1.0 + jnp.exp(-gate)) * gate_up[:, half_units:]).astype(jnp.bfloat16)
    weight = weight_ref[first : first + rows, :]
    for maps, target in ((out_0, kept_ref), (out_1, sent_ref)):
        made = jnp.dot(activated, maps[...], preferred_element_type=jnp.float32)
        target[...] = (made * weight).astype(jnp.bfloat16)


def expert_block(own, index, weights, gains, maps_in, maps_out):
    other = swap(own, "head", 1)
    rows = own.shape[0]
    kept, passed = pl.pallas_call(
        functools.partial(expert_kernel, index * rows),
        in_specs=[pl.BlockSpec(memory_space=pltpu.VMEM)] * 9,
        out_specs=[pl.BlockSpec(memory_space=pltpu.VMEM)] * 2,
        out_shape=[jax.ShapeDtypeStruct(own.shape, jnp.bfloat16)] * 2,
        name="expert_block",
    )(own, other, weights, *[g[None, :] for g in gains], *maps_in, *maps_out)
    return kept.astype(jnp.float32) + swap(passed, "head", 1).astype(jnp.float32)


def dense_experts(half_hidden, row_weights, gains, maps_in, maps_out):
    row_count, half_width = half_hidden.shape
    req_size = lax.axis_size("req")
    sent = half_hidden.astype(jnp.bfloat16)
    column = jnp.concatenate(gather_blocks(sent, "req"), axis=0)
    middle = column.shape[0] // 2

    def run(block, index):
        return expert_block(block, index, row_weights, gains, maps_in, maps_out)

    def over(value, bits):
        return swap(value.astype(jnp.bfloat16), "exp", bits).astype(jnp.float32)

    near_x = swap(column, "exp", 1)
    near_y = swap(column, "exp", 2)
    far_top = swap(near_x[:middle], "exp", 2)
    far_low = swap(near_y[middle:], "exp", 1)
    own = run(column, 0)
    for_x = run(near_x, 1)
    for_y = run(near_y, 2)
    top = own[:middle] + over(for_x[:middle], 1)
    low = own[middle:] + over(for_y[middle:], 2)
    far = run(jnp.concatenate([far_top, far_low], axis=0), 3)
    top = top + over(for_y[:middle] + over(far[:middle], 1), 2)
    low = low + over(for_x[middle:] + over(far[middle:], 2), 1)
    plane_sum = jnp.concatenate([top, low], axis=0).reshape(req_size, row_count, half_width)
    mixture = plane_sum[0]
    outgoing = plane_sum.astype(jnp.bfloat16)
    for s in range(1, req_size):
        mixture = mixture + shift(outgoing[s], "req", -s).astype(jnp.float32)
    return mixture


def sparse_experts(half_hidden, route_ids, route_weights, norm_gain, expert_in, expert_out, capacity):
    row_count, half_width = half_hidden.shape
    head_at = lax.axis_index("head")
    other = shift(half_hidden, "head", 1)
    first = jnp.where(head_at == 0, half_hidden, other)
    second = jnp.where(head_at == 0, other, half_hidden)
    hidden = jnp.concatenate([first, second], axis=1)
    normed = (
        hidden
        * lax.rsqrt(jnp.mean(hidden * hidden, axis=-1, keepdims=True) + norm_epsilon)
        * norm_gain
    ).astype(jnp.bfloat16)
    model_width = 2 * half_width
    local_experts = expert_in.shape[0]
    groups = lax.axis_size("req") * lax.axis_size("exp")
    experts_all = local_experts * groups
    expert_iota = lax.iota(jnp.int32, experts_all)
    named_count = jnp.sum((route_ids[:, :, None] == expert_iota).astype(jnp.int32), axis=1)
    earlier = jnp.cumsum(named_count, axis=0) - named_count
    slot_rank = jnp.take_along_axis(earlier, route_ids, axis=1)
    slot_index = route_ids * capacity + slot_rank
    slot_iota = lax.iota(jnp.int32, experts_all * capacity)
    placing = jnp.any(slot_index[None, :, :] == slot_iota[:, None, None], axis=2).astype(
        jnp.bfloat16
    )
    outgoing = jnp.dot(placing, normed, preferred_element_type=jnp.float32).astype(jnp.bfloat16)
    outgoing = outgoing.reshape(groups, local_experts, capacity, model_width)
    input_maps = expert_in.reshape(local_experts, model_width, -1)
    gate_up = jnp.einsum(
        "geci,eif->gecf",
        lax.all_to_all(outgoing, ("req", "exp"), split_axis=0, concat_axis=0, tiled=True),
        input_maps,
        preferred_element_type=jnp.float32,
    )
    half_units = gate_up.shape[-1] // 2
    activated = (jax.nn.silu(gate_up[..., :half_units]) * gate_up[..., half_units:]).astype(
        jnp.bfloat16
    )
    partial_value = jnp.einsum(
        "gecf,efi->geci", activated, expert_out, preferred_element_type=jnp.float32
    )
    summed = lax.psum_scatter(partial_value, "head", scatter_dimension=3, tiled=True).astype(
        jnp.bfloat16
    )
    returned = lax.all_to_all(summed, ("req", "exp"), split_axis=0, concat_axis=0, tiled=True)
    flat_results = returned.reshape(experts_all * capacity, half_width)
    picked = jnp.take(flat_results, slot_index, axis=0).astype(jnp.float32)
    return jnp.sum(picked * route_weights[:, :, None], axis=1)


def local(
    queries,
    new_keys,
    new_values,
    key_cache,
    value_cache,
    lengths,
    residual,
    out_weight,
    norm_gain,
    route_ids,
    route_weights,
    expert_in,
    expert_out,
):
    requests, span, kv, head_size = key_cache.shape
    heads = queries.shape[2]
    exp_size = lax.axis_size("exp")
    exp_at, head_at = lax.axis_index("exp"), lax.axis_index("head")
    share = heads // exp_size
    group = heads // kv
    sources = (exp_at - lax.iota(jnp.int32, exp_size)) % exp_size
    targets = [(exp_at + s) % exp_size for s in range(exp_size)]

    row_count, model_width = residual.shape
    half_width = model_width // 2
    groups = lax.axis_size("req") * exp_size
    experts_all = expert_in.shape[0] * groups
    capacity = max(2, 2 * row_count * route_ids.shape[1] // experts_all)
    dense = capacity >= row_count and experts_all == groups and exp_size == 4

    batch = requests
    starts = range(0, requests, batch)
    pieces = [
        gather_blocks(lax.slice_in_dim(queries, start, start + batch), "exp") for start in starts
    ]
    local_lengths = jnp.clip(lengths - exp_at * span, 0, span)
    split_weight = out_weight.reshape(exp_size, share * head_size, -1)
    weight_parts = [take_block(split_weight, targets[0])] + [
        shift(take_block(split_weight, targets[s]), "exp", s) for s in range(1, exp_size)
    ]
    if dense:
        row_weights = exchange_table(route_table(route_ids, route_weights))
        own_piece, row_weights = lax.optimization_barrier((pieces[0][0], row_weights))
        pieces[0] = [own_piece] + pieces[0][1:]
    received = []
    for start, gathered in zip(starts, pieces):
        messages = attend(
            gathered, sources, new_keys, new_values, key_cache, value_cache, local_lengths,
            start, 512, 256,
        )
        received.append(
            [messages[0]] + [shift(messages[s], "exp", s) for s in range(1, exp_size)]
        )
    if dense:
        maps_in = halves(expert_in[0].reshape(model_width, -1), half_width, 0)
        maps_out = halves(expert_out[0], half_width, 1)
        gains = halves(norm_gain, half_width, 0)
        own_message, maps_in, maps_out = lax.optimization_barrier(
            (received[-1][0], maps_in, maps_out)
        )
        received[-1] = [own_message] + received[-1][1:]
    group_shift = (head_size - (exp_at * share) % group) % head_size
    info = jnp.concatenate([jnp.stack([group_shift, head_at]).astype(jnp.int32), sources])
    kept, sent = merge_project(received, weight_parts, info, share, requests)
    both = kept + shift(sent, "head", 1).astype(jnp.float32)
    both = both.reshape(exp_size, row_count, half_width)
    outgoing = both.astype(jnp.bfloat16)
    hidden = lax.dynamic_slice_in_dim(residual, head_at * half_width, half_width, 1).astype(
        jnp.float32
    ) + take_block(both, targets[0])
    for s in range(1, exp_size):
        hidden = hidden + shift(take_block(outgoing, targets[s]), "exp", s).astype(jnp.float32)

    if dense:
        mixture = dense_experts(hidden, row_weights, gains, maps_in, maps_out)
    else:
        mixture = sparse_experts(
            hidden, route_ids, route_weights, norm_gain, expert_in, expert_out, capacity
        )
    return (hidden + mixture).astype(jnp.bfloat16)


def solution(mesh):
    return jax.shard_map(
        local,
        mesh=mesh,
        in_specs=(
            P("req", "exp", "head", None),
            P("req", "exp", "head", None),
            P("req", "exp", "head", None),
            P("req", "exp", "head", None),
            P("req", "exp", "head", None),
            P("req"),
            P(("req", "exp"), None),
            P("head", "exp"),
            P(),
            P(("req", "exp"), None),
            P(("req", "exp"), None),
            P(("req", "exp"), None, None, "head"),
            P(("req", "exp"), "head", None),
        ),
        out_specs=P(("req", "exp"), "head"),
        check_vma=False,
    )
```

```python
import functools
import math
import jax
import jax.numpy as jnp
from jax import lax
from jax.experimental import pallas as pl
from jax.experimental.pallas import tpu as pltpu
from jax.sharding import PartitionSpec as P

masked_score = -1e30
norm_epsilon = 1e-06


def attend_kernel(pieces, base, listed, sub, tail, factor, exp_count, info_ref, *refs):
    q_refs = refs[:pieces]
    nk_ref, nv_ref, k_ref, v_ref = refs[pieces : pieces + 4]
    out_refs = refs[pieces + 4 : pieces + 4 + exp_count]
    scratch = refs[pieces + 4 + exp_count :]
    q_all, q_cat, pattern, m_scr, l_scr, acc, p_even, p_odd, stats, turned, staged = scratch
    requests = pl.num_programs(0)
    request = pl.program_id(0)
    head_size = k_ref.shape[2]
    kv = 2
    piece_rows, heads = q_refs[0].shape[1], q_refs[0].shape[2]
    group = heads // kv
    rows = piece_rows * pieces
    lanes = rows * group
    length = info_ref[request + base]
    even_lane = lax.broadcasted_iota(jnp.int32, (lanes, 128), 1) % 2 == 0

    @pl.when(request == 0)
    def _():
        stats[...] = jnp.zeros_like(stats)
        parity = lax.broadcasted_iota(jnp.int32, (16, head_size), 0) % 2
        pattern[0] = (1 - parity).astype(jnp.float32).astype(jnp.bfloat16)
        pattern[1] = parity.astype(jnp.float32).astype(jnp.bfloat16)

    for piece in range(pieces):
        where_to = info_ref[listed + piece] * piece_rows
        q_all[pl.ds(where_to, piece_rows)] = q_refs[piece][0].astype(jnp.float32)
    for head in range(kv):
        chosen = q_all[:, head * group : (head + 1) * group, :].reshape(lanes, head_size)
        q_cat[:, head * head_size : (head + 1) * head_size] = chosen.astype(jnp.bfloat16)

    def spread(block):
        if block.shape[0] < 16:
            left = block * pattern[0, : block.shape[0]]
            right = block * pattern[1, : block.shape[0]]
        else:
            tiles = block.reshape(block.shape[0] // 16, 16, head_size)
            left = (tiles * pattern[0][None]).reshape(block.shape)
            right = (tiles * pattern[1][None]).reshape(block.shape)
        return jnp.concatenate([left, right], axis=1)

    def score(block):
        return lax.dot_general(
            q_cat[...],
            spread(block),
            (((1,), (1,)), ((), ())),
            preferred_element_type=jnp.float32,
        )

    def both_columns(even, odd):
        shape = (lanes, 128)
        return jnp.where(even_lane, jnp.broadcast_to(even, shape), jnp.broadcast_to(odd, shape))

    def reduce_parity(wide, op, neutral):
        even = op(jnp.where(even_lane, wide, neutral), axis=1, keepdims=True)
        odd = op(jnp.where(even_lane, neutral, wide), axis=1, keepdims=True)
        return even, odd

    def init():
        scores = score(nk_ref[0]) * factor
        fresh = scores.shape[1]
        even = lax.broadcasted_iota(jnp.int32, scores.shape, 1) % 2 == 0
        top_even = jnp.max(jnp.where(even, scores, -jnp.inf), axis=1, keepdims=True)
        top_odd = jnp.max(jnp.where(even, -jnp.inf, scores), axis=1, keepdims=True)
        top_even = top_even.astype(jnp.bfloat16).astype(jnp.float32)
        top_odd = top_odd.astype(jnp.bfloat16).astype(jnp.float32)
        m_scr[...] = both_columns(top_even, top_odd)
        probs = jnp.exp2(
            scores
            - jnp.where(
                even,
                jnp.broadcast_to(top_even, scores.shape),
                jnp.broadcast_to(top_odd, scores.shape),
            )
        )
        l_even = jnp.sum(jnp.where(even, probs, 0.0), axis=1, keepdims=True)
        l_odd = jnp.sum(jnp.where(even, 0.0, probs), axis=1, keepdims=True)
        lane = lax.broadcasted_iota(jnp.int32, (lanes, 128), 1)
        l_scr[...] = jnp.where(lane < 2, both_columns(l_even, l_odd), 0.0)
        acc[...] = jnp.dot(
            probs.astype(jnp.bfloat16), spread(nv_ref[0]), preferred_element_type=jnp.float32
        )

    def piece_of(ref, start, size):
        return ref[0, pl.ds(pl.multiple_of(start * kv, kv * tail), size * kv), :]

    step = 256

    def soften(start, size, target, masked):
        top = m_scr[...]
        total = l_scr[...]
        for tile in range(size * kv // step):
            scores = score(piece_of_tile(k_ref, start, tile))
            for part in range(step // 128):
                piece = scores[:, part * 128 : (part + 1) * 128]
                probs = jnp.exp2(piece * factor - top)
                if masked:
                    lane = lax.broadcasted_iota(jnp.int32, (1, 128), 1)
                    position = start + (tile * step + part * 128 + lane) // kv
                    probs = jnp.where(position < length, probs, 0.0)
                total = total + probs
                at = tile * step + part * 128
                target[:, at : at + 128] = probs.astype(jnp.bfloat16)
        l_scr[...] = total

    def piece_of_tile(ref, start, tile):
        first = pl.multiple_of(start * kv, kv * tail) + tile * step
        return ref[0, pl.ds(first, step), :]

    def weigh(start, size, source):
        values = spread(piece_of(v_ref, start, size))
        acc[...] += jnp.dot(source[:, : size * kv], values, preferred_element_type=jnp.float32)

    init()
    here = length
    pairs = here // (2 * sub)

    def loop(i, carry):
        start = pl.multiple_of(i * 2 * sub, 2 * sub)
        before = jnp.maximum(start - sub, 0)
        soften(start, sub, p_even, False)
        weigh(before, sub, p_odd)
        soften(start + sub, sub, p_odd, False)
        weigh(start, sub, p_even)
        return carry

    p_odd[...] = jnp.zeros_like(p_odd)
    lax.fori_loop(0, pairs, loop, 0)
    weigh(pl.multiple_of(jnp.maximum(pairs * 2 * sub - sub, 0), sub), sub, p_odd)

    def tail_loop(i, carry):
        start = pl.multiple_of(pairs * 2 * sub + i * tail, tail)
        soften(start, tail, p_even, True)
        weigh(start, tail, p_even)
        return carry

    lax.fori_loop(0, (here - pairs * 2 * sub + tail - 1) // tail, tail_loop, 0)
    largest = jnp.max(l_scr[...])

    @pl.when(jnp.logical_not(largest < 1e30))
    def _():
        init()

        def slow_loop(i, carry):
            start = pl.multiple_of(i * tail, tail)
            scores = score(piece_of(k_ref, start, tail)) * factor
            lane = lax.broadcasted_iota(jnp.int32, (1, tail * kv), 1)
            inside = start + lane // kv < length
            scores = jnp.where(inside, scores, masked_score)
            wide = m_scr[...]
            for part in range(tail * kv // 128):
                wide = jnp.maximum(wide, scores[:, part * 128 : (part + 1) * 128])
            even, odd = reduce_parity(wide, jnp.max, -jnp.inf)
            even = even.astype(jnp.bfloat16).astype(jnp.float32)
            odd = odd.astype(jnp.bfloat16).astype(jnp.float32)
            top = both_columns(even, odd)
            fade = jnp.exp2(m_scr[...] - top)
            total = l_scr[...] * fade
            for part in range(tail * kv // 128):
                at = part * 128
                probs = jnp.where(
                    inside[:, at : at + 128], jnp.exp2(scores[:, at : at + 128] - top), 0.0
                )
                total = total + probs
                p_even[:, at : at + 128] = probs.astype(jnp.bfloat16)
            l_scr[...] = total
            m_scr[...] = top
            for head in range(kv):
                columns = slice(head * head_size, (head + 1) * head_size)
                acc[:, columns] = acc[:, columns] * jnp.broadcast_to(
                    fade[:, head : head + 1], (lanes, head_size)
                )
            weigh(start, tail, p_even)
            return carry

        lax.fori_loop(0, (here + tail - 1) // tail, slow_loop, 0)

    share = heads // exp_count
    totals = reduce_parity(l_scr[...], jnp.sum, 0.0)
    lane = lax.broadcasted_iota(jnp.int32, (lanes, head_size), 1)
    member_of_row = lax.broadcasted_iota(jnp.int32, (lanes, head_size), 0) % group
    for head in range(kv):
        total = totals[head]
        inverse = jnp.broadcast_to(1.0 / total, (lanes, head_size))
        columns = slice(head * head_size, (head + 1) * head_size)
        turned[...] = acc[:, columns] * inverse
        upper = total.astype(jnp.bfloat16).astype(jnp.float32)
        kinds = [upper, m_scr[:, head : head + 1], total - upper]
        placed = jnp.zeros((lanes, head_size), jnp.float32)
        for kind, column in enumerate(kinds):
            placed = jnp.where(
                lane == member_of_row + 8 * kind,
                jnp.broadcast_to(column, placed.shape),
                placed,
            )
        gathered = jnp.sum(placed.reshape(rows, group, head_size), axis=1)
        stats[head] = stats[head] + pltpu.roll(gathered, 24 * request, 1)
        for member in range(group):
            index = head * group + member
            target, inside = index // share, index % share
            offset = pl.multiple_of(
                request * (share * head_size) + inside * head_size, head_size
            )
            staged[target, :, pl.ds(offset, head_size)] = turned[
                pl.ds(member, rows, stride=group), :
            ].astype(jnp.bfloat16)

    @pl.when(request == requests - 1)
    def _():
        for target in range(exp_count):
            head = target * share // group
            staged[target, :, requests * share * head_size :] = stats[head].astype(jnp.bfloat16)
        for step_away in range(exp_count):
            out_refs[step_away][...] = staged[info_ref[listed + (-step_away) % exp_count]]


def attend(queries, order, new_keys, new_values, keys, values, local_lengths, base, sub, tail):
    listed, span, kv, head_size = keys.shape
    requests, piece_rows, heads = queries[0].shape[:3]
    pieces = exp_count = len(queries)
    rows = piece_rows * pieces
    share = heads // exp_count
    fresh = new_keys.shape[1]
    width = requests * share * head_size + 128
    info = jnp.concatenate([local_lengths, order])
    factor = head_size ** (-0.5) * math.log2(math.e)
    lanes = rows * heads // kv
    flat = lambda x: x.reshape(listed, x.shape[1] * kv, head_size)
    block = lambda n: pl.BlockSpec((1, n, head_size), lambda r, info: (r + base, 0, 0))
    return pl.pallas_call(
        functools.partial(attend_kernel, pieces, base, listed, sub, tail, factor, exp_count),
        grid_spec=pltpu.PrefetchScalarGridSpec(
            num_scalar_prefetch=1,
            grid=(requests,),
            in_specs=[
                pl.BlockSpec((1, piece_rows, heads, head_size), lambda r, info: (r, 0, 0, 0))
            ]
            * pieces
            + [block(fresh * kv), block(fresh * kv), block(span * kv), block(span * kv)],
            out_specs=[pl.BlockSpec((rows, width), lambda r, info: (0, 0))] * exp_count,
            scratch_shapes=[
                pltpu.VMEM((rows, heads, head_size), jnp.float32),
                pltpu.VMEM((lanes, kv * head_size), jnp.bfloat16),
                pltpu.VMEM((2, 16, head_size), jnp.bfloat16),
                pltpu.VMEM((lanes, 128), jnp.float32),
                pltpu.VMEM((lanes, 128), jnp.float32),
                pltpu.VMEM((lanes, kv * head_size), jnp.float32),
                pltpu.VMEM((lanes, sub * kv), jnp.bfloat16),
                pltpu.VMEM((lanes, sub * kv), jnp.bfloat16),
                pltpu.VMEM((kv, rows, head_size), jnp.float32),
                pltpu.VMEM((lanes, head_size), jnp.float32),
                pltpu.VMEM((exp_count, rows, width), jnp.bfloat16),
            ],
        ),
        out_shape=[jax.ShapeDtypeStruct((rows, width), jnp.bfloat16)] * exp_count,
        compiler_params=pltpu.CompilerParams(dimension_semantics=("arbitrary",)),
        name="attend",
    )(info, *queries, flat(new_keys), flat(new_values), flat(keys), flat(values))


def merge_kernel(parts, batches, share, info_ref, *refs):
    w_refs = refs[batches * parts : (batches + 1) * parts]
    keep_ref, send_ref, attn = refs[(batches + 1) * parts :]
    rows, width = refs[0].shape
    head_size = 128
    requests = (width - head_size) // (share * head_size)
    group_shift = info_ref[0]
    half = info_ref[1]
    for batch in range(batches):
        x_refs = refs[batch * parts : (batch + 1) * parts]
        tables = []
        for x_ref in x_refs:
            table = x_ref[:, width - head_size :].astype(jnp.float32)
            tables.append(pltpu.roll(table, group_shift, 1))
        for request in range(requests):
            first = (batch * requests + request) * rows
            for member in range(share):
                at = 24 * request + member
                tops = [t[:, at + 8 : at + 9] for t in tables]
                sums = [t[:, at : at + 1] + t[:, at + 16 : at + 17] for t in tables]
                top = functools.reduce(jnp.maximum, tops)
                weights = [s * jnp.exp2(m - top) for s, m in zip(sums, tops)]
                inverse = 1.0 / functools.reduce(jnp.add, weights)
                start = (request * share + member) * head_size
                mixed = jnp.zeros((rows, head_size), jnp.float32)
                for weight, x_ref in zip(weights, x_refs):
                    part = x_ref[:, start : start + head_size].astype(jnp.float32)
                    mixed = mixed + jnp.broadcast_to(weight * inverse, part.shape) * part
                attn[
                    first : first + rows, member * head_size : (member + 1) * head_size
                ] = mixed.astype(jnp.bfloat16)
    columns = w_refs[0].shape[1]
    per_half = keep_ref.shape[1] // columns
    for part in range(parts):
        made = jnp.dot(attn[...], w_refs[part][...], preferred_element_type=jnp.float32)
        chunk = info_ref[2 + part]
        inside = pl.multiple_of((chunk % per_half) * columns, columns)

        @pl.when(chunk // per_half == half)
        def _():
            keep_ref[:, pl.ds(inside, columns)] = made

        @pl.when(chunk // per_half != half)
        def _():
            send_ref[:, pl.ds(inside, columns)] = made.astype(jnp.bfloat16)


def merge_project(batches, weights, info, share, requests):
    rows = batches[0][0].shape[0]
    columns = weights[0].shape[1]
    parts = len(weights)
    half_width = parts * columns // 2
    shape = (requests * rows, half_width)
    return pl.pallas_call(
        functools.partial(merge_kernel, parts, len(batches), share),
        in_specs=[pl.BlockSpec(memory_space=pltpu.SMEM)]
        + [pl.BlockSpec(memory_space=pltpu.VMEM)] * ((len(batches) + 1) * parts),
        out_specs=[pl.BlockSpec(memory_space=pltpu.VMEM)] * 2,
        out_shape=[
            jax.ShapeDtypeStruct(shape, jnp.float32),
            jax.ShapeDtypeStruct(shape, jnp.bfloat16),
        ],
        scratch_shapes=[pltpu.VMEM((requests * rows, share * head_size_of(weights, share)), jnp.bfloat16)],
        name="merge_project",
    )(info, *[message for batch in batches for message in batch], *weights)


def head_size_of(weights, share):
    return weights[0].shape[0] // share


def shift(value, axis, step):
    size = lax.axis_size(axis)
    return lax.ppermute(value, axis, [(i, (i + step) % size) for i in range(size)])


def take_block(value, index):
    return lax.dynamic_index_in_dim(value, index, 0, keepdims=False)


def gather_blocks(block, axis):
    return [block] + [shift(block, axis, s) for s in range(1, lax.axis_size(axis))]


def swap(value, axis, bits):
    size = lax.axis_size(axis)
    return lax.ppermute(value, axis, [(i, i ^ bits) for i in range(size)])


def route_table(route_ids, route_weights):
    groups = lax.axis_size("req") * lax.axis_size("exp")
    return jnp.sum(
        jnp.where(
            route_ids[None, :, :] == lax.iota(jnp.int32, groups)[:, None, None],
            route_weights[None, :, :],
            0.0,
        ),
        axis=2,
    )


def exchange_table(column):
    exp_size = lax.axis_size("exp")
    req_at, exp_at = lax.axis_index("req"), lax.axis_index("exp")

    def of(bits):
        picked = lax.dynamic_index_in_dim(
            column, req_at * exp_size + (exp_at ^ bits), 1, keepdims=False
        )
        return picked if bits == 0 else swap(picked, "exp", bits)

    return [of(bits).reshape(-1) for bits in range(exp_size)]


def halves(value, width, axis):
    head_at = lax.axis_index("head")
    own = lax.dynamic_slice_in_dim(value, head_at * width, width, axis)
    other = lax.dynamic_slice_in_dim(value, (1 - head_at) * width, width, axis)
    return own, other


def expert_block(own, weights, gains, maps_in, maps_out):
    other = swap(own, "head", 1)
    wide = [own.astype(jnp.float32), other.astype(jnp.float32)]
    squares = sum(jnp.sum(x * x, axis=-1, keepdims=True) for x in wide)
    factor = lax.rsqrt(squares / (2 * own.shape[1]) + norm_epsilon)
    gate_up = sum(
        jnp.dot((x * factor * gain).astype(jnp.bfloat16), maps, preferred_element_type=jnp.float32)
        for x, gain, maps in zip(wide, gains, maps_in)
    )
    half_units = gate_up.shape[-1] // 2
    activated = (jax.nn.silu(gate_up[:, :half_units]) * gate_up[:, half_units:]).astype(
        jnp.bfloat16
    )
    kept, passed = [
        jnp.dot(activated, maps, preferred_element_type=jnp.float32) * weights[:, None]
        for maps in maps_out
    ]
    return kept, passed.astype(jnp.bfloat16)


def dense_experts(half_hidden, row_weights, gains, maps_in, maps_out):
    row_count, half_width = half_hidden.shape
    req_size = lax.axis_size("req")
    sent = half_hidden.astype(jnp.bfloat16)
    column = jnp.concatenate(gather_blocks(sent, "req"), axis=0)
    middle = column.shape[0] // 2

    def run(block, index):
        return expert_block(block, row_weights[index], gains, maps_in, maps_out)

    def whole(kept, passed):
        return kept + swap(passed, "head", 1).astype(jnp.float32)

    def over(value, bits):
        return swap(value.astype(jnp.bfloat16), "exp", bits).astype(jnp.float32)

    near_x = swap(column, "exp", 1)
    near_y = swap(column, "exp", 2)
    own_kept, own_passed = run(column, 0)
    near_x, near_y, own_passed = lax.optimization_barrier((near_x, near_y, own_passed))
    far_top = swap(near_x[:middle], "exp", 2)
    far_low = swap(near_y[middle:], "exp", 1)
    own = whole(own_kept, own_passed)
    for_x = whole(*run(near_x, 1))
    for_y = whole(*run(near_y, 2))
    top = own[:middle] + over(for_x[:middle], 1)
    low = own[middle:] + over(for_y[middle:], 2)
    far = whole(*run(jnp.concatenate([far_top, far_low], axis=0), 3))
    top = top + over(for_y[:middle] + over(far[:middle], 1), 2)
    low = low + over(for_x[middle:] + over(far[middle:], 2), 1)
    plane_sum = jnp.concatenate([top, low], axis=0).reshape(req_size, row_count, half_width)
    mixture = plane_sum[0]
    outgoing = plane_sum.astype(jnp.bfloat16)
    for s in range(1, req_size):
        mixture = mixture + shift(outgoing[s], "req", -s).astype(jnp.float32)
    return mixture


def sparse_experts(half_hidden, route_ids, route_weights, norm_gain, expert_in, expert_out, capacity):
    row_count, half_width = half_hidden.shape
    head_at = lax.axis_index("head")
    other = shift(half_hidden, "head", 1)
    first = jnp.where(head_at == 0, half_hidden, other)
    second = jnp.where(head_at == 0, other, half_hidden)
    hidden = jnp.concatenate([first, second], axis=1)
    normed = (
        hidden
        * lax.rsqrt(jnp.mean(hidden * hidden, axis=-1, keepdims=True) + norm_epsilon)
        * norm_gain
    ).astype(jnp.bfloat16)
    model_width = 2 * half_width
    local_experts = expert_in.shape[0]
    groups = lax.axis_size("req") * lax.axis_size("exp")
    experts_all = local_experts * groups
    expert_iota = lax.iota(jnp.int32, experts_all)
    named_count = jnp.sum((route_ids[:, :, None] == expert_iota).astype(jnp.int32), axis=1)
    earlier = jnp.cumsum(named_count, axis=0) - named_count
    slot_rank = jnp.take_along_axis(earlier, route_ids, axis=1)
    slot_index = route_ids * capacity + slot_rank
    slot_iota = lax.iota(jnp.int32, experts_all * capacity)
    placing = jnp.any(slot_index[None, :, :] == slot_iota[:, None, None], axis=2).astype(
        jnp.bfloat16
    )
    outgoing = jnp.dot(placing, normed, preferred_element_type=jnp.float32).astype(jnp.bfloat16)
    outgoing = outgoing.reshape(groups, local_experts, capacity, model_width)
    input_maps = expert_in.reshape(local_experts, model_width, -1)
    gate_up = jnp.einsum(
        "geci,eif->gecf",
        lax.all_to_all(outgoing, ("req", "exp"), split_axis=0, concat_axis=0, tiled=True),
        input_maps,
        preferred_element_type=jnp.float32,
    )
    half_units = gate_up.shape[-1] // 2
    activated = (jax.nn.silu(gate_up[..., :half_units]) * gate_up[..., half_units:]).astype(
        jnp.bfloat16
    )
    partial_value = jnp.einsum(
        "gecf,efi->geci", activated, expert_out, preferred_element_type=jnp.float32
    )
    summed = lax.psum_scatter(partial_value, "head", scatter_dimension=3, tiled=True).astype(
        jnp.bfloat16
    )
    returned = lax.all_to_all(summed, ("req", "exp"), split_axis=0, concat_axis=0, tiled=True)
    flat_results = returned.reshape(experts_all * capacity, half_width)
    picked = jnp.take(flat_results, slot_index, axis=0).astype(jnp.float32)
    return jnp.sum(picked * route_weights[:, :, None], axis=1)


def local(
    queries,
    new_keys,
    new_values,
    key_cache,
    value_cache,
    lengths,
    residual,
    out_weight,
    norm_gain,
    route_ids,
    route_weights,
    expert_in,
    expert_out,
):
    requests, span, kv, head_size = key_cache.shape
    heads = queries.shape[2]
    exp_size = lax.axis_size("exp")
    exp_at, head_at = lax.axis_index("exp"), lax.axis_index("head")
    share = heads // exp_size
    group = heads // kv
    sources = (exp_at - lax.iota(jnp.int32, exp_size)) % exp_size
    targets = [(exp_at + s) % exp_size for s in range(exp_size)]

    row_count, model_width = residual.shape
    half_width = model_width // 2
    groups = lax.axis_size("req") * exp_size
    experts_all = expert_in.shape[0] * groups
    capacity = max(2, 2 * row_count * route_ids.shape[1] // experts_all)
    dense = capacity >= row_count and experts_all == groups and exp_size == 4

    batch = requests
    starts = range(0, requests, batch)
    pieces = [
        gather_blocks(lax.slice_in_dim(queries, start, start + batch), "exp") for start in starts
    ]
    local_lengths = jnp.clip(lengths - exp_at * span, 0, span)
    split_weight = out_weight.reshape(exp_size, share * head_size, -1)
    weight_parts = [take_block(split_weight, targets[0])] + [
        shift(take_block(split_weight, targets[s]), "exp", s) for s in range(1, exp_size)
    ]
    if dense:
        column_table = jnp.stack(gather_blocks(route_table(route_ids, route_weights), "req"))
        own_piece, column_table, flat_in = lax.optimization_barrier(
            (pieces[0][0], column_table, expert_in[0].reshape(model_width, -1))
        )
        pieces[0] = [own_piece] + pieces[0][1:]
    received = []
    for start, gathered in zip(starts, pieces):
        messages = attend(
            gathered, sources, new_keys, new_values, key_cache, value_cache, local_lengths,
            start, 512, 256,
        )
        received.append(
            [messages[0]] + [shift(messages[s], "exp", s) for s in range(1, exp_size)]
        )
    if dense:
        maps_in = halves(flat_in, half_width, 0)
        maps_out = halves(expert_out[0], half_width, 1)
        gains = halves(norm_gain, half_width, 0)
        own_message, maps_in, maps_out = lax.optimization_barrier(
            (received[-1][0], maps_in, maps_out)
        )
        received[-1] = [own_message] + received[-1][1:]
    group_shift = (head_size - (exp_at * share) % group) % head_size
    info = jnp.concatenate([jnp.stack([group_shift, head_at]).astype(jnp.int32), sources])
    kept, sent = merge_project(received, weight_parts, info, share, requests)
    if dense:
        kept, column_table = lax.optimization_barrier((kept, column_table))
        row_weights = exchange_table(column_table)
    both = kept + shift(sent, "head", 1).astype(jnp.float32)
    both = both.reshape(exp_size, row_count, half_width)
    outgoing = both.astype(jnp.bfloat16)
    hidden = lax.dynamic_slice_in_dim(residual, head_at * half_width, half_width, 1).astype(
        jnp.float32
    ) + take_block(both, targets[0])
    for s in range(1, exp_size):
        hidden = hidden + shift(take_block(outgoing, targets[s]), "exp", s).astype(jnp.float32)

    if dense:
        mixture = dense_experts(hidden, row_weights, gains, maps_in, maps_out)
    else:
        mixture = sparse_experts(
            hidden, route_ids, route_weights, norm_gain, expert_in, expert_out, capacity
        )
    return (hidden + mixture).astype(jnp.bfloat16)


def solution(mesh):
    return jax.shard_map(
        local,
        mesh=mesh,
        in_specs=(
            P("req", "exp", "head", None),
            P("req", "exp", "head", None),
            P("req", "exp", "head", None),
            P("req", "exp", "head", None),
            P("req", "exp", "head", None),
            P("req"),
            P(("req", "exp"), None),
            P("head", "exp"),
            P(),
            P(("req", "exp"), None),
            P(("req", "exp"), None),
            P(("req", "exp"), None, None, "head"),
            P(("req", "exp"), "head", None),
        ),
        out_specs=P(("req", "exp"), "head"),
        check_vma=False,
    )
```

```python
import functools
import math
import jax
import jax.numpy as jnp
from jax import lax
from jax.experimental import pallas as pl
from jax.experimental.pallas import tpu as pltpu
from jax.sharding import PartitionSpec as P


masked_score = -1e30
norm_epsilon = 1e-06


def attend_kernel(pieces, base, listed, sub, tail, factor, exp_count, info_ref, *refs):
    q_refs = refs[:pieces]
    nk_ref, nv_ref, k_ref, v_ref = refs[pieces : pieces + 4]
    out_refs = refs[pieces + 4 : pieces + 4 + exp_count]
    scratch = refs[pieces + 4 + exp_count :]
    q_all, q_cat, pattern, m_scr, l_scr, acc, p_even, p_odd, stats, turned, staged = scratch
    requests = pl.num_programs(0)
    request = pl.program_id(0)
    head_size = k_ref.shape[2]
    kv = 2
    piece_rows, heads = q_refs[0].shape[1], q_refs[0].shape[2]
    group = heads // kv
    rows = piece_rows * pieces
    lanes = rows * group
    length = info_ref[request + base]
    even_lane = lax.broadcasted_iota(jnp.int32, (lanes, 128), 1) % 2 == 0

    @pl.when(request == 0)
    def _():
        stats[...] = jnp.zeros_like(stats)
        parity = lax.broadcasted_iota(jnp.int32, (16, head_size), 0) % 2
        pattern[0] = (1 - parity).astype(jnp.float32).astype(jnp.bfloat16)
        pattern[1] = parity.astype(jnp.float32).astype(jnp.bfloat16)

    for piece in range(pieces):
        where_to = info_ref[listed + piece] * piece_rows
        q_all[pl.ds(where_to, piece_rows)] = q_refs[piece][0].astype(jnp.float32)
    for head in range(kv):
        chosen = q_all[:, head * group : (head + 1) * group, :].reshape(lanes, head_size)
        q_cat[:, head * head_size : (head + 1) * head_size] = chosen.astype(jnp.bfloat16)

    def spread(block):
        if block.shape[0] < 16:
            left = block * pattern[0, : block.shape[0]]
            right = block * pattern[1, : block.shape[0]]
        else:
            tiles = block.reshape(block.shape[0] // 16, 16, head_size)
            left = (tiles * pattern[0][None]).reshape(block.shape)
            right = (tiles * pattern[1][None]).reshape(block.shape)
        return jnp.concatenate([left, right], axis=1)

    def score(block):
        return lax.dot_general(
            q_cat[...],
            spread(block),
            (((1,), (1,)), ((), ())),
            preferred_element_type=jnp.float32,
        )

    def both_columns(even, odd):
        shape = (lanes, 128)
        return jnp.where(even_lane, jnp.broadcast_to(even, shape), jnp.broadcast_to(odd, shape))

    def reduce_parity(wide, op, neutral):
        even = op(jnp.where(even_lane, wide, neutral), axis=1, keepdims=True)
        odd = op(jnp.where(even_lane, neutral, wide), axis=1, keepdims=True)
        return even, odd

    def init():
        scores = score(nk_ref[0]) * factor
        even = lax.broadcasted_iota(jnp.int32, scores.shape, 1) % 2 == 0
        top_even = jnp.max(jnp.where(even, scores, -jnp.inf), axis=1, keepdims=True)
        top_odd = jnp.max(jnp.where(even, -jnp.inf, scores), axis=1, keepdims=True)
        top_even = top_even.astype(jnp.bfloat16).astype(jnp.float32)
        top_odd = top_odd.astype(jnp.bfloat16).astype(jnp.float32)
        m_scr[...] = both_columns(top_even, top_odd)
        probs = jnp.exp2(
            scores
            - jnp.where(
                even,
                jnp.broadcast_to(top_even, scores.shape),
                jnp.broadcast_to(top_odd, scores.shape),
            )
        )
        l_even = jnp.sum(jnp.where(even, probs, 0.0), axis=1, keepdims=True)
        l_odd = jnp.sum(jnp.where(even, 0.0, probs), axis=1, keepdims=True)
        lane = lax.broadcasted_iota(jnp.int32, (lanes, 128), 1)
        l_scr[...] = jnp.where(lane < 2, both_columns(l_even, l_odd), 0.0)
        acc[...] = jnp.dot(
            probs.astype(jnp.bfloat16), spread(nv_ref[0]), preferred_element_type=jnp.float32
        )

    def piece_of(ref, start, size):
        return ref[0, pl.ds(pl.multiple_of(start * kv, kv * tail), size * kv), :]

    step = 256

    def soften(start, size, target, masked):
        top = m_scr[...]
        total = l_scr[...]
        for tile in range(size * kv // step):
            scores = score(piece_of_tile(k_ref, start, tile))
            for part in range(step // 128):
                piece = scores[:, part * 128 : (part + 1) * 128]
                probs = jnp.exp2(piece * factor - top)
                if masked:
                    lane = lax.broadcasted_iota(jnp.int32, (1, 128), 1)
                    position = start + (tile * step + part * 128 + lane) // kv
                    probs = jnp.where(position < length, probs, 0.0)
                total = total + probs
                at = tile * step + part * 128
                target[:, at : at + 128] = probs.astype(jnp.bfloat16)
        l_scr[...] = total

    def piece_of_tile(ref, start, tile):
        first = pl.multiple_of(start * kv, kv * tail) + tile * step
        return ref[0, pl.ds(first, step), :]

    def weigh(start, size, source):
        values = spread(piece_of(v_ref, start, size))
        acc[...] += jnp.dot(source[:, : size * kv], values, preferred_element_type=jnp.float32)

    init()
    here = length
    pairs = here // (2 * sub)

    def loop(i, carry):
        start = pl.multiple_of(i * 2 * sub, 2 * sub)
        before = jnp.maximum(start - sub, 0)
        soften(start, sub, p_even, False)
        weigh(before, sub, p_odd)
        soften(start + sub, sub, p_odd, False)
        weigh(start, sub, p_even)
        return carry

    p_odd[...] = jnp.zeros_like(p_odd)
    lax.fori_loop(0, pairs, loop, 0)
    weigh(pl.multiple_of(jnp.maximum(pairs * 2 * sub - sub, 0), sub), sub, p_odd)

    def tail_loop(i, carry):
        start = pl.multiple_of(pairs * 2 * sub + i * tail, tail)
        soften(start, tail, p_even, True)
        weigh(start, tail, p_even)
        return carry

    lax.fori_loop(0, (here - pairs * 2 * sub + tail - 1) // tail, tail_loop, 0)
    largest = jnp.max(l_scr[...])

    @pl.when(jnp.logical_not(largest < 1e30))
    def _():
        init()

        def slow_loop(i, carry):
            start = pl.multiple_of(i * tail, tail)
            scores = score(piece_of(k_ref, start, tail)) * factor
            lane = lax.broadcasted_iota(jnp.int32, (1, tail * kv), 1)
            inside = start + lane // kv < length
            scores = jnp.where(inside, scores, masked_score)
            wide = m_scr[...]
            for part in range(tail * kv // 128):
                wide = jnp.maximum(wide, scores[:, part * 128 : (part + 1) * 128])
            even, odd = reduce_parity(wide, jnp.max, -jnp.inf)
            even = even.astype(jnp.bfloat16).astype(jnp.float32)
            odd = odd.astype(jnp.bfloat16).astype(jnp.float32)
            top = both_columns(even, odd)
            fade = jnp.exp2(m_scr[...] - top)
            total = l_scr[...] * fade
            for part in range(tail * kv // 128):
                at = part * 128
                probs = jnp.where(
                    inside[:, at : at + 128], jnp.exp2(scores[:, at : at + 128] - top), 0.0
                )
                total = total + probs
                p_even[:, at : at + 128] = probs.astype(jnp.bfloat16)
            l_scr[...] = total
            m_scr[...] = top
            for head in range(kv):
                columns = slice(head * head_size, (head + 1) * head_size)
                acc[:, columns] = acc[:, columns] * jnp.broadcast_to(
                    fade[:, head : head + 1], (lanes, head_size)
                )
            weigh(start, tail, p_even)
            return carry

        lax.fori_loop(0, (here + tail - 1) // tail, slow_loop, 0)

    share = heads // exp_count
    totals = reduce_parity(l_scr[...], jnp.sum, 0.0)
    lane = lax.broadcasted_iota(jnp.int32, (lanes, head_size), 1)
    member_of_row = lax.broadcasted_iota(jnp.int32, (lanes, head_size), 0) % group
    for head in range(kv):
        total = totals[head]
        inverse = jnp.broadcast_to(1.0 / total, (lanes, head_size))
        columns = slice(head * head_size, (head + 1) * head_size)
        turned[...] = acc[:, columns] * inverse
        upper = total.astype(jnp.bfloat16).astype(jnp.float32)
        kinds = [upper, m_scr[:, head : head + 1], total - upper]
        placed = jnp.zeros((lanes, head_size), jnp.float32)
        for kind, column in enumerate(kinds):
            placed = jnp.where(
                lane == member_of_row + 8 * kind,
                jnp.broadcast_to(column, placed.shape),
                placed,
            )
        gathered = jnp.sum(placed.reshape(rows, group, head_size), axis=1)
        stats[head] = stats[head] + pltpu.roll(gathered, 24 * request, 1)
        for member in range(group):
            index = head * group + member
            target, inside = index // share, index % share
            offset = pl.multiple_of(
                request * (share * head_size) + inside * head_size, head_size
            )
            staged[target, :, pl.ds(offset, head_size)] = turned[
                pl.ds(member, rows, stride=group), :
            ].astype(jnp.bfloat16)

    @pl.when(request == requests - 1)
    def _():
        for target in range(exp_count):
            head = target * share // group
            staged[target, :, requests * share * head_size :] = stats[head].astype(jnp.bfloat16)
        for step_away in range(exp_count):
            out_refs[step_away][...] = staged[info_ref[listed + (-step_away) % exp_count]]


def attend(queries, order, new_keys, new_values, keys, values, local_lengths, base, sub, tail):
    listed, span, kv, head_size = keys.shape
    requests, piece_rows, heads = queries[0].shape[:3]
    pieces = exp_count = len(queries)
    rows = piece_rows * pieces
    share = heads // exp_count
    fresh = new_keys.shape[1]
    width = requests * share * head_size + 128
    info = jnp.concatenate([local_lengths, order])
    factor = head_size ** (-0.5) * math.log2(math.e)
    lanes = rows * heads // kv
    flat = lambda x: x.reshape(listed, x.shape[1] * kv, head_size)
    block = lambda n: pl.BlockSpec((1, n, head_size), lambda r, info: (r + base, 0, 0))
    return pl.pallas_call(
        functools.partial(attend_kernel, pieces, base, listed, sub, tail, factor, exp_count),
        grid_spec=pltpu.PrefetchScalarGridSpec(
            num_scalar_prefetch=1,
            grid=(requests,),
            in_specs=[
                pl.BlockSpec((1, piece_rows, heads, head_size), lambda r, info: (r, 0, 0, 0))
            ]
            * pieces
            + [block(fresh * kv), block(fresh * kv), block(span * kv), block(span * kv)],
            out_specs=[pl.BlockSpec((rows, width), lambda r, info: (0, 0))] * exp_count,
            scratch_shapes=[
                pltpu.VMEM((rows, heads, head_size), jnp.float32),
                pltpu.VMEM((lanes, kv * head_size), jnp.bfloat16),
                pltpu.VMEM((2, 16, head_size), jnp.bfloat16),
                pltpu.VMEM((lanes, 128), jnp.float32),
                pltpu.VMEM((lanes, 128), jnp.float32),
                pltpu.VMEM((lanes, kv * head_size), jnp.float32),
                pltpu.VMEM((lanes, sub * kv), jnp.bfloat16),
                pltpu.VMEM((lanes, sub * kv), jnp.bfloat16),
                pltpu.VMEM((kv, rows, head_size), jnp.float32),
                pltpu.VMEM((lanes, head_size), jnp.float32),
                pltpu.VMEM((exp_count, rows, width), jnp.bfloat16),
            ],
        ),
        out_shape=[jax.ShapeDtypeStruct((rows, width), jnp.bfloat16)] * exp_count,
        compiler_params=pltpu.CompilerParams(dimension_semantics=("arbitrary",)),
        name="attend",
    )(info, *queries, flat(new_keys), flat(new_values), flat(keys), flat(values))


def merge_kernel(parts, batches, share, info_ref, *refs):
    w_refs = refs[batches * parts : (batches + 1) * parts]
    keep_ref, send_ref, attn = refs[(batches + 1) * parts :]
    rows, width = refs[0].shape
    head_size = 128
    requests = (width - head_size) // (share * head_size)
    group_shift = info_ref[0]
    half = info_ref[1]
    for batch in range(batches):
        x_refs = refs[batch * parts : (batch + 1) * parts]
        tables = []
        for x_ref in x_refs:
            table = x_ref[:, width - head_size :].astype(jnp.float32)
            tables.append(pltpu.roll(table, group_shift, 1))
        for request in range(requests):
            first = (batch * requests + request) * rows
            for member in range(share):
                at = 24 * request + member
                tops = [t[:, at + 8 : at + 9] for t in tables]
                sums = [t[:, at : at + 1] + t[:, at + 16 : at + 17] for t in tables]
                top = functools.reduce(jnp.maximum, tops)
                weights = [s * jnp.exp2(m - top) for s, m in zip(sums, tops)]
                inverse = 1.0 / functools.reduce(jnp.add, weights)
                start = (request * share + member) * head_size
                mixed = jnp.zeros((rows, head_size), jnp.float32)
                for weight, x_ref in zip(weights, x_refs):
                    part = x_ref[:, start : start + head_size].astype(jnp.float32)
                    mixed = mixed + jnp.broadcast_to(weight * inverse, part.shape) * part
                attn[
                    first : first + rows, member * head_size : (member + 1) * head_size
                ] = mixed.astype(jnp.bfloat16)
    columns = w_refs[0].shape[1]
    per_half = keep_ref.shape[1] // columns
    for part in range(parts):
        made = jnp.dot(attn[...], w_refs[part][...], preferred_element_type=jnp.float32)
        chunk = info_ref[2 + part]
        inside = pl.multiple_of((chunk % per_half) * columns, columns)

        @pl.when(chunk // per_half == half)
        def _():
            keep_ref[:, pl.ds(inside, columns)] = made

        @pl.when(chunk // per_half != half)
        def _():
            send_ref[:, pl.ds(inside, columns)] = made.astype(jnp.bfloat16)


def merge_project(batches, weights, info, share, requests):
    rows = batches[0][0].shape[0]
    columns = weights[0].shape[1]
    parts = len(weights)
    half_width = parts * columns // 2
    shape = (requests * rows, half_width)
    return pl.pallas_call(
        functools.partial(merge_kernel, parts, len(batches), share),
        in_specs=[pl.BlockSpec(memory_space=pltpu.SMEM)]
        + [pl.BlockSpec(memory_space=pltpu.VMEM)] * ((len(batches) + 1) * parts),
        out_specs=[pl.BlockSpec(memory_space=pltpu.VMEM)] * 2,
        out_shape=[
            jax.ShapeDtypeStruct(shape, jnp.float32),
            jax.ShapeDtypeStruct(shape, jnp.bfloat16),
        ],
        scratch_shapes=[pltpu.VMEM((requests * rows, share * head_size_of(weights, share)), jnp.bfloat16)],
        name="merge_project",
    )(info, *[message for batch in batches for message in batch], *weights)


def head_size_of(weights, share):
    return weights[0].shape[0] // share


def shift(value, axis, step):
    size = lax.axis_size(axis)
    return lax.ppermute(value, axis, [(i, (i + step) % size) for i in range(size)])


def take_block(value, index):
    return lax.dynamic_index_in_dim(value, index, 0, keepdims=False)


def gather_blocks(block, axis):
    return [block] + [shift(block, axis, s) for s in range(1, lax.axis_size(axis))]


def swap(value, axis, bits):
    size = lax.axis_size(axis)
    return lax.ppermute(value, axis, [(i, i ^ bits) for i in range(size)])


def route_table(route_ids, route_weights):
    groups = lax.axis_size("req") * lax.axis_size("exp")
    return jnp.sum(
        jnp.where(
            route_ids[None, :, :] == lax.iota(jnp.int32, groups)[:, None, None],
            route_weights[None, :, :],
            0.0,
        ),
        axis=2,
    )


def exchange_table(column):
    exp_size = lax.axis_size("exp")
    req_at, exp_at = lax.axis_index("req"), lax.axis_index("exp")

    def of(bits):
        picked = lax.dynamic_index_in_dim(
            column, req_at * exp_size + (exp_at ^ bits), 1, keepdims=False
        )
        return picked if bits == 0 else swap(picked, "exp", bits)

    return [of(bits).reshape(-1) for bits in range(exp_size)]


def halves(value, width, axis):
    head_at = lax.axis_index("head")
    own = lax.dynamic_slice_in_dim(value, head_at * width, width, axis)
    other = lax.dynamic_slice_in_dim(value, (1 - head_at) * width, width, axis)
    return own, other


def expert_block(own, weights, gains, maps_in, maps_out):
    other = swap(own, "head", 1)
    wide = [own.astype(jnp.float32), other.astype(jnp.float32)]
    squares = sum(jnp.sum(x * x, axis=-1, keepdims=True) for x in wide)
    factor = lax.rsqrt(squares / (2 * own.shape[1]) + norm_epsilon)
    scaled = [(x * factor * gain).astype(jnp.bfloat16) for x, gain in zip(wide, gains)]
    gate_up = jnp.dot(scaled[0], maps_in[0], preferred_element_type=jnp.float32)
    gate_up = gate_up + jnp.dot(scaled[1], maps_in[1], preferred_element_type=jnp.float32)
    half_units = gate_up.shape[-1] // 2
    activated = (jax.nn.silu(gate_up[:, :half_units]) * gate_up[:, half_units:]).astype(
        jnp.bfloat16
    )
    kept, passed = [
        jnp.dot(activated, maps, preferred_element_type=jnp.float32) * weights[:, None]
        for maps in maps_out
    ]
    return kept, passed.astype(jnp.bfloat16)


def dense_experts(half_hidden, row_weights, gains, maps_in, maps_out):
    row_count, half_width = half_hidden.shape
    req_size = lax.axis_size("req")
    sent = half_hidden.astype(jnp.bfloat16)
    sent, row_weights = lax.optimization_barrier((sent, row_weights))
    column = jnp.concatenate(gather_blocks(sent, "req"), axis=0)
    middle = column.shape[0] // 2

    def run(block, index):
        return expert_block(block, row_weights[index], gains, maps_in, maps_out)

    def whole(kept, passed):
        return kept + swap(passed, "head", 1).astype(jnp.float32)

    def over(value, bits):
        return swap(value.astype(jnp.bfloat16), "exp", bits).astype(jnp.float32)

    near_x = swap(column, "exp", 1)
    near_y = swap(column, "exp", 2)
    own_kept, own_passed = run(column, 0)
    near_x, near_y, own_passed = lax.optimization_barrier((near_x, near_y, own_passed))
    far_top = swap(near_x[:middle], "exp", 2)
    far_low = swap(near_y[middle:], "exp", 1)
    own = whole(own_kept, own_passed)
    for_x = whole(*run(near_x, 1))
    for_y = whole(*run(near_y, 2))
    back_x = over(for_x[:middle], 1)
    back_y = over(for_y[middle:], 2)
    top = own[:middle] + back_x
    low = own[middle:] + back_y
    far = whole(*run(jnp.concatenate([far_top, far_low], axis=0), 3))
    top = top + over(for_y[:middle] + over(far[:middle], 1), 2)
    low = low + over(for_x[middle:] + over(far[middle:], 2), 1)
    plane_sum = jnp.concatenate([top, low], axis=0).reshape(req_size, row_count, half_width)
    mixture = plane_sum[0]
    outgoing = plane_sum.astype(jnp.bfloat16)
    for s in range(1, req_size):
        mixture = mixture + shift(outgoing[s], "req", -s).astype(jnp.float32)
    return mixture


def sparse_experts(half_hidden, route_ids, route_weights, norm_gain, expert_in, expert_out, capacity):
    _, half_width = half_hidden.shape
    head_at = lax.axis_index("head")
    other = shift(half_hidden, "head", 1)
    first = jnp.where(head_at == 0, half_hidden, other)
    second = jnp.where(head_at == 0, other, half_hidden)
    hidden = jnp.concatenate([first, second], axis=1)
    normed = (
        hidden
        * lax.rsqrt(jnp.mean(hidden * hidden, axis=-1, keepdims=True) + norm_epsilon)
        * norm_gain
    ).astype(jnp.bfloat16)
    model_width = 2 * half_width
    local_experts = expert_in.shape[0]
    groups = lax.axis_size("req") * lax.axis_size("exp")
    experts_all = local_experts * groups
    expert_iota = lax.iota(jnp.int32, experts_all)
    named_count = jnp.sum((route_ids[:, :, None] == expert_iota).astype(jnp.int32), axis=1)
    earlier = jnp.cumsum(named_count, axis=0) - named_count
    slot_rank = jnp.take_along_axis(earlier, route_ids, axis=1)
    slot_index = route_ids * capacity + slot_rank
    slot_iota = lax.iota(jnp.int32, experts_all * capacity)
    placing = jnp.any(slot_index[None, :, :] == slot_iota[:, None, None], axis=2).astype(
        jnp.bfloat16
    )
    outgoing = jnp.dot(placing, normed, preferred_element_type=jnp.float32).astype(jnp.bfloat16)
    outgoing = outgoing.reshape(groups, local_experts, capacity, model_width)
    input_maps = expert_in.reshape(local_experts, model_width, -1)
    gate_up = jnp.einsum(
        "geci,eif->gecf",
        lax.all_to_all(outgoing, ("req", "exp"), split_axis=0, concat_axis=0, tiled=True),
        input_maps,
        preferred_element_type=jnp.float32,
    )
    half_units = gate_up.shape[-1] // 2
    activated = (jax.nn.silu(gate_up[..., :half_units]) * gate_up[..., half_units:]).astype(
        jnp.bfloat16
    )
    partial_value = jnp.einsum(
        "gecf,efi->geci", activated, expert_out, preferred_element_type=jnp.float32
    )
    summed = lax.psum_scatter(partial_value, "head", scatter_dimension=3, tiled=True).astype(
        jnp.bfloat16
    )
    returned = lax.all_to_all(summed, ("req", "exp"), split_axis=0, concat_axis=0, tiled=True)
    flat_results = returned.reshape(experts_all * capacity, half_width)
    picked = jnp.take(flat_results, slot_index, axis=0).astype(jnp.float32)
    return jnp.sum(picked * route_weights[:, :, None], axis=1)


def local(
    queries,
    new_keys,
    new_values,
    key_cache,
    value_cache,
    lengths,
    residual,
    out_weight,
    norm_gain,
    route_ids,
    route_weights,
    expert_in,
    expert_out,
):
    requests, span, kv, head_size = key_cache.shape
    heads = queries.shape[2]
    exp_size = lax.axis_size("exp")
    exp_at, head_at = lax.axis_index("exp"), lax.axis_index("head")
    share = heads // exp_size
    group = heads // kv
    sources = (exp_at - lax.iota(jnp.int32, exp_size)) % exp_size
    targets = [(exp_at + s) % exp_size for s in range(exp_size)]

    row_count, model_width = residual.shape
    half_width = model_width // 2
    groups = lax.axis_size("req") * exp_size
    experts_all = expert_in.shape[0] * groups
    capacity = max(2, 2 * row_count * route_ids.shape[1] // experts_all)
    dense = capacity >= row_count and experts_all == groups and exp_size == 4

    batch = requests
    starts = range(0, requests, batch)
    pieces = [
        gather_blocks(lax.slice_in_dim(queries, start, start + batch), "exp") for start in starts
    ]
    local_lengths = jnp.clip(lengths - exp_at * span, 0, span)
    split_weight = out_weight.reshape(exp_size, share * head_size, -1)
    weight_parts = [take_block(split_weight, targets[0])] + [
        shift(take_block(split_weight, targets[s]), "exp", s) for s in range(1, exp_size)
    ]
    if dense:
        column_table = jnp.stack(gather_blocks(route_table(route_ids, route_weights), "req"))
        own_piece, column_table, flat_in = lax.optimization_barrier(
            (pieces[0][0], column_table, expert_in[0].reshape(model_width, -1))
        )
        pieces[0] = [own_piece] + pieces[0][1:]
    received = []
    for start, gathered in zip(starts, pieces):
        messages = attend(
            gathered, sources, new_keys, new_values, key_cache, value_cache, local_lengths,
            start, 512, 256,
        )
        received.append(
            [messages[0]] + [shift(messages[s], "exp", s) for s in range(1, exp_size)]
        )
    if dense:
        maps_in = halves(flat_in, half_width, 0)
        maps_out = halves(expert_out[0], half_width, 1)
        gains = halves(norm_gain, half_width, 0)
        own_message, maps_in, maps_out = lax.optimization_barrier(
            (received[-1][0], maps_in, maps_out)
        )
        received[-1] = [own_message] + received[-1][1:]
    group_shift = (head_size - (exp_at * share) % group) % head_size
    info = jnp.concatenate([jnp.stack([group_shift, head_at]).astype(jnp.int32), sources])
    kept, sent = merge_project(received, weight_parts, info, share, requests)
    if dense:
        kept, column_table = lax.optimization_barrier((kept, column_table))
        row_weights = exchange_table(column_table)
    both = kept + shift(sent, "head", 1).astype(jnp.float32)
    both = both.reshape(exp_size, row_count, half_width)
    outgoing = both.astype(jnp.bfloat16)
    hidden = lax.dynamic_slice_in_dim(residual, head_at * half_width, half_width, 1).astype(
        jnp.float32
    ) + take_block(both, targets[0])
    for s in range(1, exp_size):
        hidden = hidden + shift(take_block(outgoing, targets[s]), "exp", s).astype(jnp.float32)

    if dense:
        mixture = dense_experts(hidden, row_weights, gains, maps_in, maps_out)
    else:
        mixture = sparse_experts(
            hidden, route_ids, route_weights, norm_gain, expert_in, expert_out, capacity
        )
    return (hidden + mixture).astype(jnp.bfloat16)


def solution(mesh):
    return jax.shard_map(
        local,
        mesh=mesh,
        in_specs=(
            P("req", "exp", "head", None),
            P("req", "exp", "head", None),
            P("req", "exp", "head", None),
            P("req", "exp", "head", None),
            P("req", "exp", "head", None),
            P("req"),
            P(("req", "exp"), None),
            P("head", "exp"),
            P(),
            P(("req", "exp"), None),
            P(("req", "exp"), None),
            P(("req", "exp"), None, None, "head"),
            P(("req", "exp"), "head", None),
        ),
        out_specs=P(("req", "exp"), "head"),
        check_vma=False,
    )
```

```python
import functools
import math
import jax
import jax.numpy as jnp
from jax import lax
from jax.experimental import pallas as pl
from jax.experimental.pallas import tpu as pltpu
from jax.sharding import PartitionSpec as P


masked_score = -1e30
norm_epsilon = 1e-06


def attend_kernel(pieces, base, listed, sub, tail, factor, exp_count, info_ref, *refs):
    q_refs = refs[:pieces]
    nk_ref, nv_ref, k_ref, v_ref = refs[pieces : pieces + 4]
    out_refs = refs[pieces + 4 : pieces + 4 + exp_count]
    scratch = refs[pieces + 4 + exp_count :]
    q_all, q_cat, pattern, m_scr, l_scr, acc, p_even, p_odd, stats, turned, staged = scratch
    requests = pl.num_programs(0)
    request = pl.program_id(0)
    head_size = k_ref.shape[2]
    kv = 2
    piece_rows, heads = q_refs[0].shape[1], q_refs[0].shape[2]
    group = heads // kv
    rows = piece_rows * pieces
    lanes = rows * group
    length = info_ref[request + base]
    even_lane = lax.broadcasted_iota(jnp.int32, (lanes, 128), 1) % 2 == 0

    @pl.when(request == 0)
    def _():
        stats[...] = jnp.zeros_like(stats)
        parity = lax.broadcasted_iota(jnp.int32, (16, head_size), 0) % 2
        pattern[0] = (1 - parity).astype(jnp.float32).astype(jnp.bfloat16)
        pattern[1] = parity.astype(jnp.float32).astype(jnp.bfloat16)

    for piece in range(pieces):
        where_to = info_ref[listed + piece] * piece_rows
        q_all[pl.ds(where_to, piece_rows)] = q_refs[piece][0].astype(jnp.float32)
    for head in range(kv):
        chosen = q_all[:, head * group : (head + 1) * group, :].reshape(lanes, head_size)
        q_cat[:, head * head_size : (head + 1) * head_size] = chosen.astype(jnp.bfloat16)

    def spread(block):
        if block.shape[0] < 16:
            left = block * pattern[0, : block.shape[0]]
            right = block * pattern[1, : block.shape[0]]
        else:
            tiles = block.reshape(block.shape[0] // 16, 16, head_size)
            left = (tiles * pattern[0][None]).reshape(block.shape)
            right = (tiles * pattern[1][None]).reshape(block.shape)
        return jnp.concatenate([left, right], axis=1)

    def score(block):
        return lax.dot_general(
            q_cat[...],
            spread(block),
            (((1,), (1,)), ((), ())),
            preferred_element_type=jnp.float32,
        )

    def both_columns(even, odd):
        shape = (lanes, 128)
        return jnp.where(even_lane, jnp.broadcast_to(even, shape), jnp.broadcast_to(odd, shape))

    def reduce_parity(wide, op, neutral):
        even = op(jnp.where(even_lane, wide, neutral), axis=1, keepdims=True)
        odd = op(jnp.where(even_lane, neutral, wide), axis=1, keepdims=True)
        return even, odd

    def init():
        scores = score(nk_ref[0]) * factor
        even = lax.broadcasted_iota(jnp.int32, scores.shape, 1) % 2 == 0
        top_even = jnp.max(jnp.where(even, scores, -jnp.inf), axis=1, keepdims=True)
        top_odd = jnp.max(jnp.where(even, -jnp.inf, scores), axis=1, keepdims=True)
        top_even = top_even.astype(jnp.bfloat16).astype(jnp.float32)
        top_odd = top_odd.astype(jnp.bfloat16).astype(jnp.float32)
        m_scr[...] = both_columns(top_even, top_odd)
        probs = jnp.exp2(
            scores
            - jnp.where(
                even,
                jnp.broadcast_to(top_even, scores.shape),
                jnp.broadcast_to(top_odd, scores.shape),
            )
        )
        l_even = jnp.sum(jnp.where(even, probs, 0.0), axis=1, keepdims=True)
        l_odd = jnp.sum(jnp.where(even, 0.0, probs), axis=1, keepdims=True)
        lane = lax.broadcasted_iota(jnp.int32, (lanes, 128), 1)
        l_scr[...] = jnp.where(lane < 2, both_columns(l_even, l_odd), 0.0)
        acc[...] = jnp.dot(
            probs.astype(jnp.bfloat16), spread(nv_ref[0]), preferred_element_type=jnp.float32
        )

    def piece_of(ref, start, size):
        return ref[0, pl.ds(pl.multiple_of(start * kv, kv * tail), size * kv), :]

    step = 256

    def soften(start, size, target, masked):
        top = m_scr[...]
        total = l_scr[...]
        for tile in range(size * kv // step):
            scores = score(piece_of_tile(k_ref, start, tile))
            for part in range(step // 128):
                piece = scores[:, part * 128 : (part + 1) * 128]
                probs = jnp.exp2(piece * factor - top)
                if masked:
                    lane = lax.broadcasted_iota(jnp.int32, (1, 128), 1)
                    position = start + (tile * step + part * 128 + lane) // kv
                    probs = jnp.where(position < length, probs, 0.0)
                total = total + probs
                at = tile * step + part * 128
                target[:, at : at + 128] = probs.astype(jnp.bfloat16)
        l_scr[...] = total

    def piece_of_tile(ref, start, tile):
        first = pl.multiple_of(start * kv, kv * tail) + tile * step
        return ref[0, pl.ds(first, step), :]

    def weigh(start, size, source):
        values = spread(piece_of(v_ref, start, size))
        acc[...] += jnp.dot(source[:, : size * kv], values, preferred_element_type=jnp.float32)

    init()
    here = length
    pairs = here // (2 * sub)

    def loop(i, carry):
        start = pl.multiple_of(i * 2 * sub, 2 * sub)
        before = jnp.maximum(start - sub, 0)
        soften(start, sub, p_even, False)
        weigh(before, sub, p_odd)
        soften(start + sub, sub, p_odd, False)
        weigh(start, sub, p_even)
        return carry

    p_odd[...] = jnp.zeros_like(p_odd)
    lax.fori_loop(0, pairs, loop, 0)
    weigh(pl.multiple_of(jnp.maximum(pairs * 2 * sub - sub, 0), sub), sub, p_odd)

    def tail_loop(i, carry):
        start = pl.multiple_of(pairs * 2 * sub + i * tail, tail)
        soften(start, tail, p_even, True)
        weigh(start, tail, p_even)
        return carry

    lax.fori_loop(0, (here - pairs * 2 * sub + tail - 1) // tail, tail_loop, 0)
    largest = jnp.max(l_scr[...])

    @pl.when(jnp.logical_not(largest < 1e30))
    def _():
        init()

        def slow_loop(i, carry):
            start = pl.multiple_of(i * tail, tail)
            scores = score(piece_of(k_ref, start, tail)) * factor
            lane = lax.broadcasted_iota(jnp.int32, (1, tail * kv), 1)
            inside = start + lane // kv < length
            scores = jnp.where(inside, scores, masked_score)
            wide = m_scr[...]
            for part in range(tail * kv // 128):
                wide = jnp.maximum(wide, scores[:, part * 128 : (part + 1) * 128])
            even, odd = reduce_parity(wide, jnp.max, -jnp.inf)
            even = even.astype(jnp.bfloat16).astype(jnp.float32)
            odd = odd.astype(jnp.bfloat16).astype(jnp.float32)
            top = both_columns(even, odd)
            fade = jnp.exp2(m_scr[...] - top)
            total = l_scr[...] * fade
            for part in range(tail * kv // 128):
                at = part * 128
                probs = jnp.where(
                    inside[:, at : at + 128], jnp.exp2(scores[:, at : at + 128] - top), 0.0
                )
                total = total + probs
                p_even[:, at : at + 128] = probs.astype(jnp.bfloat16)
            l_scr[...] = total
            m_scr[...] = top
            for head in range(kv):
                columns = slice(head * head_size, (head + 1) * head_size)
                acc[:, columns] = acc[:, columns] * jnp.broadcast_to(
                    fade[:, head : head + 1], (lanes, head_size)
                )
            weigh(start, tail, p_even)
            return carry

        lax.fori_loop(0, (here + tail - 1) // tail, slow_loop, 0)

    share = heads // exp_count
    totals = reduce_parity(l_scr[...], jnp.sum, 0.0)
    lane = lax.broadcasted_iota(jnp.int32, (lanes, head_size), 1)
    member_of_row = lax.broadcasted_iota(jnp.int32, (lanes, head_size), 0) % group
    for head in range(kv):
        total = totals[head]
        inverse = jnp.broadcast_to(1.0 / total, (lanes, head_size))
        columns = slice(head * head_size, (head + 1) * head_size)
        turned[...] = acc[:, columns] * inverse
        upper = total.astype(jnp.bfloat16).astype(jnp.float32)
        kinds = [upper, m_scr[:, head : head + 1], total - upper]
        placed = jnp.zeros((lanes, head_size), jnp.float32)
        for kind, column in enumerate(kinds):
            placed = jnp.where(
                lane == member_of_row + 8 * kind,
                jnp.broadcast_to(column, placed.shape),
                placed,
            )
        gathered = jnp.sum(placed.reshape(rows, group, head_size), axis=1)
        stats[head] = stats[head] + pltpu.roll(gathered, 24 * request, 1)
        for member in range(group):
            index = head * group + member
            target, inside = index // share, index % share
            offset = pl.multiple_of(
                request * (share * head_size) + inside * head_size, head_size
            )
            staged[target, :, pl.ds(offset, head_size)] = turned[
                pl.ds(member, rows, stride=group), :
            ].astype(jnp.bfloat16)

    @pl.when(request == requests - 1)
    def _():
        for target in range(exp_count):
            head = target * share // group
            staged[target, :, requests * share * head_size :] = stats[head].astype(jnp.bfloat16)
        for step_away in range(exp_count):
            out_refs[step_away][...] = staged[info_ref[listed + (-step_away) % exp_count]]


def attend(queries, order, new_keys, new_values, keys, values, local_lengths, base, sub, tail):
    listed, span, kv, head_size = keys.shape
    requests, piece_rows, heads = queries[0].shape[:3]
    pieces = exp_count = len(queries)
    rows = piece_rows * pieces
    share = heads // exp_count
    fresh = new_keys.shape[1]
    width = requests * share * head_size + 128
    info = jnp.concatenate([local_lengths, order])
    factor = head_size ** (-0.5) * math.log2(math.e)
    lanes = rows * heads // kv
    flat = lambda x: x.reshape(listed, x.shape[1] * kv, head_size)
    block = lambda n: pl.BlockSpec((1, n, head_size), lambda r, info: (r + base, 0, 0))
    return pl.pallas_call(
        functools.partial(attend_kernel, pieces, base, listed, sub, tail, factor, exp_count),
        grid_spec=pltpu.PrefetchScalarGridSpec(
            num_scalar_prefetch=1,
            grid=(requests,),
            in_specs=[
                pl.BlockSpec((1, piece_rows, heads, head_size), lambda r, info: (r, 0, 0, 0))
            ]
            * pieces
            + [block(fresh * kv), block(fresh * kv), block(span * kv), block(span * kv)],
            out_specs=[pl.BlockSpec((rows, width), lambda r, info: (0, 0))] * exp_count,
            scratch_shapes=[
                pltpu.VMEM((rows, heads, head_size), jnp.float32),
                pltpu.VMEM((lanes, kv * head_size), jnp.bfloat16),
                pltpu.VMEM((2, 16, head_size), jnp.bfloat16),
                pltpu.VMEM((lanes, 128), jnp.float32),
                pltpu.VMEM((lanes, 128), jnp.float32),
                pltpu.VMEM((lanes, kv * head_size), jnp.float32),
                pltpu.VMEM((lanes, sub * kv), jnp.bfloat16),
                pltpu.VMEM((lanes, sub * kv), jnp.bfloat16),
                pltpu.VMEM((kv, rows, head_size), jnp.float32),
                pltpu.VMEM((lanes, head_size), jnp.float32),
                pltpu.VMEM((exp_count, rows, width), jnp.bfloat16),
            ],
        ),
        out_shape=[jax.ShapeDtypeStruct((rows, width), jnp.bfloat16)] * exp_count,
        compiler_params=pltpu.CompilerParams(dimension_semantics=("arbitrary",)),
        name="attend",
    )(info, *queries, flat(new_keys), flat(new_values), flat(keys), flat(values))


def merge_kernel(parts, batches, share, info_ref, *refs):
    w_refs = refs[batches * parts : (batches + 1) * parts]
    keep_ref, send_ref, attn = refs[(batches + 1) * parts :]
    rows, width = refs[0].shape
    head_size = 128
    requests = (width - head_size) // (share * head_size)
    group_shift = info_ref[0]
    half = info_ref[1]
    for batch in range(batches):
        x_refs = refs[batch * parts : (batch + 1) * parts]
        tables = []
        for x_ref in x_refs:
            table = x_ref[:, width - head_size :].astype(jnp.float32)
            tables.append(pltpu.roll(table, group_shift, 1))
        for request in range(requests):
            first = (batch * requests + request) * rows
            for member in range(share):
                at = 24 * request + member
                tops = [t[:, at + 8 : at + 9] for t in tables]
                sums = [t[:, at : at + 1] + t[:, at + 16 : at + 17] for t in tables]
                top = functools.reduce(jnp.maximum, tops)
                weights = [s * jnp.exp2(m - top) for s, m in zip(sums, tops)]
                inverse = 1.0 / functools.reduce(jnp.add, weights)
                start = (request * share + member) * head_size
                mixed = jnp.zeros((rows, head_size), jnp.float32)
                for weight, x_ref in zip(weights, x_refs):
                    part = x_ref[:, start : start + head_size].astype(jnp.float32)
                    mixed = mixed + jnp.broadcast_to(weight * inverse, part.shape) * part
                attn[
                    first : first + rows, member * head_size : (member + 1) * head_size
                ] = mixed.astype(jnp.bfloat16)
    columns = w_refs[0].shape[1]
    per_half = keep_ref.shape[1] // columns
    for part in range(parts):
        made = jnp.dot(attn[...], w_refs[part][...], preferred_element_type=jnp.float32)
        chunk = info_ref[2 + part]
        inside = pl.multiple_of((chunk % per_half) * columns, columns)

        @pl.when(chunk // per_half == half)
        def _():
            keep_ref[:, pl.ds(inside, columns)] = made

        @pl.when(chunk // per_half != half)
        def _():
            send_ref[:, pl.ds(inside, columns)] = made.astype(jnp.bfloat16)


def merge_project(batches, weights, info, share, requests):
    rows = batches[0][0].shape[0]
    columns = weights[0].shape[1]
    parts = len(weights)
    half_width = parts * columns // 2
    shape = (requests * rows, half_width)
    return pl.pallas_call(
        functools.partial(merge_kernel, parts, len(batches), share),
        in_specs=[pl.BlockSpec(memory_space=pltpu.SMEM)]
        + [pl.BlockSpec(memory_space=pltpu.VMEM)] * ((len(batches) + 1) * parts),
        out_specs=[pl.BlockSpec(memory_space=pltpu.VMEM)] * 2,
        out_shape=[
            jax.ShapeDtypeStruct(shape, jnp.float32),
            jax.ShapeDtypeStruct(shape, jnp.bfloat16),
        ],
        scratch_shapes=[pltpu.VMEM((requests * rows, share * head_size_of(weights, share)), jnp.bfloat16)],
        name="merge_project",
    )(info, *[message for batch in batches for message in batch], *weights)


def head_size_of(weights, share):
    return weights[0].shape[0] // share


def shift(value, axis, step):
    size = lax.axis_size(axis)
    return lax.ppermute(value, axis, [(i, (i + step) % size) for i in range(size)])


def take_block(value, index):
    return lax.dynamic_index_in_dim(value, index, 0, keepdims=False)


def gather_blocks(block, axis):
    return [block] + [shift(block, axis, s) for s in range(1, lax.axis_size(axis))]


def swap(value, axis, bits):
    size = lax.axis_size(axis)
    return lax.ppermute(value, axis, [(i, i ^ bits) for i in range(size)])


def route_table(route_ids, route_weights):
    groups = lax.axis_size("req") * lax.axis_size("exp")
    return jnp.sum(
        jnp.where(
            route_ids[None, :, :] == lax.iota(jnp.int32, groups)[:, None, None],
            route_weights[None, :, :],
            0.0,
        ),
        axis=2,
    )


def exchange_table(column):
    exp_size = lax.axis_size("exp")
    req_at, exp_at = lax.axis_index("req"), lax.axis_index("exp")

    def of(bits):
        picked = lax.dynamic_index_in_dim(
            column, req_at * exp_size + (exp_at ^ bits), 1, keepdims=False
        )
        if bits == 0:
            return picked
        return swap(picked, "exp", bits)

    return [of(bits).reshape(-1) for bits in range(exp_size)]


def halves(value, width, axis):
    head_at = lax.axis_index("head")
    own = lax.dynamic_slice_in_dim(value, head_at * width, width, axis)
    other = lax.dynamic_slice_in_dim(value, (1 - head_at) * width, width, axis)
    return own, other


def expert_block(own, weights, gains, maps_in, maps_out):
    other = swap(own, "head", 1)
    wide = [own.astype(jnp.float32), other.astype(jnp.float32)]
    squares = sum(jnp.sum(x * x, axis=-1, keepdims=True) for x in wide)
    factor = lax.rsqrt(squares / (2 * own.shape[1]) + norm_epsilon)
    scaled = [(x * factor * gain).astype(jnp.bfloat16) for x, gain in zip(wide, gains)]
    gate_up = jnp.dot(scaled[0], maps_in[0], preferred_element_type=jnp.float32)
    gate_up = gate_up + jnp.dot(scaled[1], maps_in[1], preferred_element_type=jnp.float32)
    half_units = gate_up.shape[-1] // 2
    activated = (jax.nn.silu(gate_up[:, :half_units]) * gate_up[:, half_units:]).astype(
        jnp.bfloat16
    )
    kept, passed = [
        jnp.dot(activated, maps, preferred_element_type=jnp.float32) * weights[:, None]
        for maps in maps_out
    ]
    return kept, passed.astype(jnp.bfloat16)


def dense_experts(half_hidden, column_table, gains, maps_in, maps_out):
    row_count, half_width = half_hidden.shape
    req_size = lax.axis_size("req")
    sent = half_hidden.astype(jnp.bfloat16)
    sent, column_table = lax.optimization_barrier((sent, column_table))
    column = jnp.concatenate(gather_blocks(sent, "req"), axis=0)
    middle = column.shape[0] // 2

    def run(block, index):
        return expert_block(block, row_weights[index], gains, maps_in, maps_out)

    def whole(kept, passed):
        return kept + swap(passed, "head", 1).astype(jnp.float32)

    def over(value, bits):
        return swap(value.astype(jnp.bfloat16), "exp", bits).astype(jnp.float32)

    near_x = swap(column, "exp", 1)
    near_y = swap(column, "exp", 2)
    row_weights = exchange_table(column_table)
    own_kept, own_passed = run(column, 0)
    near_x, near_y, own_passed = lax.optimization_barrier((near_x, near_y, own_passed))
    far_top = swap(near_x[:middle], "exp", 2)
    far_low = swap(near_y[middle:], "exp", 1)
    own = whole(own_kept, own_passed)
    for_x = whole(*run(near_x, 1))
    for_y = whole(*run(near_y, 2))
    back_x = over(for_x[:middle], 1)
    back_y = over(for_y[middle:], 2)
    top = own[:middle] + back_x
    low = own[middle:] + back_y
    far = whole(*run(jnp.concatenate([far_top, far_low], axis=0), 3))
    top = top + over(for_y[:middle] + over(far[:middle], 1), 2)
    low = low + over(for_x[middle:] + over(far[middle:], 2), 1)
    plane_sum = jnp.concatenate([top, low], axis=0).reshape(req_size, row_count, half_width)
    mixture = plane_sum[0]
    outgoing = plane_sum.astype(jnp.bfloat16)
    for s in range(1, req_size):
        mixture = mixture + shift(outgoing[s], "req", -s).astype(jnp.float32)
    return mixture


def sparse_experts(half_hidden, route_ids, route_weights, norm_gain, expert_in, expert_out, capacity):
    _, half_width = half_hidden.shape
    head_at = lax.axis_index("head")
    other = shift(half_hidden, "head", 1)
    first = jnp.where(head_at == 0, half_hidden, other)
    second = jnp.where(head_at == 0, other, half_hidden)
    hidden = jnp.concatenate([first, second], axis=1)
    normed = (
        hidden
        * lax.rsqrt(jnp.mean(hidden * hidden, axis=-1, keepdims=True) + norm_epsilon)
        * norm_gain
    ).astype(jnp.bfloat16)
    model_width = 2 * half_width
    local_experts = expert_in.shape[0]
    groups = lax.axis_size("req") * lax.axis_size("exp")
    experts_all = local_experts * groups
    expert_iota = lax.iota(jnp.int32, experts_all)
    named_count = jnp.sum((route_ids[:, :, None] == expert_iota).astype(jnp.int32), axis=1)
    earlier = jnp.cumsum(named_count, axis=0) - named_count
    slot_rank = jnp.take_along_axis(earlier, route_ids, axis=1)
    slot_index = route_ids * capacity + slot_rank
    slot_iota = lax.iota(jnp.int32, experts_all * capacity)
    placing = jnp.any(slot_index[None, :, :] == slot_iota[:, None, None], axis=2).astype(
        jnp.bfloat16
    )
    outgoing = jnp.dot(placing, normed, preferred_element_type=jnp.float32).astype(jnp.bfloat16)
    outgoing = outgoing.reshape(groups, local_experts, capacity, model_width)
    input_maps = expert_in.reshape(local_experts, model_width, -1)
    gate_up = jnp.einsum(
        "geci,eif->gecf",
        lax.all_to_all(outgoing, ("req", "exp"), split_axis=0, concat_axis=0, tiled=True),
        input_maps,
        preferred_element_type=jnp.float32,
    )
    half_units = gate_up.shape[-1] // 2
    activated = (jax.nn.silu(gate_up[..., :half_units]) * gate_up[..., half_units:]).astype(
        jnp.bfloat16
    )
    partial_value = jnp.einsum(
        "gecf,efi->geci", activated, expert_out, preferred_element_type=jnp.float32
    )
    summed = lax.psum_scatter(partial_value, "head", scatter_dimension=3, tiled=True).astype(
        jnp.bfloat16
    )
    returned = lax.all_to_all(summed, ("req", "exp"), split_axis=0, concat_axis=0, tiled=True)
    flat_results = returned.reshape(experts_all * capacity, half_width)
    picked = jnp.take(flat_results, slot_index, axis=0).astype(jnp.float32)
    return jnp.sum(picked * route_weights[:, :, None], axis=1)


def local(
    queries,
    new_keys,
    new_values,
    key_cache,
    value_cache,
    lengths,
    residual,
    out_weight,
    norm_gain,
    route_ids,
    route_weights,
    expert_in,
    expert_out,
):
    requests, span, kv, head_size = key_cache.shape
    heads = queries.shape[2]
    exp_size = lax.axis_size("exp")
    exp_at, head_at = lax.axis_index("exp"), lax.axis_index("head")
    share = heads // exp_size
    group = heads // kv
    sources = (exp_at - lax.iota(jnp.int32, exp_size)) % exp_size
    targets = [(exp_at + s) % exp_size for s in range(exp_size)]

    row_count, model_width = residual.shape
    half_width = model_width // 2
    groups = lax.axis_size("req") * exp_size
    experts_all = expert_in.shape[0] * groups
    capacity = max(2, 2 * row_count * route_ids.shape[1] // experts_all)
    dense = capacity >= row_count and experts_all == groups and exp_size == 4

    batch = requests
    starts = range(0, requests, batch)
    pieces = [
        gather_blocks(lax.slice_in_dim(queries, start, start + batch), "exp") for start in starts
    ]
    local_lengths = jnp.clip(lengths - exp_at * span, 0, span)
    split_weight = out_weight.reshape(exp_size, share * head_size, -1)
    weight_parts = [take_block(split_weight, targets[0])] + [
        shift(take_block(split_weight, targets[s]), "exp", s) for s in range(1, exp_size)
    ]
    if dense:
        own_piece, flat_in = lax.optimization_barrier(
            (pieces[0][0], expert_in[0].reshape(model_width, -1))
        )
        pieces[0] = [own_piece] + pieces[0][1:]
    received = []
    for start, gathered in zip(starts, pieces):
        messages = attend(
            gathered, sources, new_keys, new_values, key_cache, value_cache, local_lengths,
            start, 512, 256,
        )
        received.append(
            [messages[0]] + [shift(messages[s], "exp", s) for s in range(1, exp_size)]
        )
    if dense:
        maps_in = halves(flat_in, half_width, 0)
        maps_out = halves(expert_out[0], half_width, 1)
        gains = halves(norm_gain, half_width, 0)
        own_message, maps_in, maps_out = lax.optimization_barrier(
            (received[-1][0], maps_in, maps_out)
        )
        received[-1] = [own_message] + received[-1][1:]
    group_shift = (head_size - (exp_at * share) % group) % head_size
    info = jnp.concatenate([jnp.stack([group_shift, head_at]).astype(jnp.int32), sources])
    kept, sent = merge_project(received, weight_parts, info, share, requests)
    if dense:
        kept, named, given = lax.optimization_barrier((kept, route_ids, route_weights))
        column_table = jnp.stack(gather_blocks(route_table(named, given), "req"))
    both = kept + shift(sent, "head", 1).astype(jnp.float32)
    both = both.reshape(exp_size, row_count, half_width)
    outgoing = both.astype(jnp.bfloat16)
    hidden = lax.dynamic_slice_in_dim(residual, head_at * half_width, half_width, 1).astype(
        jnp.float32
    ) + take_block(both, targets[0])
    for s in range(1, exp_size):
        hidden = hidden + shift(take_block(outgoing, targets[s]), "exp", s).astype(jnp.float32)

    if dense:
        mixture = dense_experts(hidden, column_table, gains, maps_in, maps_out)
    else:
        mixture = sparse_experts(
            hidden, route_ids, route_weights, norm_gain, expert_in, expert_out, capacity
        )
    return (hidden + mixture).astype(jnp.bfloat16)


def solution(mesh):
    return jax.shard_map(
        local,
        mesh=mesh,
        in_specs=(
            P("req", "exp", "head", None),
            P("req", "exp", "head", None),
            P("req", "exp", "head", None),
            P("req", "exp", "head", None),
            P("req", "exp", "head", None),
            P("req"),
            P(("req", "exp"), None),
            P("head", "exp"),
            P(),
            P(("req", "exp"), None),
            P(("req", "exp"), None),
            P(("req", "exp"), None, None, "head"),
            P(("req", "exp"), "head", None),
        ),
        out_specs=P(("req", "exp"), "head"),
        check_vma=False,
    )
```

```python
import functools
import math
import jax
import jax.numpy as jnp
from jax import lax
from jax.experimental import pallas as pl
from jax.experimental.pallas import tpu as pltpu
from jax.sharding import PartitionSpec as P


masked_score = -1e30
norm_epsilon = 1e-06


def attend_kernel(pieces, base, listed, sub, tail, factor, exp_count, info_ref, *refs):
    q_refs = refs[:pieces]
    nk_ref, nv_ref, k_ref, v_ref = refs[pieces : pieces + 4]
    out_refs = refs[pieces + 4 : pieces + 4 + exp_count]
    scratch = refs[pieces + 4 + exp_count :]
    q_all, q_cat, pattern, m_scr, l_scr, acc, p_even, p_odd, stats, turned, staged = scratch
    requests = pl.num_programs(0)
    request = pl.program_id(0)
    head_size = k_ref.shape[2]
    kv = 2
    piece_rows, heads = q_refs[0].shape[1], q_refs[0].shape[2]
    group = heads // kv
    rows = piece_rows * pieces
    lanes = rows * group
    length = info_ref[request + base]
    even_lane = lax.broadcasted_iota(jnp.int32, (lanes, 128), 1) % 2 == 0

    @pl.when(request == 0)
    def _():
        stats[...] = jnp.zeros_like(stats)
        parity = lax.broadcasted_iota(jnp.int32, (16, head_size), 0) % 2
        pattern[0] = (1 - parity).astype(jnp.float32).astype(jnp.bfloat16)
        pattern[1] = parity.astype(jnp.float32).astype(jnp.bfloat16)

    for piece in range(pieces):
        where_to = info_ref[listed + piece] * piece_rows
        q_all[pl.ds(where_to, piece_rows)] = q_refs[piece][0].astype(jnp.float32)
    for head in range(kv):
        chosen = q_all[:, head * group : (head + 1) * group, :].reshape(lanes, head_size)
        q_cat[:, head * head_size : (head + 1) * head_size] = chosen.astype(jnp.bfloat16)

    def spread(block):
        if block.shape[0] < 16:
            left = block * pattern[0, : block.shape[0]]
            right = block * pattern[1, : block.shape[0]]
        else:
            tiles = block.reshape(block.shape[0] // 16, 16, head_size)
            left = (tiles * pattern[0][None]).reshape(block.shape)
            right = (tiles * pattern[1][None]).reshape(block.shape)
        return jnp.concatenate([left, right], axis=1)

    def score(block):
        return lax.dot_general(
            q_cat[...],
            spread(block),
            (((1,), (1,)), ((), ())),
            preferred_element_type=jnp.float32,
        )

    def both_columns(even, odd):
        shape = (lanes, 128)
        return jnp.where(even_lane, jnp.broadcast_to(even, shape), jnp.broadcast_to(odd, shape))

    def reduce_parity(wide, op, neutral):
        even = op(jnp.where(even_lane, wide, neutral), axis=1, keepdims=True)
        odd = op(jnp.where(even_lane, neutral, wide), axis=1, keepdims=True)
        return even, odd

    def init():
        scores = score(nk_ref[0]) * factor
        even = lax.broadcasted_iota(jnp.int32, scores.shape, 1) % 2 == 0
        top_even = jnp.max(jnp.where(even, scores, -jnp.inf), axis=1, keepdims=True)
        top_odd = jnp.max(jnp.where(even, -jnp.inf, scores), axis=1, keepdims=True)
        top_even = top_even.astype(jnp.bfloat16).astype(jnp.float32)
        top_odd = top_odd.astype(jnp.bfloat16).astype(jnp.float32)
        m_scr[...] = both_columns(top_even, top_odd)
        probs = jnp.exp2(
            scores
            - jnp.where(
                even,
                jnp.broadcast_to(top_even, scores.shape),
                jnp.broadcast_to(top_odd, scores.shape),
            )
        )
        l_even = jnp.sum(jnp.where(even, probs, 0.0), axis=1, keepdims=True)
        l_odd = jnp.sum(jnp.where(even, 0.0, probs), axis=1, keepdims=True)
        lane = lax.broadcasted_iota(jnp.int32, (lanes, 128), 1)
        l_scr[...] = jnp.where(lane < 2, both_columns(l_even, l_odd), 0.0)
        acc[...] = jnp.dot(
            probs.astype(jnp.bfloat16), spread(nv_ref[0]), preferred_element_type=jnp.float32
        )

    def piece_of(ref, start, size):
        return ref[0, pl.ds(pl.multiple_of(start * kv, kv * tail), size * kv), :]

    step = 256

    def soften(start, size, target, masked):
        top = m_scr[...]
        total = l_scr[...]
        for tile in range(size * kv // step):
            scores = score(piece_of_tile(k_ref, start, tile))
            for part in range(step // 128):
                piece = scores[:, part * 128 : (part + 1) * 128]
                probs = jnp.exp2(piece * factor - top)
                if masked:
                    lane = lax.broadcasted_iota(jnp.int32, (1, 128), 1)
                    position = start + (tile * step + part * 128 + lane) // kv
                    probs = jnp.where(position < length, probs, 0.0)
                total = total + probs
                at = tile * step + part * 128
                target[:, at : at + 128] = probs.astype(jnp.bfloat16)
        l_scr[...] = total

    def piece_of_tile(ref, start, tile):
        first = pl.multiple_of(start * kv, kv * tail) + tile * step
        return ref[0, pl.ds(first, step), :]

    def weigh(start, size, source):
        values = spread(piece_of(v_ref, start, size))
        acc[...] += jnp.dot(source[:, : size * kv], values, preferred_element_type=jnp.float32)

    init()
    here = length
    pairs = here // (2 * sub)

    def loop(i, carry):
        start = pl.multiple_of(i * 2 * sub, 2 * sub)
        before = jnp.maximum(start - sub, 0)
        soften(start, sub, p_even, False)
        weigh(before, sub, p_odd)
        soften(start + sub, sub, p_odd, False)
        weigh(start, sub, p_even)
        return carry

    p_odd[...] = jnp.zeros_like(p_odd)
    lax.fori_loop(0, pairs, loop, 0)
    weigh(pl.multiple_of(jnp.maximum(pairs * 2 * sub - sub, 0), sub), sub, p_odd)

    def tail_loop(i, carry):
        start = pl.multiple_of(pairs * 2 * sub + i * tail, tail)
        soften(start, tail, p_even, True)
        weigh(start, tail, p_even)
        return carry

    lax.fori_loop(0, (here - pairs * 2 * sub + tail - 1) // tail, tail_loop, 0)
    largest = jnp.max(l_scr[...])

    @pl.when(jnp.logical_not(largest < 1e30))
    def _():
        init()

        def slow_loop(i, carry):
            start = pl.multiple_of(i * tail, tail)
            scores = score(piece_of(k_ref, start, tail)) * factor
            lane = lax.broadcasted_iota(jnp.int32, (1, tail * kv), 1)
            inside = start + lane // kv < length
            scores = jnp.where(inside, scores, masked_score)
            wide = m_scr[...]
            for part in range(tail * kv // 128):
                wide = jnp.maximum(wide, scores[:, part * 128 : (part + 1) * 128])
            even, odd = reduce_parity(wide, jnp.max, -jnp.inf)
            even = even.astype(jnp.bfloat16).astype(jnp.float32)
            odd = odd.astype(jnp.bfloat16).astype(jnp.float32)
            top = both_columns(even, odd)
            fade = jnp.exp2(m_scr[...] - top)
            total = l_scr[...] * fade
            for part in range(tail * kv // 128):
                at = part * 128
                probs = jnp.where(
                    inside[:, at : at + 128], jnp.exp2(scores[:, at : at + 128] - top), 0.0
                )
                total = total + probs
                p_even[:, at : at + 128] = probs.astype(jnp.bfloat16)
            l_scr[...] = total
            m_scr[...] = top
            for head in range(kv):
                columns = slice(head * head_size, (head + 1) * head_size)
                acc[:, columns] = acc[:, columns] * jnp.broadcast_to(
                    fade[:, head : head + 1], (lanes, head_size)
                )
            weigh(start, tail, p_even)
            return carry

        lax.fori_loop(0, (here + tail - 1) // tail, slow_loop, 0)

    share = heads // exp_count
    totals = reduce_parity(l_scr[...], jnp.sum, 0.0)
    lane = lax.broadcasted_iota(jnp.int32, (lanes, head_size), 1)
    member_of_row = lax.broadcasted_iota(jnp.int32, (lanes, head_size), 0) % group
    for head in range(kv):
        total = totals[head]
        inverse = jnp.broadcast_to(1.0 / total, (lanes, head_size))
        columns = slice(head * head_size, (head + 1) * head_size)
        turned[...] = acc[:, columns] * inverse
        upper = total.astype(jnp.bfloat16).astype(jnp.float32)
        kinds = [upper, m_scr[:, head : head + 1], total - upper]
        placed = jnp.zeros((lanes, head_size), jnp.float32)
        for kind, column in enumerate(kinds):
            placed = jnp.where(
                lane == member_of_row + 8 * kind,
                jnp.broadcast_to(column, placed.shape),
                placed,
            )
        gathered = jnp.sum(placed.reshape(rows, group, head_size), axis=1)
        stats[head] = stats[head] + pltpu.roll(gathered, 24 * request, 1)
        for member in range(group):
            index = head * group + member
            target, inside = index // share, index % share
            offset = pl.multiple_of(
                request * (share * head_size) + inside * head_size, head_size
            )
            staged[target, :, pl.ds(offset, head_size)] = turned[
                pl.ds(member, rows, stride=group), :
            ].astype(jnp.bfloat16)

    @pl.when(request == requests - 1)
    def _():
        for target in range(exp_count):
            head = target * share // group
            staged[target, :, requests * share * head_size :] = stats[head].astype(jnp.bfloat16)
        for step_away in range(exp_count):
            out_refs[step_away][...] = staged[info_ref[listed + (-step_away) % exp_count]]


def attend(queries, order, new_keys, new_values, keys, values, local_lengths, base, sub, tail):
    listed, span, kv, head_size = keys.shape
    requests, piece_rows, heads = queries[0].shape[:3]
    pieces = exp_count = len(queries)
    rows = piece_rows * pieces
    share = heads // exp_count
    fresh = new_keys.shape[1]
    width = requests * share * head_size + 128
    info = jnp.concatenate([local_lengths, order])
    factor = head_size ** (-0.5) * math.log2(math.e)
    lanes = rows * heads // kv
    flat = lambda x: x.reshape(listed, x.shape[1] * kv, head_size)
    block = lambda n: pl.BlockSpec((1, n, head_size), lambda r, info: (r + base, 0, 0))
    return pl.pallas_call(
        functools.partial(attend_kernel, pieces, base, listed, sub, tail, factor, exp_count),
        grid_spec=pltpu.PrefetchScalarGridSpec(
            num_scalar_prefetch=1,
            grid=(requests,),
            in_specs=[
                pl.BlockSpec((1, piece_rows, heads, head_size), lambda r, info: (r, 0, 0, 0))
            ]
            * pieces
            + [block(fresh * kv), block(fresh * kv), block(span * kv), block(span * kv)],
            out_specs=[pl.BlockSpec((rows, width), lambda r, info: (0, 0))] * exp_count,
            scratch_shapes=[
                pltpu.VMEM((rows, heads, head_size), jnp.float32),
                pltpu.VMEM((lanes, kv * head_size), jnp.bfloat16),
                pltpu.VMEM((2, 16, head_size), jnp.bfloat16),
                pltpu.VMEM((lanes, 128), jnp.float32),
                pltpu.VMEM((lanes, 128), jnp.float32),
                pltpu.VMEM((lanes, kv * head_size), jnp.float32),
                pltpu.VMEM((lanes, sub * kv), jnp.bfloat16),
                pltpu.VMEM((lanes, sub * kv), jnp.bfloat16),
                pltpu.VMEM((kv, rows, head_size), jnp.float32),
                pltpu.VMEM((lanes, head_size), jnp.float32),
                pltpu.VMEM((exp_count, rows, width), jnp.bfloat16),
            ],
        ),
        out_shape=[jax.ShapeDtypeStruct((rows, width), jnp.bfloat16)] * exp_count,
        compiler_params=pltpu.CompilerParams(dimension_semantics=("arbitrary",)),
        name="attend",
    )(info, *queries, flat(new_keys), flat(new_values), flat(keys), flat(values))


def merge_kernel(parts, batches, share, info_ref, *refs):
    w_refs = refs[batches * parts : (batches + 1) * parts]
    keep_ref, send_ref, attn = refs[(batches + 1) * parts :]
    rows, width = refs[0].shape
    head_size = 128
    requests = (width - head_size) // (share * head_size)
    group_shift = info_ref[0]
    half = info_ref[1]
    for batch in range(batches):
        x_refs = refs[batch * parts : (batch + 1) * parts]
        tables = []
        for x_ref in x_refs:
            table = x_ref[:, width - head_size :].astype(jnp.float32)
            tables.append(pltpu.roll(table, group_shift, 1))
        for request in range(requests):
            first = (batch * requests + request) * rows
            for member in range(share):
                at = 24 * request + member
                tops = [t[:, at + 8 : at + 9] for t in tables]
                sums = [t[:, at : at + 1] + t[:, at + 16 : at + 17] for t in tables]
                top = functools.reduce(jnp.maximum, tops)
                weights = [s * jnp.exp2(m - top) for s, m in zip(sums, tops)]
                inverse = 1.0 / functools.reduce(jnp.add, weights)
                start = (request * share + member) * head_size
                mixed = jnp.zeros((rows, head_size), jnp.float32)
                for weight, x_ref in zip(weights, x_refs):
                    part = x_ref[:, start : start + head_size].astype(jnp.float32)
                    mixed = mixed + jnp.broadcast_to(weight * inverse, part.shape) * part
                attn[
                    first : first + rows, member * head_size : (member + 1) * head_size
                ] = mixed.astype(jnp.bfloat16)
    columns = w_refs[0].shape[1]
    per_half = keep_ref.shape[1] // columns
    for part in range(parts):
        made = jnp.dot(attn[...], w_refs[part][...], preferred_element_type=jnp.float32)
        chunk = info_ref[2 + part]
        inside = pl.multiple_of((chunk % per_half) * columns, columns)

        @pl.when(chunk // per_half == half)
        def _():
            keep_ref[:, pl.ds(inside, columns)] = made

        @pl.when(chunk // per_half != half)
        def _():
            send_ref[:, pl.ds(inside, columns)] = made.astype(jnp.bfloat16)


def merge_project(batches, weights, info, share, requests):
    rows = batches[0][0].shape[0]
    columns = weights[0].shape[1]
    parts = len(weights)
    half_width = parts * columns // 2
    shape = (requests * rows, half_width)
    return pl.pallas_call(
        functools.partial(merge_kernel, parts, len(batches), share),
        in_specs=[pl.BlockSpec(memory_space=pltpu.SMEM)]
        + [pl.BlockSpec(memory_space=pltpu.VMEM)] * ((len(batches) + 1) * parts),
        out_specs=[pl.BlockSpec(memory_space=pltpu.VMEM)] * 2,
        out_shape=[
            jax.ShapeDtypeStruct(shape, jnp.float32),
            jax.ShapeDtypeStruct(shape, jnp.bfloat16),
        ],
        scratch_shapes=[pltpu.VMEM((requests * rows, share * head_size_of(weights, share)), jnp.bfloat16)],
        name="merge_project",
    )(info, *[message for batch in batches for message in batch], *weights)


def head_size_of(weights, share):
    return weights[0].shape[0] // share


def shift(value, axis, step):
    size = lax.axis_size(axis)
    return lax.ppermute(value, axis, [(i, (i + step) % size) for i in range(size)])


def take_block(value, index):
    return lax.dynamic_index_in_dim(value, index, 0, keepdims=False)


def gather_blocks(block, axis):
    return [block] + [shift(block, axis, s) for s in range(1, lax.axis_size(axis))]


def swap(value, axis, bits):
    size = lax.axis_size(axis)
    return lax.ppermute(value, axis, [(i, i ^ bits) for i in range(size)])


def route_table(route_ids, route_weights):
    groups = lax.axis_size("req") * lax.axis_size("exp")
    return jnp.sum(
        jnp.where(
            route_ids[None, :, :] == lax.iota(jnp.int32, groups)[:, None, None],
            route_weights[None, :, :],
            0.0,
        ),
        axis=2,
    )


def exchange_table(column):
    exp_size = lax.axis_size("exp")
    req_at, exp_at = lax.axis_index("req"), lax.axis_index("exp")

    def of(bits):
        picked = lax.dynamic_index_in_dim(
            column, req_at * exp_size + (exp_at ^ bits), 1, keepdims=False
        )
        return picked if bits == 0 else swap(picked, "exp", bits)

    return [of(bits).reshape(-1) for bits in range(exp_size)]


def halves(value, width, axis):
    head_at = lax.axis_index("head")
    own = lax.dynamic_slice_in_dim(value, head_at * width, width, axis)
    other = lax.dynamic_slice_in_dim(value, (1 - head_at) * width, width, axis)
    return own, other


def expert_block(own, weights, gains, maps_in, maps_out):
    other = swap(own, "head", 1)
    wide = [own.astype(jnp.float32), other.astype(jnp.float32)]
    squares = sum(jnp.sum(x * x, axis=-1, keepdims=True) for x in wide)
    factor = lax.rsqrt(squares / (2 * own.shape[1]) + norm_epsilon)
    scaled = [(x * factor * gain).astype(jnp.bfloat16) for x, gain in zip(wide, gains)]
    gate_up = jnp.dot(scaled[0], maps_in[0], preferred_element_type=jnp.float32)
    gate_up = gate_up + jnp.dot(scaled[1], maps_in[1], preferred_element_type=jnp.float32)
    half_units = gate_up.shape[-1] // 2
    activated = (jax.nn.silu(gate_up[:, :half_units]) * gate_up[:, half_units:]).astype(
        jnp.bfloat16
    )
    kept, passed = [
        jnp.dot(activated, maps, preferred_element_type=jnp.float32) * weights[:, None]
        for maps in maps_out
    ]
    return kept, passed.astype(jnp.bfloat16)


def dense_experts(half_hidden, row_weights, gains, maps_in, maps_out):
    row_count, half_width = half_hidden.shape
    req_size = lax.axis_size("req")
    sent = half_hidden.astype(jnp.bfloat16)
    sent, row_weights = lax.optimization_barrier((sent, row_weights))
    column = jnp.concatenate(gather_blocks(sent, "req"), axis=0)
    middle = column.shape[0] // 2

    def run(block, index):
        return expert_block(block, row_weights[index], gains, maps_in, maps_out)

    def whole(kept, passed):
        return kept + swap(passed, "head", 1).astype(jnp.float32)

    def over(value, bits):
        return swap(value.astype(jnp.bfloat16), "exp", bits).astype(jnp.float32)

    near_x = swap(column, "exp", 1)
    near_y = swap(column, "exp", 2)
    own_kept, own_passed = run(column, 0)
    near_x, near_y, own_passed = lax.optimization_barrier((near_x, near_y, own_passed))
    far_top = swap(near_x[:middle], "exp", 2)
    far_low = swap(near_y[middle:], "exp", 1)
    own = whole(own_kept, own_passed)
    for_x = whole(*run(near_x, 1))
    for_y = whole(*run(near_y, 2))
    back_x = over(for_x[:middle], 1)
    back_y = over(for_y[middle:], 2)
    top = own[:middle] + back_x
    low = own[middle:] + back_y
    far = whole(*run(jnp.concatenate([far_top, far_low], axis=0), 3))
    top = top + over(for_y[:middle] + over(far[:middle], 1), 2)
    low = low + over(for_x[middle:] + over(far[middle:], 2), 1)
    plane_sum = jnp.concatenate([top, low], axis=0).reshape(req_size, row_count, half_width)
    mixture = plane_sum[0]
    outgoing = plane_sum.astype(jnp.bfloat16)
    for s in range(1, req_size):
        mixture = mixture + shift(outgoing[s], "req", -s).astype(jnp.float32)
    return mixture


def sparse_experts(half_hidden, route_ids, route_weights, norm_gain, expert_in, expert_out, capacity):
    _, half_width = half_hidden.shape
    head_at = lax.axis_index("head")
    other = shift(half_hidden, "head", 1)
    first = jnp.where(head_at == 0, half_hidden, other)
    second = jnp.where(head_at == 0, other, half_hidden)
    hidden = jnp.concatenate([first, second], axis=1)
    normed = (
        hidden
        * lax.rsqrt(jnp.mean(hidden * hidden, axis=-1, keepdims=True) + norm_epsilon)
        * norm_gain
    ).astype(jnp.bfloat16)
    model_width = 2 * half_width
    local_experts = expert_in.shape[0]
    groups = lax.axis_size("req") * lax.axis_size("exp")
    experts_all = local_experts * groups
    expert_iota = lax.iota(jnp.int32, experts_all)
    named_count = jnp.sum((route_ids[:, :, None] == expert_iota).astype(jnp.int32), axis=1)
    earlier = jnp.cumsum(named_count, axis=0) - named_count
    slot_rank = jnp.take_along_axis(earlier, route_ids, axis=1)
    slot_index = route_ids * capacity + slot_rank
    slot_iota = lax.iota(jnp.int32, experts_all * capacity)
    placing = jnp.any(slot_index[None, :, :] == slot_iota[:, None, None], axis=2).astype(
        jnp.bfloat16
    )
    outgoing = jnp.dot(placing, normed, preferred_element_type=jnp.float32).astype(jnp.bfloat16)
    outgoing = outgoing.reshape(groups, local_experts, capacity, model_width)
    input_maps = expert_in.reshape(local_experts, model_width, -1)
    gate_up = jnp.einsum(
        "geci,eif->gecf",
        lax.all_to_all(outgoing, ("req", "exp"), split_axis=0, concat_axis=0, tiled=True),
        input_maps,
        preferred_element_type=jnp.float32,
    )
    half_units = gate_up.shape[-1] // 2
    activated = (jax.nn.silu(gate_up[..., :half_units]) * gate_up[..., half_units:]).astype(
        jnp.bfloat16
    )
    partial_value = jnp.einsum(
        "gecf,efi->geci", activated, expert_out, preferred_element_type=jnp.float32
    )
    summed = lax.psum_scatter(partial_value, "head", scatter_dimension=3, tiled=True).astype(
        jnp.bfloat16
    )
    returned = lax.all_to_all(summed, ("req", "exp"), split_axis=0, concat_axis=0, tiled=True)
    flat_results = returned.reshape(experts_all * capacity, half_width)
    picked = jnp.take(flat_results, slot_index, axis=0).astype(jnp.float32)
    return jnp.sum(picked * route_weights[:, :, None], axis=1)


def local(
    queries,
    new_keys,
    new_values,
    key_cache,
    value_cache,
    lengths,
    residual,
    out_weight,
    norm_gain,
    route_ids,
    route_weights,
    expert_in,
    expert_out,
):
    requests, span, kv, head_size = key_cache.shape
    heads = queries.shape[2]
    exp_size = lax.axis_size("exp")
    exp_at, head_at = lax.axis_index("exp"), lax.axis_index("head")
    share = heads // exp_size
    group = heads // kv
    sources = (exp_at - lax.iota(jnp.int32, exp_size)) % exp_size
    targets = [(exp_at + s) % exp_size for s in range(exp_size)]

    row_count, model_width = residual.shape
    half_width = model_width // 2
    groups = lax.axis_size("req") * exp_size
    experts_all = expert_in.shape[0] * groups
    capacity = max(2, 2 * row_count * route_ids.shape[1] // experts_all)
    dense = capacity >= row_count and experts_all == groups and exp_size == 4

    batch = requests
    starts = range(0, requests, batch)
    pieces = [
        gather_blocks(lax.slice_in_dim(queries, start, start + batch), "exp") for start in starts
    ]
    local_lengths = jnp.clip(lengths - exp_at * span, 0, span)
    split_weight = out_weight.reshape(exp_size, share * head_size, -1)
    weight_parts = [take_block(split_weight, targets[0])] + [
        shift(take_block(split_weight, targets[s]), "exp", s) for s in range(1, exp_size)
    ]
    if dense:
        own_piece, flat_in = lax.optimization_barrier(
            (pieces[0][0], expert_in[0].reshape(model_width, -1))
        )
        pieces[0] = [own_piece] + pieces[0][1:]
    received = []
    for start, gathered in zip(starts, pieces):
        messages = attend(
            gathered, sources, new_keys, new_values, key_cache, value_cache, local_lengths,
            start, 512, 256,
        )
        sent = [messages[0]]
        for s in range(1, exp_size):
            sent.append(shift(messages[s], "exp", s))
        received.append(sent)
    if dense:
        maps_in = halves(flat_in, half_width, 0)
        maps_out = halves(expert_out[0], half_width, 1)
        gains = halves(norm_gain, half_width, 0)
        own_message, named, given = lax.optimization_barrier(
            (received[-1][0], route_ids, route_weights)
        )
        column_table = jnp.stack(gather_blocks(route_table(named, given), "req"))
        own_message, maps_in, maps_out = lax.optimization_barrier((own_message, maps_in, maps_out))
        received[-1] = [own_message] + received[-1][1:]
    group_shift = (head_size - (exp_at * share) % group) % head_size
    info = jnp.concatenate([jnp.stack([group_shift, head_at]).astype(jnp.int32), sources])
    kept, sent = merge_project(received, weight_parts, info, share, requests)
    if dense:
        kept, column_table = lax.optimization_barrier((kept, column_table))
        row_weights = exchange_table(column_table)
    both = kept + shift(sent, "head", 1).astype(jnp.float32)
    both = both.reshape(exp_size, row_count, half_width)
    outgoing = both.astype(jnp.bfloat16)
    hidden = lax.dynamic_slice_in_dim(residual, head_at * half_width, half_width, 1).astype(
        jnp.float32
    ) + take_block(both, targets[0])
    for s in range(1, exp_size):
        hidden = hidden + shift(take_block(outgoing, targets[s]), "exp", s).astype(jnp.float32)

    if dense:
        mixture = dense_experts(hidden, row_weights, gains, maps_in, maps_out)
    else:
        mixture = sparse_experts(
            hidden, route_ids, route_weights, norm_gain, expert_in, expert_out, capacity
        )
    return (hidden + mixture).astype(jnp.bfloat16)


def solution(mesh):
    return jax.shard_map(
        local,
        mesh=mesh,
        in_specs=(
            P("req", "exp", "head", None),
            P("req", "exp", "head", None),
            P("req", "exp", "head", None),
            P("req", "exp", "head", None),
            P("req", "exp", "head", None),
            P("req"),
            P(("req", "exp"), None),
            P("head", "exp"),
            P(),
            P(("req", "exp"), None),
            P(("req", "exp"), None),
            P(("req", "exp"), None, None, "head"),
            P(("req", "exp"), "head", None),
        ),
        out_specs=P(("req", "exp"), "head"),
        check_vma=False,
    )
```
